512 devices in a mesh: px: 32 (over z, y_lo, core), pz: 16 (over x, y_hi).
Axes of the slice: x: 4, y: 8 (y_hi: 4, y_lo: 2; y = y_hi * 2 + y_lo), z: 8, core: 2. Of those that a mesh axis runs over, the one named last changes fastest.
Arguments:
- velocity: float32 [3, 64, 512, 256], P(None, 'pz', 'px'), may hold values from -6 to 6
- first_deriv: bfloat16 [512, 512], replicated, may hold values from -0.25 to 0.25
- second_deriv: bfloat16 [512, 512], replicated, may hold values from -0.25 to 0.25
- bubble_vel: float32 [3, 12288, 128], P(None, ('px', 'pz')), may hold values from -6 to 6
- owner: int32 [2, 12288, 128], P(None, ('px', 'pz')), may hold values from 0 to 16383
- dest: int32 [2, 12288], P(None, ('px', 'pz')), may hold values from -1 to 1, as said below
Outputs:
- velocity_next: float32 [3, 64, 512, 256], P(None, 'pz', 'px')
- bubble_next: float32 [3, 12288, 128], P(None, ('px', 'pz'))
The draws below stay inside these ranges and needn't reach their ends.
Inputs may be any that keep to these rules, and one draw needn't show every extreme that they name: `dest`: in each substep at most 8 rows of one device have 1 and at most 8 have -1; some device has exactly 8 rows with 1 and some device exactly 8 rows with -1. `owner`: the cell counts streamwise cells fastest, then the wall-normal rows of the owning device's block, then its spanwise cells.
All inputs are finite; a program needn't handle non-finite values.
Results may differ from the reference program's by a relative error of at most 0.0018.
Values may be sent and summed in bfloat16 or wider, within the bound.
No kernel may reach another device: no remote copies, remote signals or barrier semaphores. Data moves between devices by JAX's collectives and lax.ppermute only.
A program may use at most 64 MiB of HBM per device.

```python
import jax
import jax.numpy as jnp
from jax import lax

NY = 512
CX = 8
CZ = 4
R_DEV = 24
ROW_LEN = 128
SUBSTEPS = 2
CAP = 8
NX = 256
NZ = 64
ROWS = 12288
N_PX = 32
N_PZ = 16


def draw_dest(key, part):
    device_count = ROWS // R_DEV
    first_key, second_key, third_key = jax.random.split(key, 3)
    counts = jax.random.randint(first_key, (2, 2, device_count), 0, CAP + 1)
    chosen = jax.random.randint(second_key, (2, 2), 0, device_count)
    devices = jnp.arange(device_count)
    counts = jnp.where(devices[None, None, :] == chosen[:, :, None], CAP, counts)
    keys = jax.random.split(third_key, 2 * device_count)
    shuffled = jax.vmap(lambda single: jax.random.permutation(single, R_DEV))(keys).reshape(2, device_count, R_DEV)
    plus_count = counts[:, 0, :, None]
    minus_count = counts[:, 1, :, None]
    heading = jnp.where(shuffled < plus_count, 1, jnp.where(shuffled < plus_count + minus_count, -1, 0))
    return heading.reshape(2, ROWS).astype(jnp.int32)


def touch_ends(result, stream_key, low, largest):
    extent = result.shape
    index_at = [jax.random.randint(jax.random.fold_in(stream_key, axis), (), 0, extent[axis]) for axis in range(len(extent))]
    result = result.at[tuple(index_at)].set(low)
    longest = extent.index(max(extent))
    index_at[longest] = (index_at[longest] + 1) % extent[longest]
    return result.at[tuple(index_at)].set(largest)


def shard_levels(rng, dims, shards, least, largest):
    level, own = 1.0, jax.random.fold_in(rng, 6)
    for position, blocks in shards:
        steps = jnp.exp(jax.random.uniform(jax.random.fold_in(own, position), (blocks,), jnp.float32, least / len(shards), largest / len(shards)))
        level = level * jnp.repeat(steps, dims[position] // blocks).reshape([-1 if axis == position else 1 for axis in range(len(dims))])
    return level


def scatter_about(key, extent, width, bound, pieces=(), kind=jnp.bfloat16):
    entries = jax.random.normal(key, extent, jnp.float32) * width
    if len(pieces) > 0:
        entries = shard_levels(key, extent, pieces, -0.22, 0.18) * entries
    return jnp.clip(entries, min=-bound, max=bound).astype(kind)


def setup_inputs(seed: int = 0) -> dict:
    arg_keys = jax.random.split(jax.random.key(seed), 7)
    return {
        "velocity": scatter_about(arg_keys[0], (3, NZ, NY, NX), 1.0, 6.0, ((1, 16), (2, 32)), jnp.float32),
        "first_deriv": scatter_about(arg_keys[1], (NY, NY), NY ** -0.5, 0.25),
        "second_deriv": scatter_about(arg_keys[2], (NY, NY), NY ** -0.5, 0.25),
        "bubble_vel": scatter_about(arg_keys[3], (3, ROWS, ROW_LEN), 1.0, 6.0, ((1, 512),), jnp.float32),
        "owner": touch_ends(jax.random.randint(arg_keys[4], (SUBSTEPS, ROWS, ROW_LEN), 0, CZ * CX * NY), jax.random.fold_in(arg_keys[4], 1), 0, (CZ * CX * NY) - 1).astype(jnp.int32),
        "dest": draw_dest(jax.random.fold_in(arg_keys[6], 71), 0),
    }


step_size = 0.5
viscosity = 0.4
relax_time = 0.5
coupling = 2.0
buoyancy = 0.5
forcing = 1.0
gammas = (8.0 / 15.0, 5.0 / 12.0)
zetas = (0.0, -17.0 / 60.0)


def widened(values):
    return lax.optimization_barrier(values).astype(jnp.float32)


def reference(velocity, first_deriv, second_deriv, bubble_vel, owner, dest):
    block_rows = NY // N_PX
    row_count = bubble_vel.shape[1]
    device = jnp.arange(row_count, dtype=jnp.int32) // R_DEV
    row_px = (device // N_PZ).astype(jnp.int32)
    row_pz = (device % N_PZ).astype(jnp.int32)
    first_mat = first_deriv.astype(jnp.float32)
    second_mat = second_deriv.astype(jnp.float32)
    lift_vec = jnp.array([0.0, buoyancy, 0.0], jnp.float32).reshape(3, 1, 1)
    field = velocity
    bubbles = bubble_vel
    earlier_field = None
    earlier_rate = None
    for substep in range(2):
        cell_ids = owner[substep]
        span_plane = cell_ids // (block_rows * NX)
        within = cell_ids % (block_rows * NX)
        wall_row = within // NX
        stream_col = within % NX
        span_block = (row_pz + dest[substep]) % N_PZ
        z_index = span_block[:, None] * CZ + span_plane
        y_index = row_px[:, None] * block_rows + wall_row
        global_cell = ((z_index * NY + y_index) * NX + stream_col).astype(jnp.int32)
        flattened = field.reshape(3, -1)
        fluid_seen = jnp.take(flattened, global_cell, axis=1)
        bubble_rate = (fluid_seen - bubbles) / relax_time + lift_vec
        pushes = coupling * (bubbles - fluid_seen)
        push = jnp.zeros_like(flattened).at[:, global_cell.reshape(-1)].add(pushes.reshape(3, -1)).reshape(field.shape)
        field_bf = field.astype(jnp.bfloat16)
        normal_v = field_bf[1].astype(jnp.float32)
        parts = []
        for component in range(3):
            column = field_bf[component].astype(jnp.float32)
            slopes = jnp.einsum("ij,zjx->zix", first_mat, column).astype(jnp.bfloat16)
            curves = jnp.einsum("ij,zjx->zix", second_mat, column).astype(jnp.bfloat16)
            wall_terms = widened((-normal_v * widened(slopes) + viscosity * widened(curves)).astype(jnp.bfloat16))
            current = field[component]
            next_x = jnp.roll(current, -1, axis=2)
            prev_x = jnp.roll(current, 1, axis=2)
            next_z = jnp.roll(current, -1, axis=0)
            prev_z = jnp.roll(current, 1, axis=0)
            grad_x = 0.5 * (next_x - prev_x)
            grad_z = 0.5 * (next_z - prev_z)
            curv_x = next_x + prev_x - 2.0 * current
            curv_z = next_z + prev_z - 2.0 * current
            tendency = -(field[0] * grad_x + field[2] * grad_z) + wall_terms + viscosity * (curv_x + curv_z) + push[component]
            if component == 0:
                tendency = tendency + forcing
            parts.append(tendency)
        tendency = jnp.stack(parts)
        if substep == 0:
            field = field + step_size * (gammas[0] * tendency)
            bubbles = bubbles + step_size * (gammas[0] * bubble_rate)
        else:
            field = field + step_size * (gammas[1] * tendency + zetas[1] * earlier_field)
            bubbles = bubbles + step_size * (gammas[1] * bubble_rate + zetas[1] * earlier_rate)
        earlier_field = tendency
        earlier_rate = bubble_rate
    return field, bubbles
```

```python
import functools

import jax
import jax.numpy as jnp
from jax import lax
from jax.experimental import pallas as pl
from jax.experimental.pallas import tpu as pltpu
from jax.sharding import PartitionSpec as P

step_size = 0.5
viscosity = 0.4
relax_time = 0.5
coupling = 2.0
buoyancy = 0.5
forcing = 1.0
gammas = (8.0 / 15.0, 5.0 / 12.0)
zetas = (0.0, -17.0 / 60.0)

F32 = jnp.float32
BF16 = jnp.bfloat16
C1 = step_size * gammas[0]
C2 = step_size * gammas[1]
E2 = step_size * zetas[1]

ROWS_A = 64
FIELD_ROWS = 192
SEND_ROWS = 240
LAST_ROWS = 96


def iota(shape, dim):
    return lax.broadcasted_iota(jnp.int32, shape, dim)


def call(body, outs, scratch=()):
    return pl.pallas_call(
        body,
        out_shape=tuple(jax.ShapeDtypeStruct(s, d) for s, d in outs),
        scratch_shapes=list(scratch),
        compiler_params=pltpu.CompilerParams(vmem_limit_bytes=48 * 1024 * 1024),
    )


def exact_dot(a, b):
    return jnp.dot(a, b, precision=lax.Precision.HIGHEST, preferred_element_type=F32)


def hi_lo(x):
    hi = x.astype(BF16).astype(F32)
    return hi, x - hi


def pick_matrix(dest_row):
    up = jnp.where(dest_row == 1, 1.0, 0.0).astype(F32)
    down = jnp.where(dest_row == -1, 1.0, 0.0).astype(F32)
    slot = iota((16, 24), 0)
    marks = jnp.where(slot < 8, jnp.broadcast_to(up, (16, 24)), jnp.broadcast_to(down, (16, 24)))
    before = jnp.where(iota((24, 24), 0) < iota((24, 24), 1), 1.0, 0.0).astype(F32)
    rank = exact_dot(marks, before)
    wanted = jnp.where(slot < 8, slot, slot - 8).astype(F32)
    return jnp.where((rank == wanted) & (marks > 0.5), 1.0, 0.0).astype(F32)


def put_matrix(dest_row):
    r, c = iota((24, 24), 0), iota((24, 24), 1)
    wide = jnp.broadcast_to(dest_row, (24, 24))
    own = jnp.sum(jnp.where(r == c, wide, 0).astype(F32), axis=1, keepdims=True)
    rank_up = jnp.sum(jnp.where((c < r) & (wide == 1), 1.0, 0.0), axis=1, keepdims=True)
    rank_down = jnp.sum(jnp.where((c < r) & (wide == -1), 1.0, 0.0), axis=1, keepdims=True)
    slot = iota((24, 16), 1).astype(F32)
    hit_up = (own == 1.0) & (rank_up == slot)
    hit_down = (own == -1.0) & (rank_down + 8.0 == slot)
    return jnp.where(hit_up | hit_down, 1.0, 0.0).astype(F32)


def home_cells(cells, dest_row):
    r, c = iota((24, 24), 0), iota((24, 24), 1)
    wide = jnp.broadcast_to(dest_row, (24, 24))
    away = jnp.sum(jnp.where((r == c) & (wide != 0), 1.0, 0.0), axis=1, keepdims=True)
    row = jnp.where(away > 0.5, -1, cells >> 8)
    return row, cells & 255


def fill_columns(col, hot_ref):
    at = iota((256, 128), 0)
    for k in range(8):
        hot = jnp.where(at == jnp.broadcast_to(col[k : k + 1], (256, 128)), 1.0, 0.0)
        hot_ref[:, k * 128 : (k + 1) * 128] = hot.astype(BF16)


def fill_values(row, highs, lows, load_ref):
    at = iota((ROWS_A, 128), 0)
    for k in range(8):
        mask = at == jnp.broadcast_to(row[k : k + 1], (ROWS_A, 128))
        lanes = slice(k * 128, (k + 1) * 128)
        for part, values in enumerate((highs, lows)):
            for a in range(3):
                base = (part * 3 + a) * ROWS_A
                value = jnp.broadcast_to(values[a][k : k + 1], (ROWS_A, 128))
                load_ref[base : base + ROWS_A, lanes] = jnp.where(mask, value, 0.0).astype(BF16)
        load_ref[384:448, lanes] = jnp.where(mask, 1.0, 0.0).astype(BF16)


def scatter(load_ref, hot_ref):
    return lax.dot_general(
        load_ref[...], hot_ref[...], (((1,), (1,)), ((), ())), preferred_element_type=F32
    )


def gather(table, row, hot_ref):
    found = jnp.dot(table, hot_ref[...], preferred_element_type=F32)
    parts = found.shape[0] // FIELD_ROWS
    at = iota((ROWS_A, 128), 0)
    lines = [[], [], []]
    for k in range(8):
        mask = at == jnp.broadcast_to(row[k : k + 1], (ROWS_A, 128))
        for a in range(3):
            block = found[a * ROWS_A : (a + 1) * ROWS_A, k * 128 : (k + 1) * 128]
            for part in range(1, parts):
                base = part * FIELD_ROWS + a * ROWS_A
                block = block + found[base : base + ROWS_A, k * 128 : (k + 1) * 128]
            lines[a].append(jnp.sum(jnp.where(mask, block, 0.0), axis=0, keepdims=True))
    return [jnp.concatenate(line, axis=0) for line in lines]


def split_table(field, table_ref):
    hi, lo = hi_lo(field)
    table_ref[0:FIELD_ROWS] = hi.astype(BF16)
    table_ref[FIELD_ROWS : 2 * FIELD_ROWS] = lo.astype(BF16)


def push_of(sums, field):
    loads = sums[0:192] + sums[192:384]
    count = sums[384:448]
    return coupling * (loads - jnp.concatenate([count, count, count], axis=0) * field)


def plane(ref, a, z):
    base = (a * 4 + z) * 16
    return ref[base : base + 16, :].astype(F32)


def inner_tendency(f_ref, a, z):
    here = plane(f_ref, a, z)
    next_x = pltpu.roll(here, 255, 1)
    prev_x = pltpu.roll(here, 1, 1)
    across = next_x + prev_x - 4.0 * here
    slope_z = None
    if z < 3:
        next_z = plane(f_ref, a, z + 1)
        across = across + next_z
        slope_z = next_z
    if z > 0:
        prev_z = plane(f_ref, a, z - 1)
        across = across + prev_z
        slope_z = -prev_z if slope_z is None else slope_z - prev_z
    flow = plane(f_ref, 0, z) * (0.5 * (next_x - prev_x)) + plane(f_ref, 2, z) * (0.5 * slope_z)
    total = viscosity * across - flow
    return total + forcing if a == 0 else total


def halo_term(f_ref, below, above, a, z):
    if z == 0:
        return (viscosity + 0.5 * plane(f_ref, 2, 0)) * below
    return (viscosity - 0.5 * plane(f_ref, 2, 3)) * above


def lane_group(shape):
    return iota(shape, len(shape) - 1) // 32


def first_send(field_ref, bubble_ref, owner_ref, dest_ref, up_ref, down_ref, moved_ref):
    block = field_ref[...].astype(BF16)
    up_ref[0:FIELD_ROWS] = block
    down_ref[0:FIELD_ROWS] = block
    first, second = owner_ref[0], owner_ref[1]
    columns = [bubble_ref[a] for a in range(3)]
    columns += [((first >> 8) + 1).astype(F32), (first & 255).astype(F32)]
    picked = exact_dot(pick_matrix(dest_ref[0:1]), jnp.concatenate(columns, axis=1))
    later = jnp.concatenate([((second >> 8) + 1).astype(F32), (second & 255).astype(F32)], axis=1)
    later = exact_dot(pick_matrix(dest_ref[1:2]), later)
    moved_ref[...] = picked[:, 384:640]
    for ref, at in ((up_ref, 0), (down_ref, 8)):
        lines = []
        for a in range(3):
            lines.append(jnp.concatenate(hi_lo(picked[at : at + 8, a * 128 : (a + 1) * 128]), axis=1))
        lines += [picked[at : at + 8, 384:640], later[at : at + 8], jnp.zeros((8, 256), F32)]
        ref[FIELD_ROWS:SEND_ROWS] = jnp.concatenate(lines, axis=0).astype(BF16)


def home_first(field_ref, bubble_ref, owner_ref, dest_ref, part_ref, seen_ref,
               table_ref, row_ref, col_ref, hot_ref, load_ref, sum_ref):
    field = field_ref[...]
    split_table(field, table_ref)
    row, col = home_cells(owner_ref[0], dest_ref[0:1])
    row_ref[...] = row
    col_ref[...] = col
    sum_ref[...] = jnp.zeros_like(sum_ref)

    def step(i, carry):
        rows = pl.ds(pl.multiple_of(i * 8, 8), 8)
        row8, col8 = row_ref[rows], col_ref[rows]
        fill_columns(col8, hot_ref)
        pairs = [hi_lo(bubble_ref[a, rows]) for a in range(3)]
        fill_values(row8, [p[0] for p in pairs], [p[1] for p in pairs], load_ref)
        seen = gather(table_ref[...], row8, hot_ref)
        for a in range(3):
            seen_ref[a, rows] = seen[a]
        sum_ref[...] += scatter(load_ref, hot_ref)
        return carry

    lax.fori_loop(0, 3, step, 0)
    push = push_of(sum_ref[...], field)
    for a in range(3):
        for z in range(4):
            base = (a * 4 + z) * 16
            part_ref[base : base + 16] = inner_tendency(field_ref, a, z) + push[base : base + 16]


def tail_of(ref, line):
    base = FIELD_ROWS + line * 8
    return ref[base : base + 8, :].astype(F32)


def tail_cells(tail, line):
    at = tail[line * 8 : line * 8 + 8].astype(jnp.int32)
    return at[:, 0:128] - 1, at[:, 128:256]


def pack_pair(six, out_ref):
    group = lane_group((16, 128))
    group8 = lane_group((8, 128))
    for z in range(4):
        for half in range(2):
            tiles = [six[i][z][:, half * 128 : (half + 1) * 128] for i in range(6)]
            for o in range(4):
                def moved(x, target):
                    shift = ((target - o) % 4) * 32
                    return x if shift == 0 else pltpu.roll(x, shift, 1)
                main = moved(tiles[3], 3)
                for i in range(3):
                    main = jnp.where(group == i, moved(tiles[i], i), main)
                rest = moved(tiles[5][8:16], 3)
                rest = jnp.where(group8 == 2, moved(tiles[4][8:16], 2), rest)
                rest = jnp.where(group8 == 1, moved(tiles[5][0:8], 1), rest)
                rest = jnp.where(group8 == 0, moved(tiles[4][0:8], 0), rest)
                peer = z * 8 + half * 4 + o
                out_ref[peer] = jnp.concatenate([main, rest], axis=0).astype(BF16)


def unpack(ref, second, a, z):
    halves = []
    group = lane_group((16, 128))
    for half in range(2):
        total = None
        for o in range(4):
            chunk = ref[z * 8 + half * 4 + o].astype(F32)
            if not second:
                piece, at = chunk[0:16], a
            elif a == 0:
                piece, at = chunk[0:16], 3
            else:
                rest = chunk[16:24]
                piece, at = jnp.concatenate([rest, pltpu.roll(rest, 64, 1)], axis=0), a - 1
            shift = ((o - at) % 4) * 32
            piece = piece if shift == 0 else pltpu.roll(piece, shift, 1)
            total = piece if total is None else jnp.where(group == o, piece, total)
        halves.append(total)
    return jnp.concatenate(halves, axis=1)


def arrivals_first(field_ref, part_ref, low_ref, high_ref, tend_ref, send_ref, hot_ref, load_ref):
    field = field_ref[...]
    sums = None
    for ref in (low_ref, high_ref):
        tail = ref[FIELD_ROWS:SEND_ROWS, :].astype(F32)
        row, col = tail_cells(tail, 3)
        fill_columns(col, hot_ref)
        highs = [tail[a * 8 : a * 8 + 8, 0:128] for a in range(3)]
        lows = [tail[a * 8 : a * 8 + 8, 128:256] for a in range(3)]
        fill_values(row, highs, lows, load_ref)
        got = scatter(load_ref, hot_ref)
        sums = got if sums is None else sums + got
    push = push_of(sums, field)
    six = [[None] * 4 for _ in range(6)]
    for a in range(3):
        for z in range(4):
            base = (a * 4 + z) * 16
            total = part_ref[base : base + 16] + push[base : base + 16]
            if z == 0 or z == 3:
                total = total + halo_term(field_ref, plane(low_ref, a, 3), plane(high_ref, a, 0), a, z)
            tend_ref[base : base + 16] = total
            here = field_ref[base : base + 16]
            six[a][z] = here
            six[3 + a][z] = here + C1 * total
    pack_pair(six, send_ref)


def bubbles_first(low_ref, high_ref, moved_ref, seen_ref, bubble_ref, owner_ref, dest_ref,
                  rate_ref, next_ref, slots_ref, sum_ref, row_ref, col_ref, hot_ref, load_ref):
    found = [[], [], []]
    for at, ref in ((0, high_ref), (8, low_ref)):
        cells = moved_ref[at : at + 8].astype(jnp.int32)
        fill_columns(cells[:, 128:256], hot_ref)
        seen = gather(ref[0:FIELD_ROWS], cells[:, 0:128] - 1, hot_ref)
        for a in range(3):
            found[a].append(seen[a])
    found = jnp.concatenate([jnp.concatenate(f, axis=0) for f in found], axis=1)
    back = exact_dot(put_matrix(dest_ref[0:1]), found)
    after = []
    for a in range(3):
        here = bubble_ref[a]
        rate = (seen_ref[a] + back[:, a * 128 : (a + 1) * 128] - here) / relax_time
        if a == 1:
            rate = rate + buoyancy
        rate_ref[a] = rate
        after.append(here + C1 * rate)
        next_ref[a] = after[a]
    picked = exact_dot(pick_matrix(dest_ref[1:2]), jnp.concatenate(after, axis=1))
    for at in (0, 8):
        for a in range(3):
            line = at * 3 + a * 8
            slots_ref[line : line + 8] = jnp.concatenate(
                hi_lo(picked[at : at + 8, a * 128 : (a + 1) * 128]), axis=1
            )
    row, col = home_cells(owner_ref[1], dest_ref[1:2])
    row_ref[...] = row
    col_ref[...] = col
    sum_ref[...] = jnp.zeros_like(sum_ref)

    def step(i, carry):
        rows = pl.ds(pl.multiple_of(i * 8, 8), 8)
        fill_columns(col_ref[rows], hot_ref)
        pairs = [hi_lo(next_ref[a, rows]) for a in range(3)]
        fill_values(row_ref[rows], [p[0] for p in pairs], [p[1] for p in pairs], load_ref)
        sum_ref[...] += scatter(load_ref, hot_ref)
        return carry

    lax.fori_loop(0, 3, step, 0)


def columns_body(got_ref, first_ref, second_ref, send_ref):
    got = got_ref[...].astype(F32)
    main = got[:, 0:16].reshape(512, 128)
    rest = got[:, 16:24].reshape(256, 128)
    other = pltpu.roll(rest, 64, 1)
    rest = jnp.concatenate([rest.reshape(32, 8, 128), other.reshape(32, 8, 128)], axis=1).reshape(512, 128)
    group = lane_group((512, 128))
    guess = jnp.where(group == 0, pltpu.roll(main, 32, 1), pltpu.roll(rest, 32, 1))

    def wall(x):
        field = x.astype(BF16)
        wide = field.astype(F32)
        normal = jnp.where(group == 0, pltpu.roll(wide, 96, 1), jnp.where(group == 2, pltpu.roll(wide, 32, 1), wide))
        slopes = jnp.dot(first_ref[...], field, preferred_element_type=F32).astype(BF16).astype(F32)
        curves = jnp.dot(second_ref[...], field, preferred_element_type=F32).astype(BF16).astype(F32)
        return (viscosity * curves - normal * slopes).astype(BF16).astype(F32)

    wall_1 = wall(main)
    wall_2 = wall(guess + C1 * wall_1)
    back = pltpu.roll(wall_2, 96, 1)
    ahead = pltpu.roll(wall_2, 32, 1)
    out = jnp.where(group == 3, back, wall_1).reshape(32, 16, 128)
    group8 = lane_group((32, 8, 128))
    tail = jnp.where(group8 < 2, back.reshape(32, 16, 128)[:, 0:8], ahead.reshape(32, 16, 128)[:, 8:16])
    send_ref[...] = jnp.concatenate([out, tail], axis=1).astype(BF16)


def middle_body(wall_ref, field_ref, part_ref, low_ref, high_ref, slots_ref,
                next_ref, tend_ref, up_ref, down_ref, table_ref, hot_ref):
    for a in range(3):
        for z in range(4):
            base = (a * 4 + z) * 16
            total = part_ref[base : base + 16] + unpack(wall_ref, False, a, z)
            tend_ref[base : base + 16] = total
            next_ref[base : base + 16] = field_ref[base : base + 16] + C1 * total
    split_table(next_ref[...], table_ref)
    for ref, out_ref, z, at in ((low_ref, down_ref, 0, 24), (high_ref, up_ref, 3, 0)):
        tail = ref[FIELD_ROWS:SEND_ROWS, :].astype(F32)
        row, col = tail_cells(tail, 4)
        fill_columns(col, hot_ref)
        seen = gather(table_ref[...], row, hot_ref)
        lines = [plane(next_ref, a, z) for a in range(3)]
        lines.append(slots_ref[at : at + 24])
        lines += [jnp.concatenate(hi_lo(seen[a]), axis=1) for a in range(3)]
        out_ref[...] = jnp.concatenate(lines, axis=0).astype(BF16)


def home_second(wall_ref, field_ref, tend_ref, sum_ref, bubble_ref, rate_ref, owner_ref, dest_ref,
                base_ref, late_ref, table_ref, row_ref, col_ref, hot_ref):
    field = field_ref[...]
    push = push_of(sum_ref[...], field)
    for a in range(3):
        for z in range(4):
            base = (a * 4 + z) * 16
            total = inner_tendency(field_ref, a, z) + push[base : base + 16] + unpack(wall_ref, True, a, z)
            earlier = tend_ref[base : base + 16]
            base_ref[base : base + 16] = field_ref[base : base + 16] + (C2 * total + E2 * earlier)
    split_table(field, table_ref)
    row, col = home_cells(owner_ref[1], dest_ref[1:2])
    row_ref[...] = row
    col_ref[...] = col

    def step(i, carry):
        rows = pl.ds(pl.multiple_of(i * 8, 8), 8)
        fill_columns(col_ref[rows], hot_ref)
        seen = gather(table_ref[...], row_ref[rows], hot_ref)
        for a in range(3):
            here = bubble_ref[a, rows]
            rate = (seen[a] - here) / relax_time
            if a == 1:
                rate = rate + buoyancy
            late_ref[a, rows] = here + (C2 * rate + E2 * rate_ref[a, rows])
        return carry

    lax.fori_loop(0, 3, step, 0)


def arrivals_second(base_ref, field_ref, low_ref, high_ref, low2_ref, high2_ref, late_ref, dest_ref,
                    out_ref, bubble_ref, hot_ref, load_ref):
    field = field_ref[...]
    sums = None
    for ref, ref2 in ((low_ref, low2_ref), (high_ref, high2_ref)):
        tail = ref[FIELD_ROWS:SEND_ROWS, :].astype(F32)
        row, col = tail_cells(tail, 4)
        fill_columns(col, hot_ref)
        extra = ref2[48:96, :].astype(F32)
        highs = [extra[a * 8 : a * 8 + 8, 0:128] for a in range(3)]
        lows = [extra[a * 8 : a * 8 + 8, 128:256] for a in range(3)]
        fill_values(row, highs, lows, load_ref)
        got = scatter(load_ref, hot_ref)
        sums = got if sums is None else sums + got
    push = push_of(sums, field)
    for a in range(3):
        for z in range(4):
            base = (a * 4 + z) * 16
            total = push[base : base + 16]
            if z == 0 or z == 3:
                below = low2_ref[a * 16 : a * 16 + 16, :].astype(F32)
                above = high2_ref[a * 16 : a * 16 + 16, :].astype(F32)
                total = total + halo_term(field_ref, below, above, a, z)
            out_ref[base : base + 16] = base_ref[base : base + 16] + C2 * total
    from_high = high2_ref[48:96, :].astype(F32)
    from_low = low2_ref[48:96, :].astype(F32)
    found = []
    for a in range(3):
        line = 24 + a * 8
        high = from_high[line : line + 8, 0:128] + from_high[line : line + 8, 128:256]
        low = from_low[line : line + 8, 0:128] + from_low[line : line + 8, 128:256]
        found.append(jnp.concatenate([high, low], axis=0))
    back = exact_dot(put_matrix(dest_ref[1:2]), jnp.concatenate(found, axis=1))
    for a in range(3):
        bubble_ref[a] = late_ref[a] + (C2 / relax_time) * back[:, a * 128 : (a + 1) * 128]


def shifted(x, by):
    length = lax.axis_size("pz")
    return lax.ppermute(x, "pz", [(i, (i + by) % length) for i in range(length)])


def exchange(x):
    return lax.all_to_all(x, "px", split_axis=0, concat_axis=0, tiled=True)


def on_device(velocity, first_deriv, second_deriv, bubble_vel, owner, dest):
    field = velocity.reshape(FIELD_ROWS, 256)
    block = ((FIELD_ROWS, 256), F32)
    rows = ((3, 24, 128), F32)
    hot = pltpu.VMEM((256, 1024), BF16)
    load = pltpu.VMEM((448, 1024), BF16)
    table = pltpu.VMEM((384, 256), BF16)
    ids = pltpu.VMEM((24, 128), jnp.int32)
    packed = ((32, 24, 128), BF16)

    sends = ((SEND_ROWS, 256), BF16)
    up, down, moved = call(first_send, (sends, sends, ((16, 256), F32)))(field, bubble_vel, owner, dest)
    low, high = shifted(up, 1), shifted(down, -1)
    part, seen = call(
        home_first, (block, rows), (table, ids, ids, hot, load, pltpu.VMEM((448, 256), F32))
    )(field, bubble_vel, owner, dest)
    part, to_columns = call(arrivals_first, (block, packed), (hot, load))(field, part, low, high)
    columns = exchange(to_columns)
    rate, bubbles, slots, sums = call(
        bubbles_first, (rows, rows, ((48, 256), F32), ((448, 256), F32)), (ids, ids, hot, load)
    )(low, high, moved, seen, bubble_vel, owner, dest)
    (walls,) = call(columns_body, (packed,))(columns, first_deriv, second_deriv)
    walls = exchange(walls)
    lasts = ((LAST_ROWS, 256), BF16)
    middle, tend, up, down = call(middle_body, (block, block, lasts, lasts), (table, hot))(
        walls, field, part, low, high, slots
    )
    low2, high2 = shifted(up, 1), shifted(down, -1)
    base, late = call(home_second, (block, rows), (table, ids, ids, hot))(
        walls, middle, tend, sums, bubbles, rate, owner, dest
    )
    field, bubbles = call(arrivals_second, (block, rows), (hot, load))(
        base, middle, low, high, low2, high2, late, dest
    )
    return (field.reshape(velocity.shape), bubbles)


def solution(mesh):
    return jax.shard_map(
        on_device,
        mesh=mesh,
        in_specs=(
            P(None, "pz", "px", None),
            P(),
            P(),
            P(None, ("px", "pz"), None),
            P(None, ("px", "pz"), None),
            P(None, ("px", "pz")),
        ),
        out_specs=(P(None, "pz", "px", None), P(None, ("px", "pz"), None)),
        check_vma=False,
    )
```

```python
import functools

import jax
import jax.numpy as jnp
from jax import lax
from jax.experimental import pallas as pl
from jax.experimental.pallas import tpu as pltpu
from jax.sharding import PartitionSpec as P

step_size = 0.5
viscosity = 0.4
relax_time = 0.5
coupling = 2.0
buoyancy = 0.5
forcing = 1.0
gammas = (8.0 / 15.0, 5.0 / 12.0)
zetas = (0.0, -17.0 / 60.0)

F32 = jnp.float32
BF16 = jnp.bfloat16
C1 = step_size * gammas[0]
C2 = step_size * gammas[1]
E2 = step_size * zetas[1]

ROWS_A = 64
FIELD_ROWS = 192
SEND_ROWS = 240
LAST_ROWS = 96


def iota(shape, dim):
    return lax.broadcasted_iota(jnp.int32, shape, dim)


def call(body, outs, scratch=()):
    return pl.pallas_call(
        body,
        out_shape=tuple(jax.ShapeDtypeStruct(s, d) for s, d in outs),
        scratch_shapes=list(scratch),
        compiler_params=pltpu.CompilerParams(vmem_limit_bytes=48 * 1024 * 1024),
    )


def exact_dot(a, b):
    return jnp.dot(a, b, precision=lax.Precision.HIGHEST, preferred_element_type=F32)


def hi_lo(x):
    hi = x.astype(BF16).astype(F32)
    return hi, x - hi


def pick_matrix(dest_row):
    up = jnp.where(dest_row == 1, 1.0, 0.0).astype(F32)
    down = jnp.where(dest_row == -1, 1.0, 0.0).astype(F32)
    slot = iota((16, 24), 0)
    marks = jnp.where(slot < 8, jnp.broadcast_to(up, (16, 24)), jnp.broadcast_to(down, (16, 24)))
    before = jnp.where(iota((24, 24), 0) < iota((24, 24), 1), 1.0, 0.0).astype(F32)
    rank = exact_dot(marks, before)
    wanted = jnp.where(slot < 8, slot, slot - 8).astype(F32)
    return jnp.where((rank == wanted) & (marks > 0.5), 1.0, 0.0).astype(F32)


def put_matrix(dest_row):
    r, c = iota((24, 24), 0), iota((24, 24), 1)
    wide = jnp.broadcast_to(dest_row, (24, 24))
    own = jnp.sum(jnp.where(r == c, wide, 0).astype(F32), axis=1, keepdims=True)
    rank_up = jnp.sum(jnp.where((c < r) & (wide == 1), 1.0, 0.0), axis=1, keepdims=True)
    rank_down = jnp.sum(jnp.where((c < r) & (wide == -1), 1.0, 0.0), axis=1, keepdims=True)
    slot = iota((24, 16), 1).astype(F32)
    hit_up = (own == 1.0) & (rank_up == slot)
    hit_down = (own == -1.0) & (rank_down + 8.0 == slot)
    return jnp.where(hit_up | hit_down, 1.0, 0.0).astype(F32)


def home_cells(cells, dest_row):
    r, c = iota((24, 24), 0), iota((24, 24), 1)
    wide = jnp.broadcast_to(dest_row, (24, 24))
    away = jnp.sum(jnp.where((r == c) & (wide != 0), 1.0, 0.0), axis=1, keepdims=True)
    row = jnp.where(away > 0.5, -1, cells >> 8)
    return row, cells & 255


def spread(line):
    return jnp.broadcast_to(line, (16, 128)).astype(BF16)


def row_numbers(count):
    at = iota((16, 128), 0)
    return [(at + 16 * q).astype(F32).astype(BF16) for q in range(count)]


def fill_columns(col, hot_ref):
    numbers = row_numbers(16)
    one, zero = jnp.ones((16, 128), BF16), jnp.zeros((16, 128), BF16)
    col = col.astype(F32)
    for k in range(8):
        here = spread(col[k : k + 1])
        for q in range(16):
            hot_ref[q * 16 : q * 16 + 16, k * 128 : (k + 1) * 128] = jnp.where(numbers[q] == here, one, zero)


def fill_values(row, highs, lows, load_ref):
    numbers = row_numbers(4)
    one, zero = jnp.ones((16, 128), BF16), jnp.zeros((16, 128), BF16)
    row = row.astype(F32)
    for k in range(8):
        here = spread(row[k : k + 1])
        masks = [numbers[q] == here for q in range(4)]
        values = [spread(x[k : k + 1]) for x in (*highs, *lows)] + [one]
        for part, value in enumerate(values[: load_ref.shape[0] // ROWS_A]):
            for q in range(4):
                at = part * ROWS_A + q * 16
                load_ref[at : at + 16, k * 128 : (k + 1) * 128] = jnp.where(masks[q], value, zero)


def scatter(load_ref, hot_ref):
    return lax.dot_general(
        load_ref[...], hot_ref[...], (((1,), (1,)), ((), ())), preferred_element_type=F32
    )


def gather(table, row, hot_ref):
    found = jnp.dot(table, hot_ref[...], preferred_element_type=F32)
    parts = found.shape[0] // FIELD_ROWS
    at = iota((ROWS_A, 128), 0)
    lines = [[], [], []]
    for k in range(8):
        mask = at == jnp.broadcast_to(row[k : k + 1], (ROWS_A, 128))
        for a in range(3):
            block = found[a * ROWS_A : (a + 1) * ROWS_A, k * 128 : (k + 1) * 128]
            for part in range(1, parts):
                base = part * FIELD_ROWS + a * ROWS_A
                block = block + found[base : base + ROWS_A, k * 128 : (k + 1) * 128]
            lines[a].append(jnp.sum(jnp.where(mask, block, 0.0), axis=0, keepdims=True))
    return [jnp.concatenate(line, axis=0) for line in lines]


def split_table(field, table_ref):
    hi, lo = hi_lo(field)
    table_ref[0:FIELD_ROWS] = hi.astype(BF16)
    table_ref[FIELD_ROWS : 2 * FIELD_ROWS] = lo.astype(BF16)


def push_of(sums, field):
    loads = sums[0:192] + sums[192:384]
    count = sums[384:448]
    return coupling * (loads - jnp.concatenate([count, count, count], axis=0) * field)


def plane(ref, a, z):
    base = (a * 4 + z) * 16
    return ref[base : base + 16, :].astype(F32)


def inner_tendency(f_ref, a, z):
    here = plane(f_ref, a, z)
    next_x = pltpu.roll(here, 255, 1)
    prev_x = pltpu.roll(here, 1, 1)
    across = next_x + prev_x - 4.0 * here
    slope_z = None
    if z < 3:
        next_z = plane(f_ref, a, z + 1)
        across = across + next_z
        slope_z = next_z
    if z > 0:
        prev_z = plane(f_ref, a, z - 1)
        across = across + prev_z
        slope_z = -prev_z if slope_z is None else slope_z - prev_z
    flow = plane(f_ref, 0, z) * (0.5 * (next_x - prev_x)) + plane(f_ref, 2, z) * (0.5 * slope_z)
    total = viscosity * across - flow
    return total + forcing if a == 0 else total


def halo_term(f_ref, below, above, a, z):
    if z == 0:
        return (viscosity + 0.5 * plane(f_ref, 2, 0)) * below
    return (viscosity - 0.5 * plane(f_ref, 2, 3)) * above


def lane_group(shape):
    return iota(shape, len(shape) - 1) // 32


def first_send(field_hbm, bubble_hbm, owner_hbm, dest_hbm, up_ref, down_ref, moved_ref,
               field_ref, bubble_ref, owner_ref, dest_ref, sems):
    pairs = ((dest_hbm, dest_ref), (owner_hbm, owner_ref), (bubble_hbm, bubble_ref), (field_hbm, field_ref))
    copies = [pltpu.make_async_copy(src, dst, sems.at[i]) for i, (src, dst) in enumerate(pairs)]
    for copy in copies:
        copy.start()
    for copy in copies[:3]:
        copy.wait()
    first, second = owner_ref[0], owner_ref[1]
    columns = [bubble_ref[a] for a in range(3)]
    columns += [((first >> 8) + 1).astype(F32), (first & 255).astype(F32)]
    picked = exact_dot(pick_matrix(dest_ref[0:1]), jnp.concatenate(columns, axis=1))
    later = jnp.concatenate([((second >> 8) + 1).astype(F32), (second & 255).astype(F32)], axis=1)
    later = exact_dot(pick_matrix(dest_ref[1:2]), later)
    moved_ref[...] = picked[:, 384:640]
    for ref, at in ((up_ref, 0), (down_ref, 8)):
        lines = []
        for a in range(3):
            lines.append(jnp.concatenate(hi_lo(picked[at : at + 8, a * 128 : (a + 1) * 128]), axis=1))
        lines += [picked[at : at + 8, 384:640], later[at : at + 8], jnp.zeros((8, 256), F32)]
        ref[FIELD_ROWS:SEND_ROWS] = jnp.concatenate(lines, axis=0).astype(BF16)
    copies[3].wait()
    block = field_ref[...].astype(BF16)
    up_ref[0:FIELD_ROWS] = block
    down_ref[0:FIELD_ROWS] = block


def home_first(field_ref, bubble_ref, owner_ref, dest_ref, part_ref, seen_ref,
               table_ref, row_ref, col_ref, hot_ref, load_ref, sum_ref):
    field = field_ref[...]
    split_table(field, table_ref)
    row, col = home_cells(owner_ref[0], dest_ref[0:1])
    row_ref[...] = row
    col_ref[...] = col
    sum_ref[...] = jnp.zeros_like(sum_ref)

    def step(i, carry):
        rows = pl.ds(pl.multiple_of(i * 8, 8), 8)
        row8, col8 = row_ref[rows], col_ref[rows]
        fill_columns(col8, hot_ref)
        pairs = [hi_lo(bubble_ref[a, rows]) for a in range(3)]
        fill_values(row8, [p[0] for p in pairs], [p[1] for p in pairs], load_ref)
        seen = gather(table_ref[...], row8, hot_ref)
        for a in range(3):
            seen_ref[a, rows] = seen[a]
        sum_ref[...] += scatter(load_ref, hot_ref)
        return carry

    lax.fori_loop(0, 3, step, 0)
    push = push_of(sum_ref[...], field)
    for a in range(3):
        for z in range(4):
            base = (a * 4 + z) * 16
            part_ref[base : base + 16] = inner_tendency(field_ref, a, z) + push[base : base + 16]


def tail_of(ref):
    return ref[FIELD_ROWS:SEND_ROWS, :].astype(F32)


def tail_cells(tail, line):
    at = tail[line * 8 : line * 8 + 8].astype(jnp.int32)
    return at[:, 0:128] - 1, at[:, 128:256]


def pack_pair(six, out_ref):
    group = lane_group((16, 128))
    group8 = lane_group((8, 128))
    for z in range(4):
        for half in range(2):
            tiles = [six[i][z][:, half * 128 : (half + 1) * 128] for i in range(6)]
            for o in range(4):
                def moved(x, target):
                    shift = ((target - o) % 4) * 32
                    return x if shift == 0 else pltpu.roll(x, shift, 1)
                main = moved(tiles[3], 3)
                for i in range(3):
                    main = jnp.where(group == i, moved(tiles[i], i), main)
                rest = moved(tiles[5][8:16], 3)
                rest = jnp.where(group8 == 2, moved(tiles[4][8:16], 2), rest)
                rest = jnp.where(group8 == 1, moved(tiles[5][0:8], 1), rest)
                rest = jnp.where(group8 == 0, moved(tiles[4][0:8], 0), rest)
                peer = z * 8 + half * 4 + o
                out_ref[peer] = jnp.concatenate([main, rest], axis=0).astype(BF16)


def unpack(ref, second, a, z):
    halves = []
    group = lane_group((16, 128))
    for half in range(2):
        total = None
        for o in range(4):
            chunk = ref[z * 8 + half * 4 + o].astype(F32)
            if not second:
                piece, at = chunk[0:16], a
            elif a == 0:
                piece, at = chunk[0:16], 3
            else:
                rest = chunk[16:24]
                piece, at = jnp.concatenate([rest, pltpu.roll(rest, 64, 1)], axis=0), a - 1
            shift = ((o - at) % 4) * 32
            piece = piece if shift == 0 else pltpu.roll(piece, shift, 1)
            total = piece if total is None else jnp.where(group == o, piece, total)
        halves.append(total)
    return jnp.concatenate(halves, axis=1)


def arrivals_first(field_ref, part_ref, low_ref, high_ref, tend_ref, send_ref, hot_ref, load_ref):
    field = field_ref[...]
    sums = None
    for ref in (low_ref, high_ref):
        tail = tail_of(ref)
        row, col = tail_cells(tail, 3)
        fill_columns(col, hot_ref)
        highs = [tail[a * 8 : a * 8 + 8, 0:128] for a in range(3)]
        lows = [tail[a * 8 : a * 8 + 8, 128:256] for a in range(3)]
        fill_values(row, highs, lows, load_ref)
        got = scatter(load_ref, hot_ref)
        sums = got if sums is None else sums + got
    push = push_of(sums, field)
    six = [[None] * 4 for _ in range(6)]
    for a in range(3):
        for z in range(4):
            base = (a * 4 + z) * 16
            total = part_ref[base : base + 16] + push[base : base + 16]
            if z == 0 or z == 3:
                total = total + halo_term(field_ref, plane(low_ref, a, 3), plane(high_ref, a, 0), a, z)
            tend_ref[base : base + 16] = total
            here = field_ref[base : base + 16]
            six[a][z] = here
            six[3 + a][z] = (here - here.astype(BF16).astype(F32)) + C1 * total
    pack_pair(six, send_ref)


def bubbles_first(low_ref, high_ref, moved_ref, seen_ref, bubble_ref, owner_ref, dest_ref,
                  rate_ref, next_ref, slots_ref, sum_ref, come_ref,
                  row_ref, col_ref, hot_ref, load_ref, ones_ref):
    found = [[], [], []]
    for at, ref in ((0, high_ref), (8, low_ref)):
        cells = moved_ref[at : at + 8].astype(jnp.int32)
        fill_columns(cells[:, 128:256], hot_ref)
        seen = gather(ref[0:FIELD_ROWS], cells[:, 0:128] - 1, hot_ref)
        for a in range(3):
            found[a].append(seen[a])
    found = jnp.concatenate([jnp.concatenate(f, axis=0) for f in found], axis=1)
    back = exact_dot(put_matrix(dest_ref[0:1]), found)
    after = []
    for a in range(3):
        here = bubble_ref[a]
        rate = (seen_ref[a] + back[:, a * 128 : (a + 1) * 128] - here) / relax_time
        if a == 1:
            rate = rate + buoyancy
        rate_ref[a] = rate
        after.append(here + C1 * rate)
        next_ref[a] = after[a]
    picked = exact_dot(pick_matrix(dest_ref[1:2]), jnp.concatenate(after, axis=1))
    for at in (0, 8):
        for a in range(3):
            line = at * 3 + a * 8
            slots_ref[line : line + 8] = jnp.concatenate(
                hi_lo(picked[at : at + 8, a * 128 : (a + 1) * 128]), axis=1
            )
    row, col = home_cells(owner_ref[1], dest_ref[1:2])
    row_ref[...] = row
    col_ref[...] = col
    sum_ref[...] = jnp.zeros_like(sum_ref)

    def step(i, carry):
        rows = pl.ds(pl.multiple_of(i * 8, 8), 8)
        fill_columns(col_ref[rows], hot_ref)
        pairs = [hi_lo(next_ref[a, rows]) for a in range(3)]
        fill_values(row_ref[rows], [p[0] for p in pairs], [p[1] for p in pairs], load_ref)
        sum_ref[...] += scatter(load_ref, hot_ref)
        return carry

    lax.fori_loop(0, 3, step, 0)
    for i, ref in enumerate((low_ref, high_ref)):
        row, col = tail_cells(tail_of(ref), 4)
        fill_columns(col, come_ref.at[i])
        fill_values(row, (), (), ones_ref)
        sum_ref[384:448] += scatter(ones_ref, come_ref.at[i])


def columns_body(got_ref, first_ref, second_ref, send_ref):
    got = got_ref[...].astype(F32)
    main = got[:, 0:16].reshape(512, 128)
    rest = got[:, 16:24].reshape(256, 128)
    other = pltpu.roll(rest, 64, 1)
    rest = jnp.concatenate([rest.reshape(32, 8, 128), other.reshape(32, 8, 128)], axis=1).reshape(512, 128)
    group = lane_group((512, 128))
    gain = jnp.where(group == 0, pltpu.roll(main, 32, 1), pltpu.roll(rest, 32, 1))

    def wall(x):
        field = x.astype(BF16)
        wide = field.astype(F32)
        normal = jnp.where(group == 0, pltpu.roll(wide, 96, 1), jnp.where(group == 2, pltpu.roll(wide, 32, 1), wide))
        slopes = jnp.dot(first_ref[...], field, preferred_element_type=F32).astype(BF16).astype(F32)
        curves = jnp.dot(second_ref[...], field, preferred_element_type=F32).astype(BF16).astype(F32)
        return (viscosity * curves - normal * slopes).astype(BF16).astype(F32)

    wall_1 = wall(main)
    wall_2 = wall(main + (gain + C1 * wall_1))
    back = pltpu.roll(wall_2, 96, 1)
    ahead = pltpu.roll(wall_2, 32, 1)
    out = jnp.where(group == 3, back, wall_1).reshape(32, 16, 128)
    group8 = lane_group((32, 8, 128))
    tail = jnp.where(group8 < 2, back.reshape(32, 16, 128)[:, 0:8], ahead.reshape(32, 16, 128)[:, 8:16])
    send_ref[...] = jnp.concatenate([out, tail], axis=1).astype(BF16)


def middle_body(wall_ref, field_ref, part_ref, low_ref, high_ref, slots_ref, come_ref,
                next_ref, tend_ref, up_ref, down_ref, table_ref):
    for a in range(3):
        for z in range(4):
            base = (a * 4 + z) * 16
            total = part_ref[base : base + 16] + unpack(wall_ref, False, a, z)
            tend_ref[base : base + 16] = total
            next_ref[base : base + 16] = field_ref[base : base + 16] + C1 * total
    split_table(next_ref[...], table_ref)
    ends = ((low_ref, down_ref, 0, 24), (high_ref, up_ref, 3, 0))
    for i, (ref, out_ref, z, at) in enumerate(ends):
        row, _ = tail_cells(tail_of(ref), 4)
        seen = gather(table_ref[...], row, come_ref.at[i])
        lines = [plane(next_ref, a, z) for a in range(3)]
        lines.append(slots_ref[at : at + 24])
        lines += [jnp.concatenate(hi_lo(seen[a]), axis=1) for a in range(3)]
        out_ref[...] = jnp.concatenate(lines, axis=0).astype(BF16)


def home_second(wall_ref, field_ref, tend_ref, sum_ref, bubble_ref, rate_ref, owner_ref, dest_ref,
                base_ref, late_ref, table_ref, row_ref, col_ref, hot_ref):
    field = field_ref[...]
    push = push_of(sum_ref[...], field)
    for a in range(3):
        for z in range(4):
            base = (a * 4 + z) * 16
            total = inner_tendency(field_ref, a, z) + push[base : base + 16] + unpack(wall_ref, True, a, z)
            earlier = tend_ref[base : base + 16]
            base_ref[base : base + 16] = field_ref[base : base + 16] + (C2 * total + E2 * earlier)
    split_table(field, table_ref)
    row, col = home_cells(owner_ref[1], dest_ref[1:2])
    row_ref[...] = row
    col_ref[...] = col

    def step(i, carry):
        rows = pl.ds(pl.multiple_of(i * 8, 8), 8)
        fill_columns(col_ref[rows], hot_ref)
        seen = gather(table_ref[...], row_ref[rows], hot_ref)
        for a in range(3):
            here = bubble_ref[a, rows]
            rate = (seen[a] - here) / relax_time
            if a == 1:
                rate = rate + buoyancy
            late_ref[a, rows] = here + (C2 * rate + E2 * rate_ref[a, rows])
        return carry

    lax.fori_loop(0, 3, step, 0)


def arrivals_second(base_ref, field_ref, low_ref, high_ref, low2_ref, high2_ref, late_ref, dest_ref, come_ref,
                    out_ref, bubble_ref, load_ref):
    sums = None
    for i, (ref, ref2) in enumerate(((low_ref, low2_ref), (high_ref, high2_ref))):
        row, _ = tail_cells(tail_of(ref), 4)
        extra = ref2[48:96, :].astype(F32)
        highs = [extra[a * 8 : a * 8 + 8, 0:128] for a in range(3)]
        lows = [extra[a * 8 : a * 8 + 8, 128:256] for a in range(3)]
        fill_values(row, highs, lows, load_ref)
        got = scatter(load_ref, come_ref.at[i])
        sums = got if sums is None else sums + got
    push = coupling * (sums[0:192] + sums[192:384])
    for a in range(3):
        for z in range(4):
            base = (a * 4 + z) * 16
            total = push[base : base + 16]
            if z == 0 or z == 3:
                below = low2_ref[a * 16 : a * 16 + 16, :].astype(F32)
                above = high2_ref[a * 16 : a * 16 + 16, :].astype(F32)
                total = total + halo_term(field_ref, below, above, a, z)
            out_ref[base : base + 16] = base_ref[base : base + 16] + C2 * total
    from_high = high2_ref[48:96, :].astype(F32)
    from_low = low2_ref[48:96, :].astype(F32)
    found = []
    for a in range(3):
        line = 24 + a * 8
        high = from_high[line : line + 8, 0:128] + from_high[line : line + 8, 128:256]
        low = from_low[line : line + 8, 0:128] + from_low[line : line + 8, 128:256]
        found.append(jnp.concatenate([high, low], axis=0))
    back = exact_dot(put_matrix(dest_ref[1:2]), jnp.concatenate(found, axis=1))
    for a in range(3):
        bubble_ref[a] = late_ref[a] + (C2 / relax_time) * back[:, a * 128 : (a + 1) * 128]


def shifted(x, by):
    length = lax.axis_size("pz")
    return lax.ppermute(x, "pz", [(i, (i + by) % length) for i in range(length)])


def exchange(x):
    return lax.all_to_all(x, "px", split_axis=0, concat_axis=0, tiled=True)


def on_device(velocity, first_deriv, second_deriv, bubble_vel, owner, dest):
    field = velocity.reshape(FIELD_ROWS, 256)
    block = ((FIELD_ROWS, 256), F32)
    rows = ((3, 24, 128), F32)
    hot = pltpu.VMEM((256, 1024), BF16)
    load = pltpu.VMEM((448, 1024), BF16)
    table = pltpu.VMEM((384, 256), BF16)
    ids = pltpu.VMEM((24, 128), jnp.int32)
    packed = ((32, 24, 128), BF16)

    velocity_in, bubbles_in, owner_in, dest_in = (
        pltpu.with_memory_space_constraint(x, pltpu.HBM) for x in (field, bubble_vel, owner, dest)
    )
    up, down, moved, field, bubble_vel, owner, dest = pl.pallas_call(
        first_send,
        in_specs=[pl.BlockSpec(memory_space=pltpu.HBM)] * 4,
        out_shape=(
            pltpu.VMEM((SEND_ROWS, 256), BF16),
            pltpu.VMEM((SEND_ROWS, 256), BF16),
            pltpu.VMEM((16, 256), F32),
            pltpu.VMEM((FIELD_ROWS, 256), F32),
            pltpu.VMEM((3, 24, 128), F32),
            pltpu.VMEM((2, 24, 128), jnp.int32),
            pltpu.VMEM((2, 24), jnp.int32),
        ),
        scratch_shapes=[pltpu.SemaphoreType.DMA((4,))],
    )(velocity_in, bubbles_in, owner_in, dest_in)
    low, high = shifted(up, 1), shifted(down, -1)
    part, seen = call(
        home_first, (block, rows), (table, ids, ids, hot, load, pltpu.VMEM((448, 256), F32))
    )(field, bubble_vel, owner, dest)
    part, to_columns = call(arrivals_first, (block, packed), (hot, load))(field, part, low, high)
    columns = exchange(to_columns)
    rate, bubbles, slots, sums, come = call(
        bubbles_first,
        (rows, rows, ((48, 256), F32), ((448, 256), F32), ((2, 256, 1024), BF16)),
        (ids, ids, hot, load, pltpu.VMEM((64, 1024), BF16)),
    )(low, high, moved, seen, bubble_vel, owner, dest)
    (walls,) = call(columns_body, (packed,))(columns, first_deriv, second_deriv)
    walls = exchange(walls)
    lasts = ((LAST_ROWS, 256), BF16)
    middle, tend, up, down = call(middle_body, (block, block, lasts, lasts), (table,))(
        walls, field, part, low, high, slots, come
    )
    low2, high2 = shifted(up, 1), shifted(down, -1)
    base, late = call(home_second, (block, rows), (table, ids, ids, hot))(
        walls, middle, tend, sums, bubbles, rate, owner, dest
    )
    field, bubbles = call(arrivals_second, (block, rows), (pltpu.VMEM((384, 1024), BF16),))(
        base, middle, low, high, low2, high2, late, dest, come
    )
    return (field.reshape(velocity.shape), bubbles)


def solution(mesh):
    return jax.shard_map(
        on_device,
        mesh=mesh,
        in_specs=(
            P(None, "pz", "px", None),
            P(),
            P(),
            P(None, ("px", "pz"), None),
            P(None, ("px", "pz"), None),
            P(None, ("px", "pz")),
        ),
        out_specs=(P(None, "pz", "px", None), P(None, ("px", "pz"), None)),
        check_vma=False,
    )
```

```python
import functools

import jax
import jax.numpy as jnp
from jax import lax
from jax.experimental import pallas as pl
from jax.experimental.pallas import tpu as pltpu
from jax.sharding import PartitionSpec as P

step_size = 0.5
viscosity = 0.4
relax_time = 0.5
coupling = 2.0
buoyancy = 0.5
forcing = 1.0
gammas = (8.0 / 15.0, 5.0 / 12.0)
zetas = (0.0, -17.0 / 60.0)

F32 = jnp.float32
BF16 = jnp.bfloat16
C1 = step_size * gammas[0]
C2 = step_size * gammas[1]
E2 = step_size * zetas[1]

ROWS_A = 64
FIELD_ROWS = 192
SEND_ROWS = 240
LAST_ROWS = 96


def iota(shape, dim):
    return lax.broadcasted_iota(jnp.int32, shape, dim)


def call(body, outs, scratch=()):
    return pl.pallas_call(
        body,
        out_shape=tuple(jax.ShapeDtypeStruct(s, d) for s, d in outs),
        scratch_shapes=list(scratch),
        compiler_params=pltpu.CompilerParams(vmem_limit_bytes=48 * 1024 * 1024),
    )


def exact_dot(a, b):
    return jnp.dot(a, b, precision=lax.Precision.HIGHEST, preferred_element_type=F32)


def hi_lo(x):
    hi = x.astype(BF16).astype(F32)
    return hi, x - hi


def pick_matrix(dest_row):
    up = jnp.where(dest_row == 1, 1.0, 0.0).astype(F32)
    down = jnp.where(dest_row == -1, 1.0, 0.0).astype(F32)
    slot = iota((16, 24), 0)
    marks = jnp.where(slot < 8, jnp.broadcast_to(up, (16, 24)), jnp.broadcast_to(down, (16, 24)))
    before = jnp.where(iota((24, 24), 0) < iota((24, 24), 1), 1.0, 0.0).astype(F32)
    rank = jnp.dot(marks.astype(BF16), before.astype(BF16), preferred_element_type=F32)
    wanted = jnp.where(slot < 8, slot, slot - 8).astype(F32)
    return jnp.where((rank == wanted) & (marks > 0.5), 1.0, 0.0).astype(F32)


def put_matrix(dest_row):
    r, c = iota((24, 24), 0), iota((24, 24), 1)
    wide = jnp.broadcast_to(dest_row, (24, 24))
    own = jnp.sum(jnp.where(r == c, wide, 0).astype(F32), axis=1, keepdims=True)
    rank_up = jnp.sum(jnp.where((c < r) & (wide == 1), 1.0, 0.0), axis=1, keepdims=True)
    rank_down = jnp.sum(jnp.where((c < r) & (wide == -1), 1.0, 0.0), axis=1, keepdims=True)
    slot = iota((24, 16), 1).astype(F32)
    hit_up = (own == 1.0) & (rank_up == slot)
    hit_down = (own == -1.0) & (rank_down + 8.0 == slot)
    return jnp.where(hit_up | hit_down, 1.0, 0.0).astype(F32)


def home_cells(cells, dest_row):
    r, c = iota((24, 24), 0), iota((24, 24), 1)
    wide = jnp.broadcast_to(dest_row, (24, 24))
    away = jnp.sum(jnp.where((r == c) & (wide != 0), 1.0, 0.0), axis=1, keepdims=True)
    row = jnp.where(away > 0.5, -1, cells >> 8)
    return row, cells & 255


def spread(line):
    return jnp.broadcast_to(line, (16, 128)).astype(BF16)


def row_numbers(count):
    at = iota((16, 128), 0)
    return [(at + 16 * q).astype(F32).astype(BF16) for q in range(count)]


def fill_columns(col, hot_ref):
    numbers = row_numbers(16)
    one, zero = jnp.ones((16, 128), BF16), jnp.zeros((16, 128), BF16)
    col = col.astype(F32)
    for k in range(8):
        here = spread(col[k : k + 1])
        for q in range(16):
            hot_ref[q * 16 : q * 16 + 16, k * 128 : (k + 1) * 128] = jnp.where(numbers[q] == here, one, zero)


def fill_values(row, highs, lows, load_ref):
    numbers = row_numbers(4)
    one, zero = jnp.ones((16, 128), BF16), jnp.zeros((16, 128), BF16)
    row = row.astype(F32)
    for k in range(8):
        here = spread(row[k : k + 1])
        masks = [numbers[q] == here for q in range(4)]
        values = [spread(x[k : k + 1]) for x in (*highs, *lows)] + [one]
        for part, value in enumerate(values[: load_ref.shape[0] // ROWS_A]):
            for q in range(4):
                at = part * ROWS_A + q * 16
                load_ref[at : at + 16, k * 128 : (k + 1) * 128] = jnp.where(masks[q], value, zero)


def scatter(load_ref, hot_ref):
    return lax.dot_general(
        load_ref[...], hot_ref[...], (((1,), (1,)), ((), ())), preferred_element_type=F32
    )


def gather(table, row, hot_ref):
    found = jnp.dot(table, hot_ref[...], preferred_element_type=F32)
    parts = found.shape[0] // FIELD_ROWS
    at = iota((ROWS_A, 128), 0)
    lines = [[], [], []]
    for k in range(8):
        mask = at == jnp.broadcast_to(row[k : k + 1], (ROWS_A, 128))
        for a in range(3):
            block = found[a * ROWS_A : (a + 1) * ROWS_A, k * 128 : (k + 1) * 128]
            for part in range(1, parts):
                base = part * FIELD_ROWS + a * ROWS_A
                block = block + found[base : base + ROWS_A, k * 128 : (k + 1) * 128]
            lines[a].append(jnp.sum(jnp.where(mask, block, 0.0), axis=0, keepdims=True))
    return [jnp.concatenate(line, axis=0) for line in lines]


def split_table(field, table_ref):
    hi, lo = hi_lo(field)
    table_ref[0:FIELD_ROWS] = hi.astype(BF16)
    table_ref[FIELD_ROWS : 2 * FIELD_ROWS] = lo.astype(BF16)


def push_of(sums, field):
    loads = sums[0:192] + sums[192:384]
    count = sums[384:448]
    return coupling * (loads - jnp.concatenate([count, count, count], axis=0) * field)


def plane(ref, a, z):
    base = (a * 4 + z) * 16
    return ref[base : base + 16, :].astype(F32)


def inner_tendency(f_ref, a, z):
    here = plane(f_ref, a, z)
    next_x = pltpu.roll(here, 255, 1)
    prev_x = pltpu.roll(here, 1, 1)
    across = next_x + prev_x - 4.0 * here
    slope_z = None
    if z < 3:
        next_z = plane(f_ref, a, z + 1)
        across = across + next_z
        slope_z = next_z
    if z > 0:
        prev_z = plane(f_ref, a, z - 1)
        across = across + prev_z
        slope_z = -prev_z if slope_z is None else slope_z - prev_z
    flow = plane(f_ref, 0, z) * (0.5 * (next_x - prev_x)) + plane(f_ref, 2, z) * (0.5 * slope_z)
    total = viscosity * across - flow
    return total + forcing if a == 0 else total


def below_term(f_ref, below):
    return (viscosity + 0.5 * plane(f_ref, 2, 0)) * below


def above_term(f_ref, above):
    return (viscosity - 0.5 * plane(f_ref, 2, 3)) * above


def lane_group(shape):
    return iota(shape, len(shape) - 1) // 32


def first_send(field_hbm, bubble_hbm, owner_hbm, dest_hbm, up_ref, down_ref, moved_ref,
               field_ref, bubble_ref, owner_ref, dest_ref, sems):
    pairs = ((dest_hbm, dest_ref), (owner_hbm, owner_ref), (bubble_hbm, bubble_ref), (field_hbm, field_ref))
    copies = [pltpu.make_async_copy(src, dst, sems.at[i]) for i, (src, dst) in enumerate(pairs)]
    for copy in copies:
        copy.start()
    for copy in copies[:3]:
        copy.wait()
    first, second = owner_ref[0], owner_ref[1]
    parts = []
    for a in range(3):
        parts += hi_lo(bubble_ref[a])
    parts += [((first >> 8) + 1).astype(F32), (first & 255).astype(F32)]
    parts = jnp.concatenate(parts, axis=1).astype(BF16)
    picked = jnp.dot(pick_matrix(dest_ref[0:1]).astype(BF16), parts, preferred_element_type=F32)
    later = jnp.concatenate([((second >> 8) + 1).astype(F32), (second & 255).astype(F32)], axis=1)
    later = jnp.dot(pick_matrix(dest_ref[1:2]).astype(BF16), later.astype(BF16), preferred_element_type=F32)
    moved_ref[...] = picked[:, 768:1024]
    for ref, at in ((up_ref, 0), (down_ref, 8)):
        lines = [picked[at : at + 8, i * 256 : (i + 1) * 256] for i in range(4)]
        lines += [later[at : at + 8], jnp.zeros((8, 256), F32)]
        ref[FIELD_ROWS:SEND_ROWS] = jnp.concatenate(lines, axis=0).astype(BF16)
    copies[3].wait()
    block = field_ref[...].astype(BF16)
    up_ref[0:FIELD_ROWS] = block
    down_ref[0:FIELD_ROWS] = block


def home_first(field_ref, bubble_ref, owner_ref, dest_ref, part_ref, seen_ref,
               table_ref, row_ref, col_ref, hot_ref, load_ref, sum_ref):
    field = field_ref[...]
    split_table(field, table_ref)
    row, col = home_cells(owner_ref[0], dest_ref[0:1])
    row_ref[...] = row
    col_ref[...] = col
    sum_ref[...] = jnp.zeros_like(sum_ref)

    def step(i, carry):
        rows = pl.ds(pl.multiple_of(i * 8, 8), 8)
        row8, col8 = row_ref[rows], col_ref[rows]
        fill_columns(col8, hot_ref)
        pairs = [hi_lo(bubble_ref[a, rows]) for a in range(3)]
        fill_values(row8, [p[0] for p in pairs], [p[1] for p in pairs], load_ref)
        seen = gather(table_ref[...], row8, hot_ref)
        for a in range(3):
            seen_ref[a, rows] = seen[a]
        sum_ref[...] += scatter(load_ref, hot_ref)
        return carry

    lax.fori_loop(0, 3, step, 0)
    push = push_of(sum_ref[...], field)
    for a in range(3):
        for z in range(4):
            base = (a * 4 + z) * 16
            part_ref[base : base + 16] = inner_tendency(field_ref, a, z) + push[base : base + 16]


def tail_of(ref):
    return ref[FIELD_ROWS:SEND_ROWS, :].astype(F32)


def tail_cells(tail, line):
    at = tail[line * 8 : line * 8 + 8].astype(jnp.int32)
    return at[:, 0:128] - 1, at[:, 128:256]


def pack_pair(six, out_ref):
    group = lane_group((16, 128))
    group8 = lane_group((8, 128))
    for z in range(4):
        for half in range(2):
            tiles = [six[i][z][:, half * 128 : (half + 1) * 128] for i in range(6)]
            for o in range(4):
                def moved(x, target):
                    shift = ((target - o) % 4) * 32
                    return x if shift == 0 else pltpu.roll(x, shift, 1)
                main = moved(tiles[3], 3)
                for i in range(3):
                    main = jnp.where(group == i, moved(tiles[i], i), main)
                rest = moved(tiles[5][8:16], 3)
                rest = jnp.where(group8 == 2, moved(tiles[4][8:16], 2), rest)
                rest = jnp.where(group8 == 1, moved(tiles[5][0:8], 1), rest)
                rest = jnp.where(group8 == 0, moved(tiles[4][0:8], 0), rest)
                peer = z * 8 + half * 4 + o
                out_ref[peer] = jnp.concatenate([main, rest], axis=0).astype(BF16)


def unpack(ref, second, a, z):
    halves = []
    group = lane_group((16, 128))
    for half in range(2):
        total = None
        for o in range(4):
            chunk = ref[z * 8 + half * 4 + o].astype(F32)
            if not second:
                piece, at = chunk[0:16], a
            elif a == 0:
                piece, at = chunk[0:16], 3
            else:
                rest = chunk[16:24]
                piece, at = jnp.concatenate([rest, pltpu.roll(rest, 64, 1)], axis=0), a - 1
            shift = ((o - at) % 4) * 32
            piece = piece if shift == 0 else pltpu.roll(piece, shift, 1)
            total = piece if total is None else jnp.where(group == o, piece, total)
        halves.append(total)
    return jnp.concatenate(halves, axis=1)


def arrived(cells_ref, values_ref, first_line, cell_line, load_ref):
    row, col = tail_cells(tail_of(cells_ref), cell_line)
    tail = values_ref[first_line : first_line + 48, :].astype(F32)
    highs = [tail[a * 8 : a * 8 + 8, 0:128] for a in range(3)]
    lows = [tail[a * 8 : a * 8 + 8, 128:256] for a in range(3)]
    fill_values(row, highs, lows, load_ref)
    return col


def low_first(field_ref, part_ref, low_ref, out_ref, hot_ref, load_ref):
    fill_columns(arrived(low_ref, low_ref, FIELD_ROWS, 3, load_ref), hot_ref)
    push = push_of(scatter(load_ref, hot_ref), field_ref[...])
    for a in range(3):
        for z in range(4):
            base = (a * 4 + z) * 16
            total = part_ref[base : base + 16] + push[base : base + 16]
            out_ref[base : base + 16] = total + below_term(field_ref, plane(low_ref, a, 3)) if z == 0 else total


def high_first(field_ref, part_ref, high_ref, tend_ref, send_ref, hot_ref, load_ref):
    fill_columns(arrived(high_ref, high_ref, FIELD_ROWS, 3, load_ref), hot_ref)
    push = push_of(scatter(load_ref, hot_ref), field_ref[...])
    six = [[None] * 4 for _ in range(6)]
    for a in range(3):
        for z in range(4):
            base = (a * 4 + z) * 16
            total = part_ref[base : base + 16] + push[base : base + 16]
            if z == 3:
                total = total + above_term(field_ref, plane(high_ref, a, 0))
            tend_ref[base : base + 16] = total
            here = field_ref[base : base + 16]
            six[a][z] = here
            six[3 + a][z] = (here - here.astype(BF16).astype(F32)) + C1 * total
    pack_pair(six, send_ref)


def bubbles_first(low_ref, high_ref, moved_ref, seen_ref, bubble_ref, owner_ref, dest_ref,
                  rate_ref, next_ref, slots_ref, sum_ref, come_ref,
                  row_ref, col_ref, hot_ref, load_ref, ones_ref):
    found = [[], [], []]
    for at, ref in ((0, high_ref), (8, low_ref)):
        cells = moved_ref[at : at + 8].astype(jnp.int32)
        fill_columns(cells[:, 128:256], hot_ref)
        seen = gather(ref[0:FIELD_ROWS], cells[:, 0:128] - 1, hot_ref)
        for a in range(3):
            found[a].append(seen[a])
    found = jnp.concatenate([jnp.concatenate(f, axis=0) for f in found], axis=1)
    back = exact_dot(put_matrix(dest_ref[0:1]), found)
    after = []
    for a in range(3):
        here = bubble_ref[a]
        rate = (seen_ref[a] + back[:, a * 128 : (a + 1) * 128] - here) / relax_time
        if a == 1:
            rate = rate + buoyancy
        rate_ref[a] = rate
        after.append(here + C1 * rate)
        next_ref[a] = after[a]
    picked = exact_dot(pick_matrix(dest_ref[1:2]), jnp.concatenate(after, axis=1))
    for at in (0, 8):
        for a in range(3):
            line = at * 3 + a * 8
            slots_ref[line : line + 8] = jnp.concatenate(
                hi_lo(picked[at : at + 8, a * 128 : (a + 1) * 128]), axis=1
            )
    row, col = home_cells(owner_ref[1], dest_ref[1:2])
    row_ref[...] = row
    col_ref[...] = col
    sum_ref[...] = jnp.zeros_like(sum_ref)

    def step(i, carry):
        rows = pl.ds(pl.multiple_of(i * 8, 8), 8)
        fill_columns(col_ref[rows], hot_ref)
        pairs = [hi_lo(next_ref[a, rows]) for a in range(3)]
        fill_values(row_ref[rows], [p[0] for p in pairs], [p[1] for p in pairs], load_ref)
        sum_ref[...] += scatter(load_ref, hot_ref)
        return carry

    lax.fori_loop(0, 3, step, 0)
    for i, ref in enumerate((low_ref, high_ref)):
        row, col = tail_cells(tail_of(ref), 4)
        fill_columns(col, come_ref.at[i])
        fill_values(row, (), (), ones_ref)
        sum_ref[384:448] += scatter(ones_ref, come_ref.at[i])


def columns_body(got_ref, first_ref, second_ref, send_ref):
    got = got_ref[...].astype(F32)
    main = got[:, 0:16].reshape(512, 128)
    rest = got[:, 16:24].reshape(256, 128)
    other = pltpu.roll(rest, 64, 1)
    rest = jnp.concatenate([rest.reshape(32, 8, 128), other.reshape(32, 8, 128)], axis=1).reshape(512, 128)
    group = lane_group((512, 128))
    gain = jnp.where(group == 0, pltpu.roll(main, 32, 1), pltpu.roll(rest, 32, 1))

    def wall(x):
        field = x.astype(BF16)
        wide = field.astype(F32)
        normal = jnp.where(group == 0, pltpu.roll(wide, 96, 1), jnp.where(group == 2, pltpu.roll(wide, 32, 1), wide))
        slopes = jnp.dot(first_ref[...], field, preferred_element_type=F32).astype(BF16).astype(F32)
        curves = jnp.dot(second_ref[...], field, preferred_element_type=F32).astype(BF16).astype(F32)
        return (viscosity * curves - normal * slopes).astype(BF16).astype(F32)

    wall_1 = wall(main)
    wall_2 = wall(main + (gain + C1 * wall_1))
    back = pltpu.roll(wall_2, 96, 1)
    ahead = pltpu.roll(wall_2, 32, 1)
    out = jnp.where(group == 3, back, wall_1).reshape(32, 16, 128)
    group8 = lane_group((32, 8, 128))
    tail = jnp.where(group8 < 2, back.reshape(32, 16, 128)[:, 0:8], ahead.reshape(32, 16, 128)[:, 8:16])
    send_ref[...] = jnp.concatenate([out, tail], axis=1).astype(BF16)


def middle_body(wall_ref, field_ref, part_ref, low_ref, high_ref, slots_ref, come_ref,
                next_ref, tend_ref, up_ref, down_ref, table_ref):
    for a in range(3):
        for z in range(4):
            base = (a * 4 + z) * 16
            total = part_ref[base : base + 16] + unpack(wall_ref, False, a, z)
            tend_ref[base : base + 16] = total
            next_ref[base : base + 16] = field_ref[base : base + 16] + C1 * total
    split_table(next_ref[...], table_ref)
    ends = ((low_ref, down_ref, 0, 24), (high_ref, up_ref, 3, 0))
    for i, (ref, out_ref, z, at) in enumerate(ends):
        row, _ = tail_cells(tail_of(ref), 4)
        seen = gather(table_ref[...], row, come_ref.at[i])
        lines = [plane(next_ref, a, z) for a in range(3)]
        lines.append(slots_ref[at : at + 24])
        lines += [jnp.concatenate(hi_lo(seen[a]), axis=1) for a in range(3)]
        out_ref[...] = jnp.concatenate(lines, axis=0).astype(BF16)


def home_second(wall_ref, field_ref, tend_ref, sum_ref, bubble_ref, rate_ref, owner_ref, dest_ref,
                base_ref, late_ref, table_ref, row_ref, col_ref, hot_ref):
    field = field_ref[...]
    push = push_of(sum_ref[...], field)
    for a in range(3):
        for z in range(4):
            base = (a * 4 + z) * 16
            total = inner_tendency(field_ref, a, z) + push[base : base + 16] + unpack(wall_ref, True, a, z)
            earlier = tend_ref[base : base + 16]
            base_ref[base : base + 16] = field_ref[base : base + 16] + (C2 * total + E2 * earlier)
    split_table(field, table_ref)
    row, col = home_cells(owner_ref[1], dest_ref[1:2])
    row_ref[...] = row
    col_ref[...] = col

    def step(i, carry):
        rows = pl.ds(pl.multiple_of(i * 8, 8), 8)
        fill_columns(col_ref[rows], hot_ref)
        seen = gather(table_ref[...], row_ref[rows], hot_ref)
        for a in range(3):
            here = bubble_ref[a, rows]
            rate = (seen[a] - here) / relax_time
            if a == 1:
                rate = rate + buoyancy
            late_ref[a, rows] = here + (C2 * rate + E2 * rate_ref[a, rows])
        return carry

    lax.fori_loop(0, 3, step, 0)


def late_sum(cells_ref, values_ref, i, come_ref, load_ref):
    arrived(cells_ref, values_ref, 48, 4, load_ref)
    sums = scatter(load_ref, come_ref.at[i])
    return C2 * coupling * (sums[0:192] + sums[192:384])


def low_second(base_ref, field_ref, low_ref, low2_ref, come_ref, out_ref, load_ref):
    push = late_sum(low_ref, low2_ref, 0, come_ref, load_ref)
    for a in range(3):
        for z in range(4):
            base = (a * 4 + z) * 16
            total = base_ref[base : base + 16] + push[base : base + 16]
            if z == 0:
                total = total + C2 * below_term(field_ref, low2_ref[a * 16 : a * 16 + 16, :].astype(F32))
            out_ref[base : base + 16] = total


def high_second(base_ref, field_ref, high_ref, low2_ref, high2_ref, late_ref, dest_ref, come_ref,
                out_ref, bubble_ref, load_ref):
    found = []
    from_low, from_high = low2_ref[48:96, :].astype(F32), high2_ref[48:96, :].astype(F32)
    for a in range(3):
        line = 24 + a * 8
        high = from_high[line : line + 8, 0:128] + from_high[line : line + 8, 128:256]
        low = from_low[line : line + 8, 0:128] + from_low[line : line + 8, 128:256]
        found.append(jnp.concatenate([high, low], axis=0))
    back = exact_dot(put_matrix(dest_ref[1:2]), jnp.concatenate(found, axis=1))
    for a in range(3):
        bubble_ref[a] = late_ref[a] + (C2 / relax_time) * back[:, a * 128 : (a + 1) * 128]
    push = late_sum(high_ref, high2_ref, 1, come_ref, load_ref)
    for a in range(3):
        for z in range(4):
            base = (a * 4 + z) * 16
            total = base_ref[base : base + 16] + push[base : base + 16]
            if z == 3:
                total = total + C2 * above_term(field_ref, high2_ref[a * 16 : a * 16 + 16, :].astype(F32))
            out_ref[base : base + 16] = total


def shifted(x, by):
    length = lax.axis_size("pz")
    return lax.ppermute(x, "pz", [(i, (i + by) % length) for i in range(length)])


def exchange(x):
    return lax.all_to_all(x, "px", split_axis=0, concat_axis=0, tiled=True)


def on_device(velocity, first_deriv, second_deriv, bubble_vel, owner, dest):
    field = velocity.reshape(FIELD_ROWS, 256)
    block = ((FIELD_ROWS, 256), F32)
    rows = ((3, 24, 128), F32)
    hot = pltpu.VMEM((256, 1024), BF16)
    load = pltpu.VMEM((448, 1024), BF16)
    table = pltpu.VMEM((384, 256), BF16)
    ids = pltpu.VMEM((24, 128), jnp.int32)
    packed = ((32, 24, 128), BF16)

    velocity_in, bubbles_in, owner_in, dest_in = (
        pltpu.with_memory_space_constraint(x, pltpu.HBM) for x in (field, bubble_vel, owner, dest)
    )
    up, down, moved, field, bubble_vel, owner, dest = pl.pallas_call(
        first_send,
        in_specs=[pl.BlockSpec(memory_space=pltpu.HBM)] * 4,
        out_shape=(
            pltpu.VMEM((SEND_ROWS, 256), BF16),
            pltpu.VMEM((SEND_ROWS, 256), BF16),
            pltpu.VMEM((16, 256), F32),
            pltpu.VMEM((FIELD_ROWS, 256), F32),
            pltpu.VMEM((3, 24, 128), F32),
            pltpu.VMEM((2, 24, 128), jnp.int32),
            pltpu.VMEM((2, 24), jnp.int32),
        ),
        scratch_shapes=[pltpu.SemaphoreType.DMA((4,))],
    )(velocity_in, bubbles_in, owner_in, dest_in)
    low, high = shifted(up, 1), shifted(down, -1)
    part, seen = call(
        home_first, (block, rows), (table, ids, ids, hot, load, pltpu.VMEM((448, 256), F32))
    )(field, bubble_vel, owner, dest)
    (part,) = call(low_first, (block,), (hot, load))(field, part, low)
    part, to_columns = call(high_first, (block, packed), (hot, load))(field, part, high)
    columns = exchange(to_columns)
    rate, bubbles, slots, sums, come = call(
        bubbles_first,
        (rows, rows, ((48, 256), F32), ((448, 256), F32), ((2, 256, 1024), BF16)),
        (ids, ids, hot, load, pltpu.VMEM((64, 1024), BF16)),
    )(low, high, moved, seen, bubble_vel, owner, dest)
    (walls,) = call(columns_body, (packed,))(columns, first_deriv, second_deriv)
    walls = exchange(walls)
    lasts = ((LAST_ROWS, 256), BF16)
    middle, tend, up, down = call(middle_body, (block, block, lasts, lasts), (table,))(
        walls, field, part, low, high, slots, come
    )
    low2, high2 = shifted(up, 1), shifted(down, -1)
    base, late = call(home_second, (block, rows), (table, ids, ids, hot))(
        walls, middle, tend, sums, bubbles, rate, owner, dest
    )
    late_load = pltpu.VMEM((384, 1024), BF16)
    (base,) = call(low_second, (block,), (late_load,))(base, middle, low, low2, come)
    field, bubbles = call(high_second, (block, rows), (late_load,))(
        base, middle, high, low2, high2, late, dest, come
    )
    return (field.reshape(velocity.shape), bubbles)


def solution(mesh):
    return jax.shard_map(
        on_device,
        mesh=mesh,
        in_specs=(
            P(None, "pz", "px", None),
            P(),
            P(),
            P(None, ("px", "pz"), None),
            P(None, ("px", "pz"), None),
            P(None, ("px", "pz")),
        ),
        out_specs=(P(None, "pz", "px", None), P(None, ("px", "pz"), None)),
        check_vma=False,
    )
```

```python
import functools

import jax
import jax.numpy as jnp
from jax import lax
from jax.experimental import pallas as pl
from jax.experimental.pallas import tpu as pltpu
from jax.sharding import PartitionSpec as P

step_size = 0.5
viscosity = 0.4
relax_time = 0.5
coupling = 2.0
buoyancy = 0.5
forcing = 1.0
gammas = (8.0 / 15.0, 5.0 / 12.0)
zetas = (0.0, -17.0 / 60.0)

F32 = jnp.float32
BF16 = jnp.bfloat16
C1 = step_size * gammas[0]
C2 = step_size * gammas[1]
E2 = step_size * zetas[1]

ROWS_A = 64
FIELD_ROWS = 192
SEND_ROWS = 240
LAST_ROWS = 96


def iota(shape, dim):
    return lax.broadcasted_iota(jnp.int32, shape, dim)


def call(body, outs, scratch=()):
    return pl.pallas_call(
        body,
        out_shape=tuple(jax.ShapeDtypeStruct(s, d) for s, d in outs),
        scratch_shapes=list(scratch),
        compiler_params=pltpu.CompilerParams(vmem_limit_bytes=48 * 1024 * 1024),
    )


def hi_lo(x):
    hi = x.astype(BF16).astype(F32)
    return hi, x - hi


def pick_matrix(dest_row):
    up = jnp.where(dest_row == 1, 1.0, 0.0).astype(F32)
    down = jnp.where(dest_row == -1, 1.0, 0.0).astype(F32)
    slot = iota((16, 24), 0)
    marks = jnp.where(slot < 8, jnp.broadcast_to(up, (16, 24)), jnp.broadcast_to(down, (16, 24)))
    before = jnp.where(iota((24, 24), 0) < iota((24, 24), 1), 1.0, 0.0).astype(F32)
    rank = jnp.dot(marks.astype(BF16), before.astype(BF16), preferred_element_type=F32)
    wanted = jnp.where(slot < 8, slot, slot - 8).astype(F32)
    return jnp.where((rank == wanted) & (marks > 0.5), 1.0, 0.0).astype(F32)


def put_matrix(dest_row):
    r, c = iota((24, 24), 0), iota((24, 24), 1)
    wide = jnp.broadcast_to(dest_row, (24, 24))
    own = jnp.sum(jnp.where(r == c, wide, 0).astype(F32), axis=1, keepdims=True)
    rank_up = jnp.sum(jnp.where((c < r) & (wide == 1), 1.0, 0.0), axis=1, keepdims=True)
    rank_down = jnp.sum(jnp.where((c < r) & (wide == -1), 1.0, 0.0), axis=1, keepdims=True)
    slot = iota((24, 16), 1).astype(F32)
    hit_up = (own == 1.0) & (rank_up == slot)
    hit_down = (own == -1.0) & (rank_down + 8.0 == slot)
    return jnp.where(hit_up | hit_down, 1.0, 0.0).astype(F32)


def home_cells(cells, dest_row):
    r, c = iota((24, 24), 0), iota((24, 24), 1)
    wide = jnp.broadcast_to(dest_row, (24, 24))
    away = jnp.sum(jnp.where((r == c) & (wide != 0), 1.0, 0.0), axis=1, keepdims=True)
    row = jnp.where(away > 0.5, -1, cells >> 8)
    return row, cells & 255


def spread(line):
    return jnp.broadcast_to(line, (16, 128)).astype(BF16)


def row_numbers(count):
    at = iota((16, 128), 0)
    return [(at + 16 * q).astype(F32).astype(BF16) for q in range(count)]


def fill_columns(col, hot_ref):
    numbers = row_numbers(16)
    one, zero = jnp.ones((16, 128), BF16), jnp.zeros((16, 128), BF16)
    col = col.astype(F32)
    for k in range(8):
        here = spread(col[k : k + 1])
        for q in range(16):
            hot_ref[q * 16 : q * 16 + 16, k * 128 : (k + 1) * 128] = jnp.where(numbers[q] == here, one, zero)


def fill_values(row, highs, lows, load_ref):
    numbers = row_numbers(4)
    one, zero = jnp.ones((16, 128), BF16), jnp.zeros((16, 128), BF16)
    row = row.astype(F32)
    for k in range(8):
        here = spread(row[k : k + 1])
        masks = [numbers[q] == here for q in range(4)]
        values = [spread(x[k : k + 1]) for x in (*highs, *lows)] + [one]
        for part, value in enumerate(values[: load_ref.shape[0] // ROWS_A]):
            for q in range(4):
                at = part * ROWS_A + q * 16
                load_ref[at : at + 16, k * 128 : (k + 1) * 128] = jnp.where(masks[q], value, zero)


def scatter(load_ref, hot_ref):
    return lax.dot_general(
        load_ref[...], hot_ref[...], (((1,), (1,)), ((), ())), preferred_element_type=F32
    )


def gather(table, row, hot_ref):
    found = jnp.dot(table, hot_ref[...], preferred_element_type=F32)
    parts = found.shape[0] // FIELD_ROWS
    at = iota((ROWS_A, 128), 0)
    lines = [[], [], []]
    for k in range(8):
        mask = at == jnp.broadcast_to(row[k : k + 1], (ROWS_A, 128))
        for a in range(3):
            block = found[a * ROWS_A : (a + 1) * ROWS_A, k * 128 : (k + 1) * 128]
            for part in range(1, parts):
                base = part * FIELD_ROWS + a * ROWS_A
                block = block + found[base : base + ROWS_A, k * 128 : (k + 1) * 128]
            lines[a].append(jnp.sum(jnp.where(mask, block, 0.0), axis=0, keepdims=True))
    return [jnp.concatenate(line, axis=0) for line in lines]


def split_table(field, table_ref):
    hi, lo = hi_lo(field)
    table_ref[0:FIELD_ROWS] = hi.astype(BF16)
    table_ref[FIELD_ROWS : 2 * FIELD_ROWS] = lo.astype(BF16)


def push_of(sums, field):
    loads = sums[0:192] + sums[192:384]
    count = sums[384:448]
    return coupling * (loads - jnp.concatenate([count, count, count], axis=0) * field)


def plane(ref, a, z):
    base = (a * 4 + z) * 16
    return ref[base : base + 16, :].astype(F32)


def inner_tendency(f_ref, a, z):
    here = plane(f_ref, a, z)
    next_x = pltpu.roll(here, 255, 1)
    prev_x = pltpu.roll(here, 1, 1)
    across = next_x + prev_x - 4.0 * here
    slope_z = None
    if z < 3:
        next_z = plane(f_ref, a, z + 1)
        across = across + next_z
        slope_z = next_z
    if z > 0:
        prev_z = plane(f_ref, a, z - 1)
        across = across + prev_z
        slope_z = -prev_z if slope_z is None else slope_z - prev_z
    flow = plane(f_ref, 0, z) * (0.5 * (next_x - prev_x)) + plane(f_ref, 2, z) * (0.5 * slope_z)
    total = viscosity * across - flow
    return total + forcing if a == 0 else total


def below_term(f_ref, below):
    return (viscosity + 0.5 * plane(f_ref, 2, 0)) * below


def above_term(f_ref, above):
    return (viscosity - 0.5 * plane(f_ref, 2, 3)) * above


def lane_group(shape):
    return iota(shape, len(shape) - 1) // 32


def first_send(field_hbm, bubble_hbm, owner_hbm, dest_hbm, up_ref, down_ref, moved_ref,
               field_ref, bubble_ref, owner_ref, dest_ref, sems):
    pairs = ((dest_hbm, dest_ref), (owner_hbm, owner_ref), (bubble_hbm, bubble_ref), (field_hbm, field_ref))
    copies = [pltpu.make_async_copy(src, dst, sems.at[i]) for i, (src, dst) in enumerate(pairs)]
    for copy in copies:
        copy.start()
    for copy in copies[:3]:
        copy.wait()
    first, second = owner_ref[0], owner_ref[1]
    parts = []
    for a in range(3):
        parts += hi_lo(bubble_ref[a])
    parts += [((first >> 8) + 1).astype(F32), (first & 255).astype(F32)]
    parts = jnp.concatenate(parts, axis=1).astype(BF16)
    picked = jnp.dot(pick_matrix(dest_ref[0:1]).astype(BF16), parts, preferred_element_type=F32)
    later = jnp.concatenate([((second >> 8) + 1).astype(F32), (second & 255).astype(F32)], axis=1)
    later = jnp.dot(pick_matrix(dest_ref[1:2]).astype(BF16), later.astype(BF16), preferred_element_type=F32)
    moved_ref[...] = picked[:, 768:1024]
    for ref, at in ((up_ref, 0), (down_ref, 8)):
        lines = [picked[at : at + 8, i * 256 : (i + 1) * 256] for i in range(4)]
        lines += [later[at : at + 8], jnp.zeros((8, 256), F32)]
        ref[FIELD_ROWS:SEND_ROWS] = jnp.concatenate(lines, axis=0).astype(BF16)
    copies[3].wait()
    block = field_ref[...].astype(BF16)
    up_ref[0:FIELD_ROWS] = block
    down_ref[0:FIELD_ROWS] = block


def home_first(field_ref, bubble_ref, owner_ref, dest_ref, part_ref, seen_ref, put_ref, pick_ref,
               table_ref, row_ref, col_ref, hot_ref, load_ref, sum_ref):
    field = field_ref[...]
    split_table(field, table_ref)
    put_ref[...] = put_matrix(dest_ref[0:1])
    pick_ref[...] = pick_matrix(dest_ref[1:2])
    row, col = home_cells(owner_ref[0], dest_ref[0:1])
    row_ref[...] = row
    col_ref[...] = col
    sum_ref[...] = jnp.zeros_like(sum_ref)

    def step(i, carry):
        rows = pl.ds(pl.multiple_of(i * 8, 8), 8)
        row8, col8 = row_ref[rows], col_ref[rows]
        fill_columns(col8, hot_ref)
        pairs = [hi_lo(bubble_ref[a, rows]) for a in range(3)]
        fill_values(row8, [p[0] for p in pairs], [p[1] for p in pairs], load_ref)
        seen = gather(table_ref[...], row8, hot_ref)
        for a in range(3):
            seen_ref[a, rows] = seen[a]
        sum_ref[...] += scatter(load_ref, hot_ref)
        return carry

    lax.fori_loop(0, 3, step, 0)
    push = push_of(sum_ref[...], field)
    for a in range(3):
        for z in range(4):
            base = (a * 4 + z) * 16
            part_ref[base : base + 16] = inner_tendency(field_ref, a, z) + push[base : base + 16]


def tail_of(ref):
    return ref[FIELD_ROWS:SEND_ROWS, :].astype(F32)


def tail_cells(tail, line):
    at = tail[line * 8 : line * 8 + 8].astype(jnp.int32)
    return at[:, 0:128] - 1, at[:, 128:256]


def pack_pair(six, out_ref):
    group = lane_group((16, 128))
    group8 = lane_group((8, 128))
    for z in range(4):
        for half in range(2):
            tiles = [six[i][z][:, half * 128 : (half + 1) * 128] for i in range(6)]
            for o in range(4):
                def moved(x, target):
                    shift = ((target - o) % 4) * 32
                    return x if shift == 0 else pltpu.roll(x, shift, 1)
                main = moved(tiles[3], 3)
                for i in range(3):
                    main = jnp.where(group == i, moved(tiles[i], i), main)
                rest = moved(tiles[5][8:16], 3)
                rest = jnp.where(group8 == 2, moved(tiles[4][8:16], 2), rest)
                rest = jnp.where(group8 == 1, moved(tiles[5][0:8], 1), rest)
                rest = jnp.where(group8 == 0, moved(tiles[4][0:8], 0), rest)
                peer = z * 8 + half * 4 + o
                out_ref[peer] = jnp.concatenate([main, rest], axis=0).astype(BF16)


def unpack(ref, second, a, z):
    halves = []
    group = lane_group((16, 128))
    for half in range(2):
        total = None
        for o in range(4):
            chunk = ref[z * 8 + half * 4 + o].astype(F32)
            if not second:
                piece, at = chunk[0:16], a
            elif a == 0:
                piece, at = chunk[0:16], 3
            else:
                rest = chunk[16:24]
                piece, at = jnp.concatenate([rest, pltpu.roll(rest, 64, 1)], axis=0), a - 1
            shift = ((o - at) % 4) * 32
            piece = piece if shift == 0 else pltpu.roll(piece, shift, 1)
            total = piece if total is None else jnp.where(group == o, piece, total)
        halves.append(total)
    return jnp.concatenate(halves, axis=1)


def arrived(cells_ref, values_ref, first_line, cell_line, load_ref):
    row, col = tail_cells(tail_of(cells_ref), cell_line)
    tail = values_ref[first_line : first_line + 48, :].astype(F32)
    highs = [tail[a * 8 : a * 8 + 8, 0:128] for a in range(3)]
    lows = [tail[a * 8 : a * 8 + 8, 128:256] for a in range(3)]
    fill_values(row, highs, lows, load_ref)
    return col


def seen_afar(moved_ref, at, far_ref, hot_ref):
    cells = moved_ref[at : at + 8].astype(jnp.int32)
    fill_columns(cells[:, 128:256], hot_ref)
    return gather(far_ref[0:FIELD_ROWS], cells[:, 0:128] - 1, hot_ref)


def low_first(field_ref, part_ref, low_ref, moved_ref, out_ref, afar_ref, come_ref, hot_ref, load_ref):
    fill_columns(tail_cells(tail_of(low_ref), 4)[1], come_ref)
    for a, line in enumerate(seen_afar(moved_ref, 8, low_ref, hot_ref)):
        afar_ref[a] = line
    fill_columns(arrived(low_ref, low_ref, FIELD_ROWS, 3, load_ref), hot_ref)
    push = push_of(scatter(load_ref, hot_ref), field_ref[...])
    for a in range(3):
        for z in range(4):
            base = (a * 4 + z) * 16
            total = part_ref[base : base + 16] + push[base : base + 16]
            out_ref[base : base + 16] = total + below_term(field_ref, plane(low_ref, a, 3)) if z == 0 else total


def high_first(field_ref, part_ref, high_ref, moved_ref, afar_ref, seen_ref, bubble_ref, put_ref, pick_ref,
               tend_ref, send_ref, rate_ref, next_ref, slots_ref, come_ref, hot_ref, load_ref):
    fill_columns(tail_cells(tail_of(high_ref), 4)[1], come_ref)
    near = seen_afar(moved_ref, 0, high_ref, hot_ref)
    found = jnp.concatenate([jnp.concatenate([near[a], afar_ref[a]], axis=0) for a in range(3)], axis=1)
    back = jnp.dot(put_ref[...].astype(BF16), found.astype(BF16), preferred_element_type=F32)
    after = []
    for a in range(3):
        here = bubble_ref[a]
        rate = (seen_ref[a] + back[:, a * 128 : (a + 1) * 128] - here) / relax_time
        if a == 1:
            rate = rate + buoyancy
        rate_ref[a] = rate
        after.append(here + C1 * rate)
        next_ref[a] = after[a]
    parts = jnp.concatenate([piece for x in after for piece in hi_lo(x)], axis=1).astype(BF16)
    picked = jnp.dot(pick_ref[...].astype(BF16), parts, preferred_element_type=F32)
    for at in (0, 8):
        for a in range(3):
            line = at * 3 + a * 8
            slots_ref[line : line + 8] = picked[at : at + 8, a * 256 : (a + 1) * 256]
    fill_columns(arrived(high_ref, high_ref, FIELD_ROWS, 3, load_ref), hot_ref)
    push = push_of(scatter(load_ref, hot_ref), field_ref[...])
    six = [[None] * 4 for _ in range(6)]
    for a in range(3):
        for z in range(4):
            base = (a * 4 + z) * 16
            total = part_ref[base : base + 16] + push[base : base + 16]
            if z == 3:
                total = total + above_term(field_ref, plane(high_ref, a, 0))
            tend_ref[base : base + 16] = total
            here = field_ref[base : base + 16]
            six[a][z] = here
            six[3 + a][z] = (here - here.astype(BF16).astype(F32)) + C1 * total
    pack_pair(six, send_ref)


def columns_body(got_ref, first_ref, second_ref, send_ref):
    got = got_ref[...].astype(F32)
    main = got[:, 0:16].reshape(512, 128)
    rest = got[:, 16:24].reshape(256, 128)
    other = pltpu.roll(rest, 64, 1)
    rest = jnp.concatenate([rest.reshape(32, 8, 128), other.reshape(32, 8, 128)], axis=1).reshape(512, 128)
    group = lane_group((512, 128))
    gain = jnp.where(group == 0, pltpu.roll(main, 32, 1), pltpu.roll(rest, 32, 1))

    def wall(x):
        field = x.astype(BF16)
        wide = field.astype(F32)
        normal = jnp.where(group == 0, pltpu.roll(wide, 96, 1), jnp.where(group == 2, pltpu.roll(wide, 32, 1), wide))
        slopes = jnp.dot(first_ref[...], field, preferred_element_type=F32).astype(BF16).astype(F32)
        curves = jnp.dot(second_ref[...], field, preferred_element_type=F32).astype(BF16).astype(F32)
        return (viscosity * curves - normal * slopes).astype(BF16).astype(F32)

    wall_1 = wall(main)
    wall_2 = wall(main + (gain + C1 * wall_1))
    back = pltpu.roll(wall_2, 96, 1)
    ahead = pltpu.roll(wall_2, 32, 1)
    out = jnp.where(group == 3, back, wall_1).reshape(32, 16, 128)
    group8 = lane_group((32, 8, 128))
    tail = jnp.where(group8 < 2, back.reshape(32, 16, 128)[:, 0:8], ahead.reshape(32, 16, 128)[:, 8:16])
    send_ref[...] = jnp.concatenate([out, tail], axis=1).astype(BF16)


def middle_body(wall_ref, field_ref, part_ref, low_ref, high_ref, slots_ref, come_low_ref, come_high_ref,
                next_ref, tend_ref, up_ref, down_ref, table_ref):
    for a in range(3):
        for z in range(4):
            base = (a * 4 + z) * 16
            total = part_ref[base : base + 16] + unpack(wall_ref, False, a, z)
            tend_ref[base : base + 16] = total
            next_ref[base : base + 16] = field_ref[base : base + 16] + C1 * total
    split_table(next_ref[...], table_ref)
    ends = ((low_ref, come_low_ref, down_ref, 0, 24), (high_ref, come_high_ref, up_ref, 3, 0))
    for ref, come_ref, out_ref, z, at in ends:
        row, _ = tail_cells(tail_of(ref), 4)
        seen = gather(table_ref[...], row, come_ref)
        lines = [plane(next_ref, a, z) for a in range(3)]
        lines.append(slots_ref[at : at + 24])
        lines += [jnp.concatenate(hi_lo(seen[a]), axis=1) for a in range(3)]
        out_ref[...] = jnp.concatenate(lines, axis=0).astype(BF16)


def home_second(wall_ref, field_ref, tend_ref, bubble_ref, rate_ref, owner_ref, dest_ref,
                base_ref, late_ref, put_ref, table_ref, row_ref, col_ref, hot_ref, load_ref, sum_ref):
    field = field_ref[...]
    split_table(field, table_ref)
    put_ref[...] = put_matrix(dest_ref[1:2])
    row, col = home_cells(owner_ref[1], dest_ref[1:2])
    row_ref[...] = row
    col_ref[...] = col
    sum_ref[...] = jnp.zeros_like(sum_ref)

    def step(i, carry):
        rows = pl.ds(pl.multiple_of(i * 8, 8), 8)
        row8 = row_ref[rows]
        fill_columns(col_ref[rows], hot_ref)
        pairs = [hi_lo(bubble_ref[a, rows]) for a in range(3)]
        fill_values(row8, [p[0] for p in pairs], [p[1] for p in pairs], load_ref)
        seen = gather(table_ref[...], row8, hot_ref)
        for a in range(3):
            here = bubble_ref[a, rows]
            rate = (seen[a] - here) / relax_time
            if a == 1:
                rate = rate + buoyancy
            late_ref[a, rows] = here + (C2 * rate + E2 * rate_ref[a, rows])
        sum_ref[...] += scatter(load_ref, hot_ref)
        return carry

    lax.fori_loop(0, 3, step, 0)
    push = push_of(sum_ref[...], field)
    for a in range(3):
        for z in range(4):
            base = (a * 4 + z) * 16
            total = inner_tendency(field_ref, a, z) + push[base : base + 16] + unpack(wall_ref, True, a, z)
            earlier = tend_ref[base : base + 16]
            base_ref[base : base + 16] = field_ref[base : base + 16] + (C2 * total + E2 * earlier)


def late_push(cells_ref, values_ref, field_ref, come_ref, load_ref):
    arrived(cells_ref, values_ref, 48, 4, load_ref)
    return push_of(scatter(load_ref, come_ref), field_ref[...])


def low_second(base_ref, field_ref, low_ref, low2_ref, come_ref, out_ref, load_ref):
    push = late_push(low_ref, low2_ref, field_ref, come_ref, load_ref)
    for a in range(3):
        for z in range(4):
            base = (a * 4 + z) * 16
            total = base_ref[base : base + 16] + C2 * push[base : base + 16]
            if z == 0:
                total = total + C2 * below_term(field_ref, low2_ref[a * 16 : a * 16 + 16, :].astype(F32))
            out_ref[base : base + 16] = total


def high_second(base_ref, field_ref, high_ref, low2_ref, high2_ref, late_ref, put_ref, come_ref,
                out_ref, bubble_ref, load_ref):
    returned = jnp.concatenate(
        [jnp.concatenate([ref[72 + a * 8 : 80 + a * 8, :].astype(F32) for ref in (high2_ref, low2_ref)], axis=0)
         for a in range(3)],
        axis=1,
    )
    back = jnp.dot(put_ref[...].astype(BF16), returned.astype(BF16), preferred_element_type=F32)
    for a in range(3):
        seen = back[:, a * 256 : a * 256 + 128] + back[:, a * 256 + 128 : a * 256 + 256]
        bubble_ref[a] = late_ref[a] + (C2 / relax_time) * seen
    push = late_push(high_ref, high2_ref, field_ref, come_ref, load_ref)
    for a in range(3):
        for z in range(4):
            base = (a * 4 + z) * 16
            total = base_ref[base : base + 16] + C2 * push[base : base + 16]
            if z == 3:
                total = total + C2 * above_term(field_ref, high2_ref[a * 16 : a * 16 + 16, :].astype(F32))
            out_ref[base : base + 16] = total


def shifted(x, by):
    length = lax.axis_size("pz")
    return lax.ppermute(x, "pz", [(i, (i + by) % length) for i in range(length)])


def exchange(x):
    return lax.all_to_all(x, "px", split_axis=0, concat_axis=0, tiled=True)


def on_device(velocity, first_deriv, second_deriv, bubble_vel, owner, dest):
    field = velocity.reshape(FIELD_ROWS, 256)
    block = ((FIELD_ROWS, 256), F32)
    rows = ((3, 24, 128), F32)
    hot = pltpu.VMEM((256, 1024), BF16)
    load = pltpu.VMEM((448, 1024), BF16)
    table = pltpu.VMEM((384, 256), BF16)
    ids = pltpu.VMEM((24, 128), jnp.int32)
    packed = ((32, 24, 128), BF16)

    velocity_in, bubbles_in, owner_in, dest_in = (
        pltpu.with_memory_space_constraint(x, pltpu.HBM) for x in (field, bubble_vel, owner, dest)
    )
    up, down, moved, field, bubble_vel, owner, dest = pl.pallas_call(
        first_send,
        in_specs=[pl.BlockSpec(memory_space=pltpu.HBM)] * 4,
        out_shape=(
            pltpu.VMEM((SEND_ROWS, 256), BF16),
            pltpu.VMEM((SEND_ROWS, 256), BF16),
            pltpu.VMEM((16, 256), F32),
            pltpu.VMEM((FIELD_ROWS, 256), F32),
            pltpu.VMEM((3, 24, 128), F32),
            pltpu.VMEM((2, 24, 128), jnp.int32),
            pltpu.VMEM((2, 24), jnp.int32),
        ),
        scratch_shapes=[pltpu.SemaphoreType.DMA((4,))],
    )(velocity_in, bubbles_in, owner_in, dest_in)
    low, high = shifted(up, 1), shifted(down, -1)
    part, seen, put, pick = call(
        home_first, (block, rows, ((24, 16), F32), ((16, 24), F32)), (table, ids, ids, hot, load, pltpu.VMEM((448, 256), F32))
    )(field, bubble_vel, owner, dest)
    spread_hot = ((256, 1024), BF16)
    part, afar, come_low = call(low_first, (block, ((3, 8, 128), F32), spread_hot), (hot, load))(
        field, part, low, moved
    )
    part, to_columns, rate, bubbles, slots, come_high = call(
        high_first, (block, packed, rows, rows, ((48, 256), F32), spread_hot), (hot, load)
    )(field, part, high, moved, afar, seen, bubble_vel, put, pick)
    columns = exchange(to_columns)
    (walls,) = call(columns_body, (packed,))(columns, first_deriv, second_deriv)
    walls = exchange(walls)
    lasts = ((LAST_ROWS, 256), BF16)
    middle, tend, up, down = call(middle_body, (block, block, lasts, lasts), (table,))(
        walls, field, part, low, high, slots, come_low, come_high
    )
    low2, high2 = shifted(up, 1), shifted(down, -1)
    base, late, put = call(
        home_second, (block, rows, ((24, 16), F32)), (table, ids, ids, hot, load, pltpu.VMEM((448, 256), F32))
    )(walls, middle, tend, bubbles, rate, owner, dest)
    (base,) = call(low_second, (block,), (load,))(base, middle, low, low2, come_low)
    field, bubbles = call(high_second, (block, rows), (load,))(
        base, middle, high, low2, high2, late, put, come_high
    )
    return (field.reshape(velocity.shape), bubbles)


def solution(mesh):
    return jax.shard_map(
        on_device,
        mesh=mesh,
        in_specs=(
            P(None, "pz", "px", None),
            P(),
            P(),
            P(None, ("px", "pz"), None),
            P(None, ("px", "pz"), None),
            P(None, ("px", "pz")),
        ),
        out_specs=(P(None, "pz", "px", None), P(None, ("px", "pz"), None)),
        check_vma=False,
    )
```

```python
import functools

import jax
import jax.numpy as jnp
from jax import lax
from jax.experimental import pallas as pl
from jax.experimental.pallas import tpu as pltpu
from jax.sharding import PartitionSpec as P

step_size = 0.5
viscosity = 0.4
relax_time = 0.5
coupling = 2.0
buoyancy = 0.5
forcing = 1.0
gammas = (8.0 / 15.0, 5.0 / 12.0)
zetas = (0.0, -17.0 / 60.0)

F32 = jnp.float32
BF16 = jnp.bfloat16
C1 = step_size * gammas[0]
C2 = step_size * gammas[1]
E2 = step_size * zetas[1]

ROWS_A = 64
FIELD_ROWS = 192
SEND_ROWS = 240
LAST_ROWS = 96


def iota(shape, dim):
    return lax.broadcasted_iota(jnp.int32, shape, dim)


def call(body, outs, scratch=()):
    return pl.pallas_call(
        body,
        out_shape=tuple(jax.ShapeDtypeStruct(s, d) for s, d in outs),
        scratch_shapes=list(scratch),
        compiler_params=pltpu.CompilerParams(vmem_limit_bytes=48 * 1024 * 1024),
    )


def hi_lo(x):
    hi = x.astype(BF16).astype(F32)
    return hi, x - hi


def pick_matrix(dest_row):
    up = jnp.where(dest_row == 1, 1.0, 0.0).astype(F32)
    down = jnp.where(dest_row == -1, 1.0, 0.0).astype(F32)
    slot = iota((16, 24), 0)
    marks = jnp.where(slot < 8, jnp.broadcast_to(up, (16, 24)), jnp.broadcast_to(down, (16, 24)))
    before = jnp.where(iota((24, 24), 0) < iota((24, 24), 1), 1.0, 0.0).astype(F32)
    rank = jnp.dot(marks.astype(BF16), before.astype(BF16), preferred_element_type=F32)
    wanted = jnp.where(slot < 8, slot, slot - 8).astype(F32)
    return jnp.where((rank == wanted) & (marks > 0.5), 1.0, 0.0).astype(F32)


def put_matrix(dest_row):
    r, c = iota((24, 24), 0), iota((24, 24), 1)
    wide = jnp.broadcast_to(dest_row, (24, 24))
    own = jnp.sum(jnp.where(r == c, wide, 0).astype(F32), axis=1, keepdims=True)
    rank_up = jnp.sum(jnp.where((c < r) & (wide == 1), 1.0, 0.0), axis=1, keepdims=True)
    rank_down = jnp.sum(jnp.where((c < r) & (wide == -1), 1.0, 0.0), axis=1, keepdims=True)
    slot = iota((24, 16), 1).astype(F32)
    hit_up = (own == 1.0) & (rank_up == slot)
    hit_down = (own == -1.0) & (rank_down + 8.0 == slot)
    return jnp.where(hit_up | hit_down, 1.0, 0.0).astype(F32)


def home_cells(cells, dest_row):
    r, c = iota((24, 24), 0), iota((24, 24), 1)
    wide = jnp.broadcast_to(dest_row, (24, 24))
    away = jnp.sum(jnp.where((r == c) & (wide != 0), 1.0, 0.0), axis=1, keepdims=True)
    row = jnp.where(away > 0.5, -1, cells >> 8)
    return row, cells & 255


def spread(line):
    return jnp.broadcast_to(line, (16, 128)).astype(BF16)


def row_numbers(count):
    at = iota((16, 128), 0)
    return [(at + 16 * q).astype(F32).astype(BF16) for q in range(count)]


def fill_columns(col, hot_ref):
    numbers = row_numbers(16)
    one, zero = jnp.ones((16, 128), BF16), jnp.zeros((16, 128), BF16)
    col = col.astype(F32)
    for k in range(8):
        here = spread(col[k : k + 1])
        for q in range(16):
            hot_ref[q * 16 : q * 16 + 16, k * 128 : (k + 1) * 128] = jnp.where(numbers[q] == here, one, zero)


def fill_values(row, highs, lows, load_ref):
    numbers = row_numbers(4)
    one, zero = jnp.ones((16, 128), BF16), jnp.zeros((16, 128), BF16)
    row = row.astype(F32)
    for k in range(8):
        here = spread(row[k : k + 1])
        masks = [numbers[q] == here for q in range(4)]
        values = [spread(x[k : k + 1]) for x in (*highs, *lows)] + [one]
        for part, value in enumerate(values[: load_ref.shape[0] // ROWS_A]):
            for q in range(4):
                at = part * ROWS_A + q * 16
                load_ref[at : at + 16, k * 128 : (k + 1) * 128] = jnp.where(masks[q], value, zero)


def scatter(load_ref, hot_ref):
    return lax.dot_general(
        load_ref[...], hot_ref[...], (((1,), (1,)), ((), ())), preferred_element_type=F32
    )


def gather(table, row, hot_ref):
    found = jnp.dot(table, hot_ref[...], preferred_element_type=F32)
    parts = found.shape[0] // FIELD_ROWS
    at = iota((ROWS_A, 128), 0)
    lines = [[], [], []]
    for k in range(8):
        mask = at == jnp.broadcast_to(row[k : k + 1], (ROWS_A, 128))
        for a in range(3):
            block = found[a * ROWS_A : (a + 1) * ROWS_A, k * 128 : (k + 1) * 128]
            for part in range(1, parts):
                base = part * FIELD_ROWS + a * ROWS_A
                block = block + found[base : base + ROWS_A, k * 128 : (k + 1) * 128]
            lines[a].append(jnp.sum(jnp.where(mask, block, 0.0), axis=0, keepdims=True))
    return [jnp.concatenate(line, axis=0) for line in lines]


def split_table(field, table_ref):
    hi, lo = hi_lo(field)
    table_ref[0:FIELD_ROWS] = hi.astype(BF16)
    table_ref[FIELD_ROWS : 2 * FIELD_ROWS] = lo.astype(BF16)


def push_of(sums, field):
    loads = sums[0:192] + sums[192:384]
    count = sums[384:448]
    return coupling * (loads - jnp.concatenate([count, count, count], axis=0) * field)


def plane(ref, a, z):
    base = (a * 4 + z) * 16
    return ref[base : base + 16, :].astype(F32)


def inner_tendency(f_ref, a, z):
    here = plane(f_ref, a, z)
    next_x = pltpu.roll(here, 255, 1)
    prev_x = pltpu.roll(here, 1, 1)
    across = next_x + prev_x - 4.0 * here
    slope_z = None
    if z < 3:
        next_z = plane(f_ref, a, z + 1)
        across = across + next_z
        slope_z = next_z
    if z > 0:
        prev_z = plane(f_ref, a, z - 1)
        across = across + prev_z
        slope_z = -prev_z if slope_z is None else slope_z - prev_z
    flow = plane(f_ref, 0, z) * (0.5 * (next_x - prev_x)) + plane(f_ref, 2, z) * (0.5 * slope_z)
    total = viscosity * across - flow
    return total + forcing if a == 0 else total


def below_term(f_ref, below):
    return (viscosity + 0.5 * plane(f_ref, 2, 0)) * below


def above_term(f_ref, above):
    return (viscosity - 0.5 * plane(f_ref, 2, 3)) * above


def lane_group(shape):
    return iota(shape, len(shape) - 1) // 32


def first_send(field_hbm, bubble_hbm, owner_hbm, dest_hbm, up_ref, down_ref, moved_ref,
               field_ref, bubble_ref, owner_ref, dest_ref, sems):
    pairs = ((dest_hbm, dest_ref), (owner_hbm, owner_ref), (bubble_hbm, bubble_ref), (field_hbm, field_ref))
    copies = [pltpu.make_async_copy(src, dst, sems.at[i]) for i, (src, dst) in enumerate(pairs)]
    for copy in copies:
        copy.start()
    for copy in copies[:3]:
        copy.wait()
    first, second = owner_ref[0], owner_ref[1]
    parts = []
    for a in range(3):
        parts += hi_lo(bubble_ref[a])
    parts += [((first >> 8) + 1).astype(F32), (first & 255).astype(F32)]
    parts = jnp.concatenate(parts, axis=1).astype(BF16)
    picked = jnp.dot(pick_matrix(dest_ref[0:1]).astype(BF16), parts, preferred_element_type=F32)
    later = jnp.concatenate([((second >> 8) + 1).astype(F32), (second & 255).astype(F32)], axis=1)
    later = jnp.dot(pick_matrix(dest_ref[1:2]).astype(BF16), later.astype(BF16), preferred_element_type=F32)
    moved_ref[...] = picked[:, 768:1024]
    for ref, at in ((up_ref, 0), (down_ref, 8)):
        lines = [picked[at : at + 8, i * 256 : (i + 1) * 256] for i in range(4)]
        lines += [later[at : at + 8], jnp.zeros((8, 256), F32)]
        ref[FIELD_ROWS:SEND_ROWS] = jnp.concatenate(lines, axis=0).astype(BF16)
    copies[3].wait()
    block = field_ref[...].astype(BF16)
    up_ref[0:FIELD_ROWS] = block
    down_ref[0:FIELD_ROWS] = block


def home_first(field_ref, bubble_ref, owner_ref, dest_ref, part_ref, seen_ref, put_ref, pick_ref,
               table_ref, hot_ref, load_ref):
    field = field_ref[...]
    split_table(field, table_ref)
    put_ref[...] = put_matrix(dest_ref[0:1])
    pick_ref[...] = pick_matrix(dest_ref[1:2])
    row, col = home_cells(owner_ref[0], dest_ref[0:1])
    sums = None
    for i in range(3):
        rows = slice(i * 8, i * 8 + 8)
        fill_columns(col[rows], hot_ref.at[i])
        pairs = [hi_lo(bubble_ref[a, rows]) for a in range(3)]
        fill_values(row[rows], [p[0] for p in pairs], [p[1] for p in pairs], load_ref.at[i])
        got = scatter(load_ref.at[i], hot_ref.at[i])
        sums = got if sums is None else sums + got
        seen = gather(table_ref[...], row[rows], hot_ref.at[i])
        for a in range(3):
            seen_ref[a, rows] = seen[a]
    push = push_of(sums, field)
    for a in range(3):
        for z in range(4):
            base = (a * 4 + z) * 16
            part_ref[base : base + 16] = inner_tendency(field_ref, a, z) + push[base : base + 16]


def tail_of(ref):
    return ref[FIELD_ROWS:SEND_ROWS, :].astype(F32)


def tail_cells(tail, line):
    at = tail[line * 8 : line * 8 + 8].astype(jnp.int32)
    return at[:, 0:128] - 1, at[:, 128:256]


def pack_pair(six, out_ref):
    group = lane_group((16, 128))
    group8 = lane_group((8, 128))
    for z in range(4):
        for half in range(2):
            tiles = [six[i][z][:, half * 128 : (half + 1) * 128] for i in range(6)]
            for o in range(4):
                def moved(x, target):
                    shift = ((target - o) % 4) * 32
                    return x if shift == 0 else pltpu.roll(x, shift, 1)
                main = moved(tiles[3], 3)
                for i in range(3):
                    main = jnp.where(group == i, moved(tiles[i], i), main)
                rest = moved(tiles[5][8:16], 3)
                rest = jnp.where(group8 == 2, moved(tiles[4][8:16], 2), rest)
                rest = jnp.where(group8 == 1, moved(tiles[5][0:8], 1), rest)
                rest = jnp.where(group8 == 0, moved(tiles[4][0:8], 0), rest)
                peer = z * 8 + half * 4 + o
                out_ref[peer] = jnp.concatenate([main, rest], axis=0).astype(BF16)


def unpack(ref, second, a, z):
    halves = []
    group = lane_group((16, 128))
    for half in range(2):
        total = None
        for o in range(4):
            chunk = ref[z * 8 + half * 4 + o].astype(F32)
            if not second:
                piece, at = chunk[0:16], a
            elif a == 0:
                piece, at = chunk[0:16], 3
            else:
                rest = chunk[16:24]
                piece, at = jnp.concatenate([rest, pltpu.roll(rest, 64, 1)], axis=0), a - 1
            shift = ((o - at) % 4) * 32
            piece = piece if shift == 0 else pltpu.roll(piece, shift, 1)
            total = piece if total is None else jnp.where(group == o, piece, total)
        halves.append(total)
    return jnp.concatenate(halves, axis=1)


def arrived(cells_ref, values_ref, first_line, cell_line, load_ref):
    row, col = tail_cells(tail_of(cells_ref), cell_line)
    tail = values_ref[first_line : first_line + 48, :].astype(F32)
    highs = [tail[a * 8 : a * 8 + 8, 0:128] for a in range(3)]
    lows = [tail[a * 8 : a * 8 + 8, 128:256] for a in range(3)]
    fill_values(row, highs, lows, load_ref)
    return col


def seen_afar(moved_ref, at, far_ref, hot_ref):
    cells = moved_ref[at : at + 8].astype(jnp.int32)
    fill_columns(cells[:, 128:256], hot_ref)
    return gather(far_ref[0:FIELD_ROWS], cells[:, 0:128] - 1, hot_ref)


def low_first(field_ref, part_ref, low_ref, moved_ref, out_ref, afar_ref, come_ref, hot_ref, far_ref, load_ref):
    fill_columns(tail_cells(tail_of(low_ref), 4)[1], come_ref)
    for a, line in enumerate(seen_afar(moved_ref, 8, low_ref, far_ref)):
        afar_ref[a] = line
    fill_columns(arrived(low_ref, low_ref, FIELD_ROWS, 3, load_ref), hot_ref)
    push = push_of(scatter(load_ref, hot_ref), field_ref[...])
    for a in range(3):
        for z in range(4):
            base = (a * 4 + z) * 16
            total = part_ref[base : base + 16] + push[base : base + 16]
            out_ref[base : base + 16] = total + below_term(field_ref, plane(low_ref, a, 3)) if z == 0 else total


def high_first(field_ref, part_ref, high_ref, moved_ref, afar_ref, seen_ref, bubble_ref, put_ref, pick_ref,
               tend_ref, send_ref, rate_ref, next_ref, slots_ref, come_ref, hot_ref, far_ref, load_ref):
    fill_columns(arrived(high_ref, high_ref, FIELD_ROWS, 3, load_ref), hot_ref)
    sums = scatter(load_ref, hot_ref)
    fill_columns(tail_cells(tail_of(high_ref), 4)[1], come_ref)
    near = seen_afar(moved_ref, 0, high_ref, far_ref)
    found = jnp.concatenate([jnp.concatenate([near[a], afar_ref[a]], axis=0) for a in range(3)], axis=1)
    back = jnp.dot(put_ref[...].astype(BF16), found.astype(BF16), preferred_element_type=F32)
    after = []
    for a in range(3):
        here = bubble_ref[a]
        rate = (seen_ref[a] + back[:, a * 128 : (a + 1) * 128] - here) / relax_time
        if a == 1:
            rate = rate + buoyancy
        rate_ref[a] = rate
        after.append(here + C1 * rate)
        next_ref[a] = after[a]
    parts = jnp.concatenate([piece for x in after for piece in hi_lo(x)], axis=1).astype(BF16)
    picked = jnp.dot(pick_ref[...].astype(BF16), parts, preferred_element_type=F32)
    for at in (0, 8):
        for a in range(3):
            line = at * 3 + a * 8
            slots_ref[line : line + 8] = picked[at : at + 8, a * 256 : (a + 1) * 256]
    push = push_of(sums, field_ref[...])
    six = [[None] * 4 for _ in range(6)]
    for a in range(3):
        for z in range(4):
            base = (a * 4 + z) * 16
            total = part_ref[base : base + 16] + push[base : base + 16]
            if z == 3:
                total = total + above_term(field_ref, plane(high_ref, a, 0))
            tend_ref[base : base + 16] = total
            here = field_ref[base : base + 16]
            six[a][z] = here
            six[3 + a][z] = (here - here.astype(BF16).astype(F32)) + C1 * total
    pack_pair(six, send_ref)


def columns_body(got_ref, first_ref, second_ref, send_ref):
    got = got_ref[...].astype(F32)
    main = got[:, 0:16].reshape(512, 128)
    rest = got[:, 16:24].reshape(256, 128)
    other = pltpu.roll(rest, 64, 1)
    rest = jnp.concatenate([rest.reshape(32, 8, 128), other.reshape(32, 8, 128)], axis=1).reshape(512, 128)
    group = lane_group((512, 128))
    gain = jnp.where(group == 0, pltpu.roll(main, 32, 1), pltpu.roll(rest, 32, 1))

    def wall(x):
        field = x.astype(BF16)
        wide = field.astype(F32)
        normal = jnp.where(group == 0, pltpu.roll(wide, 96, 1), jnp.where(group == 2, pltpu.roll(wide, 32, 1), wide))
        slopes = jnp.dot(first_ref[...], field, preferred_element_type=F32).astype(BF16).astype(F32)
        curves = jnp.dot(second_ref[...], field, preferred_element_type=F32).astype(BF16).astype(F32)
        return (viscosity * curves - normal * slopes).astype(BF16).astype(F32)

    wall_1 = wall(main)
    wall_2 = wall(main + (gain + C1 * wall_1))
    back = pltpu.roll(wall_2, 96, 1)
    ahead = pltpu.roll(wall_2, 32, 1)
    out = jnp.where(group == 3, back, wall_1).reshape(32, 16, 128)
    group8 = lane_group((32, 8, 128))
    tail = jnp.where(group8 < 2, back.reshape(32, 16, 128)[:, 0:8], ahead.reshape(32, 16, 128)[:, 8:16])
    send_ref[...] = jnp.concatenate([out, tail], axis=1).astype(BF16)


def middle_body(wall_ref, field_ref, part_ref, low_ref, high_ref, slots_ref, come_low_ref, come_high_ref,
                next_ref, tend_ref, up_ref, down_ref, table_ref):
    for a in range(3):
        for z in range(4):
            base = (a * 4 + z) * 16
            total = part_ref[base : base + 16] + unpack(wall_ref, False, a, z)
            tend_ref[base : base + 16] = total
            next_ref[base : base + 16] = field_ref[base : base + 16] + C1 * total
    split_table(next_ref[...], table_ref)
    ends = ((low_ref, come_low_ref, down_ref, 0, 24), (high_ref, come_high_ref, up_ref, 3, 0))
    for ref, come_ref, out_ref, z, at in ends:
        row, _ = tail_cells(tail_of(ref), 4)
        seen = gather(table_ref[...], row, come_ref)
        lines = [plane(next_ref, a, z) for a in range(3)]
        lines.append(slots_ref[at : at + 24])
        lines += [jnp.concatenate(hi_lo(seen[a]), axis=1) for a in range(3)]
        out_ref[...] = jnp.concatenate(lines, axis=0).astype(BF16)


def home_second(wall_ref, field_ref, tend_ref, bubble_ref, rate_ref, owner_ref, dest_ref,
                base_ref, late_ref, put_ref, table_ref, hot_ref, load_ref):
    field = field_ref[...]
    split_table(field, table_ref)
    put_ref[...] = put_matrix(dest_ref[1:2])
    row, col = home_cells(owner_ref[1], dest_ref[1:2])

    sums = None
    for i in range(3):
        rows = slice(i * 8, i * 8 + 8)
        hot, load = hot_ref.at[i], load_ref.at[i]
        fill_columns(col[rows], hot)
        pairs = [hi_lo(bubble_ref[a, rows]) for a in range(3)]
        fill_values(row[rows], [p[0] for p in pairs], [p[1] for p in pairs], load)
        got = scatter(load_ref.at[i], hot_ref.at[i])
        sums = got if sums is None else sums + got
        seen = gather(table_ref[...], row[rows], hot_ref.at[i])
        for a in range(3):
            here = bubble_ref[a, rows]
            rate = (seen[a] - here) / relax_time
            if a == 1:
                rate = rate + buoyancy
            late_ref[a, rows] = here + (C2 * rate + E2 * rate_ref[a, rows])
    push = push_of(sums, field)
    for a in range(3):
        for z in range(4):
            base = (a * 4 + z) * 16
            total = inner_tendency(field_ref, a, z) + push[base : base + 16] + unpack(wall_ref, True, a, z)
            earlier = tend_ref[base : base + 16]
            base_ref[base : base + 16] = field_ref[base : base + 16] + (C2 * total + E2 * earlier)


def late_push(cells_ref, values_ref, field_ref, come_ref, load_ref):
    arrived(cells_ref, values_ref, 48, 4, load_ref)
    return push_of(scatter(load_ref, come_ref), field_ref[...])


def low_second(base_ref, field_ref, low_ref, low2_ref, come_ref, out_ref, load_ref):
    push = late_push(low_ref, low2_ref, field_ref, come_ref, load_ref)
    for a in range(3):
        for z in range(4):
            base = (a * 4 + z) * 16
            total = base_ref[base : base + 16] + C2 * push[base : base + 16]
            if z == 0:
                total = total + C2 * below_term(field_ref, low2_ref[a * 16 : a * 16 + 16, :].astype(F32))
            out_ref[base : base + 16] = total


def high_second(base_ref, field_ref, high_ref, low2_ref, high2_ref, late_ref, put_ref, come_ref,
                out_ref, bubble_ref, load_ref):
    returned = jnp.concatenate(
        [jnp.concatenate([ref[72 + a * 8 : 80 + a * 8, :].astype(F32) for ref in (high2_ref, low2_ref)], axis=0)
         for a in range(3)],
        axis=1,
    )
    back = jnp.dot(put_ref[...].astype(BF16), returned.astype(BF16), preferred_element_type=F32)
    for a in range(3):
        seen = back[:, a * 256 : a * 256 + 128] + back[:, a * 256 + 128 : a * 256 + 256]
        bubble_ref[a] = late_ref[a] + (C2 / relax_time) * seen
    push = late_push(high_ref, high2_ref, field_ref, come_ref, load_ref)
    for a in range(3):
        for z in range(4):
            base = (a * 4 + z) * 16
            total = base_ref[base : base + 16] + C2 * push[base : base + 16]
            if z == 3:
                total = total + C2 * above_term(field_ref, high2_ref[a * 16 : a * 16 + 16, :].astype(F32))
            out_ref[base : base + 16] = total


def shifted(x, by):
    length = lax.axis_size("pz")
    return lax.ppermute(x, "pz", [(i, (i + by) % length) for i in range(length)])


def exchange(x):
    return lax.all_to_all(x, "px", split_axis=0, concat_axis=0, tiled=True)


def on_device(velocity, first_deriv, second_deriv, bubble_vel, owner, dest):
    field = velocity.reshape(FIELD_ROWS, 256)
    block = ((FIELD_ROWS, 256), F32)
    rows = ((3, 24, 128), F32)
    hot = pltpu.VMEM((256, 1024), BF16)
    load = pltpu.VMEM((448, 1024), BF16)
    table = pltpu.VMEM((384, 256), BF16)
    hots, loads = pltpu.VMEM((3, 256, 1024), BF16), pltpu.VMEM((3, 448, 1024), BF16)
    packed = ((32, 24, 128), BF16)

    velocity_in, bubbles_in, owner_in, dest_in = (
        pltpu.with_memory_space_constraint(x, pltpu.HBM) for x in (field, bubble_vel, owner, dest)
    )
    up, down, moved, field, bubble_vel, owner, dest = pl.pallas_call(
        first_send,
        in_specs=[pl.BlockSpec(memory_space=pltpu.HBM)] * 4,
        out_shape=(
            pltpu.VMEM((SEND_ROWS, 256), BF16),
            pltpu.VMEM((SEND_ROWS, 256), BF16),
            pltpu.VMEM((16, 256), F32),
            pltpu.VMEM((FIELD_ROWS, 256), F32),
            pltpu.VMEM((3, 24, 128), F32),
            pltpu.VMEM((2, 24, 128), jnp.int32),
            pltpu.VMEM((2, 24), jnp.int32),
        ),
        scratch_shapes=[pltpu.SemaphoreType.DMA((4,))],
    )(velocity_in, bubbles_in, owner_in, dest_in)
    low, high = shifted(up, 1), shifted(down, -1)
    part, seen, put, pick = call(
        home_first, (block, rows, ((24, 16), F32), ((16, 24), F32)), (table, hots, loads)
    )(field, bubble_vel, owner, dest)
    spread_hot = ((256, 1024), BF16)
    part, afar, come_low = call(low_first, (block, ((3, 8, 128), F32), spread_hot), (hot, hot, load))(
        field, part, low, moved
    )
    part, to_columns, rate, bubbles, slots, come_high = call(
        high_first, (block, packed, rows, rows, ((48, 256), F32), spread_hot), (hot, hot, load)
    )(field, part, high, moved, afar, seen, bubble_vel, put, pick)
    columns = exchange(to_columns)
    (walls,) = call(columns_body, (packed,))(columns, first_deriv, second_deriv)
    walls = exchange(walls)
    lasts = ((LAST_ROWS, 256), BF16)
    middle, tend, up, down = call(middle_body, (block, block, lasts, lasts), (table,))(
        walls, field, part, low, high, slots, come_low, come_high
    )
    low2, high2 = shifted(up, 1), shifted(down, -1)
    base, late, put = call(
        home_second, (block, rows, ((24, 16), F32)), (table, hots, loads)
    )(walls, middle, tend, bubbles, rate, owner, dest)
    (base,) = call(low_second, (block,), (load,))(base, middle, low, low2, come_low)
    field, bubbles = call(high_second, (block, rows), (load,))(
        base, middle, high, low2, high2, late, put, come_high
    )
    return (field.reshape(velocity.shape), bubbles)


def solution(mesh):
    return jax.shard_map(
        on_device,
        mesh=mesh,
        in_specs=(
            P(None, "pz", "px", None),
            P(),
            P(),
            P(None, ("px", "pz"), None),
            P(None, ("px", "pz"), None),
            P(None, ("px", "pz")),
        ),
        out_specs=(P(None, "pz", "px", None), P(None, ("px", "pz"), None)),
        check_vma=False,
    )
```

```python
import functools

import jax
import jax.numpy as jnp
from jax import lax
from jax.experimental import pallas as pl
from jax.experimental.pallas import tpu as pltpu
from jax.sharding import PartitionSpec as P

step_size = 0.5
viscosity = 0.4
relax_time = 0.5
coupling = 2.0
buoyancy = 0.5
forcing = 1.0
gammas = (8.0 / 15.0, 5.0 / 12.0)
zetas = (0.0, -17.0 / 60.0)

F32 = jnp.float32
BF16 = jnp.bfloat16
C1 = step_size * gammas[0]
C2 = step_size * gammas[1]
E2 = step_size * zetas[1]

ROWS_A = 64
FIELD_ROWS = 192
SEND_ROWS = 240
LAST_ROWS = 96


def iota(shape, dim):
    return lax.broadcasted_iota(jnp.int32, shape, dim)


def call(body, outs, scratch=()):
    return pl.pallas_call(
        body,
        out_shape=tuple(jax.ShapeDtypeStruct(s, d) for s, d in outs),
        scratch_shapes=list(scratch),
        compiler_params=pltpu.CompilerParams(vmem_limit_bytes=48 * 1024 * 1024),
    )


def hi_lo(x):
    hi = x.astype(BF16).astype(F32)
    return hi, x - hi


def pick_matrix(dest_row):
    up = jnp.where(dest_row == 1, 1.0, 0.0).astype(F32)
    down = jnp.where(dest_row == -1, 1.0, 0.0).astype(F32)
    slot = iota((16, 24), 0)
    marks = jnp.where(slot < 8, jnp.broadcast_to(up, (16, 24)), jnp.broadcast_to(down, (16, 24)))
    before = jnp.where(iota((24, 24), 0) < iota((24, 24), 1), 1.0, 0.0).astype(F32)
    rank = jnp.dot(marks.astype(BF16), before.astype(BF16), preferred_element_type=F32)
    wanted = jnp.where(slot < 8, slot, slot - 8).astype(F32)
    return jnp.where((rank == wanted) & (marks > 0.5), 1.0, 0.0).astype(F32)


def put_matrix(dest_row):
    r, c = iota((24, 24), 0), iota((24, 24), 1)
    wide = jnp.broadcast_to(dest_row, (24, 24))
    own = jnp.sum(jnp.where(r == c, wide, 0).astype(F32), axis=1, keepdims=True)
    rank_up = jnp.sum(jnp.where((c < r) & (wide == 1), 1.0, 0.0), axis=1, keepdims=True)
    rank_down = jnp.sum(jnp.where((c < r) & (wide == -1), 1.0, 0.0), axis=1, keepdims=True)
    slot = iota((24, 16), 1).astype(F32)
    hit_up = (own == 1.0) & (rank_up == slot)
    hit_down = (own == -1.0) & (rank_down + 8.0 == slot)
    return jnp.where(hit_up | hit_down, 1.0, 0.0).astype(F32)


def home_cells(cells, dest_row):
    r, c = iota((24, 24), 0), iota((24, 24), 1)
    wide = jnp.broadcast_to(dest_row, (24, 24))
    away = jnp.sum(jnp.where((r == c) & (wide != 0), 1.0, 0.0), axis=1, keepdims=True)
    row = jnp.where(away > 0.5, -1, cells >> 8)
    return row, cells & 255


def spread(line):
    return jnp.broadcast_to(line, (16, 128)).astype(BF16)


def row_numbers(count):
    at = iota((16, 128), 0)
    return [(at + 16 * q).astype(F32).astype(BF16) for q in range(count)]


def fill_columns(col, hot_ref):
    numbers = row_numbers(16)
    one, zero = jnp.ones((16, 128), BF16), jnp.zeros((16, 128), BF16)
    col = col.astype(F32)
    for k in range(8):
        here = spread(col[k : k + 1])
        for q in range(16):
            hot_ref[q * 16 : q * 16 + 16, k * 128 : (k + 1) * 128] = jnp.where(numbers[q] == here, one, zero)


def fill_values(row, highs, lows, load_ref):
    numbers = row_numbers(4)
    one, zero = jnp.ones((16, 128), BF16), jnp.zeros((16, 128), BF16)
    row = row.astype(F32)
    for k in range(8):
        here = spread(row[k : k + 1])
        masks = [numbers[q] == here for q in range(4)]
        values = [spread(x[k : k + 1]) for x in (*highs, *lows)] + [one]
        for part, value in enumerate(values[: load_ref.shape[0] // ROWS_A]):
            for q in range(4):
                at = part * ROWS_A + q * 16
                load_ref[at : at + 16, k * 128 : (k + 1) * 128] = jnp.where(masks[q], value, zero)


def scatter(load_ref, hot_ref):
    return lax.dot_general(
        load_ref[...], hot_ref[...], (((1,), (1,)), ((), ())), preferred_element_type=F32
    )


def gather(table, row, hot_ref):
    found = jnp.dot(table, hot_ref[...], preferred_element_type=F32)
    parts = found.shape[0] // FIELD_ROWS
    at = iota((ROWS_A, 128), 0)
    lines = [[], [], []]
    for k in range(8):
        mask = at == jnp.broadcast_to(row[k : k + 1], (ROWS_A, 128))
        for a in range(3):
            block = found[a * ROWS_A : (a + 1) * ROWS_A, k * 128 : (k + 1) * 128]
            for part in range(1, parts):
                base = part * FIELD_ROWS + a * ROWS_A
                block = block + found[base : base + ROWS_A, k * 128 : (k + 1) * 128]
            lines[a].append(jnp.sum(jnp.where(mask, block, 0.0), axis=0, keepdims=True))
    return [jnp.concatenate(line, axis=0) for line in lines]


def split_table(field, table_ref):
    hi, lo = hi_lo(field)
    table_ref[0:FIELD_ROWS] = hi.astype(BF16)
    table_ref[FIELD_ROWS : 2 * FIELD_ROWS] = lo.astype(BF16)


def push_of(sums, field):
    loads = sums[0:192] + sums[192:384]
    count = sums[384:448]
    return coupling * (loads - jnp.concatenate([count, count, count], axis=0) * field)


def plane(ref, a, z):
    base = (a * 4 + z) * 16
    return ref[base : base + 16, :].astype(F32)


def inner_tendency(f_ref, a, z):
    here = plane(f_ref, a, z)
    next_x = pltpu.roll(here, 255, 1)
    prev_x = pltpu.roll(here, 1, 1)
    across = next_x + prev_x - 4.0 * here
    slope_z = None
    if z < 3:
        next_z = plane(f_ref, a, z + 1)
        across = across + next_z
        slope_z = next_z
    if z > 0:
        prev_z = plane(f_ref, a, z - 1)
        across = across + prev_z
        slope_z = -prev_z if slope_z is None else slope_z - prev_z
    flow = plane(f_ref, 0, z) * (0.5 * (next_x - prev_x)) + plane(f_ref, 2, z) * (0.5 * slope_z)
    total = viscosity * across - flow
    return total + forcing if a == 0 else total


def below_term(f_ref, below):
    return (viscosity + 0.5 * plane(f_ref, 2, 0)) * below


def above_term(f_ref, above):
    return (viscosity - 0.5 * plane(f_ref, 2, 3)) * above


def lane_group(shape):
    return iota(shape, len(shape) - 1) // 32


def first_send(field_hbm, bubble_hbm, owner_hbm, dest_hbm, up_ref, down_ref, moved_ref,
               field_ref, bubble_ref, owner_ref, dest_ref, sems):
    pairs = ((dest_hbm, dest_ref), (owner_hbm, owner_ref), (bubble_hbm, bubble_ref), (field_hbm, field_ref))
    copies = [pltpu.make_async_copy(src, dst, sems.at[i]) for i, (src, dst) in enumerate(pairs)]
    for copy in copies:
        copy.start()
    for copy in copies[:3]:
        copy.wait()
    first, second = owner_ref[0], owner_ref[1]
    parts = []
    for a in range(3):
        parts += hi_lo(bubble_ref[a])
    parts += [((first >> 8) + 1).astype(F32), (first & 255).astype(F32)]
    parts = jnp.concatenate(parts, axis=1).astype(BF16)
    picked = jnp.dot(pick_matrix(dest_ref[0:1]).astype(BF16), parts, preferred_element_type=F32)
    later = jnp.concatenate([((second >> 8) + 1).astype(F32), (second & 255).astype(F32)], axis=1)
    later = jnp.dot(pick_matrix(dest_ref[1:2]).astype(BF16), later.astype(BF16), preferred_element_type=F32)
    moved_ref[...] = picked[:, 768:1024]
    for ref, at in ((up_ref, 0), (down_ref, 8)):
        lines = [picked[at : at + 8, i * 256 : (i + 1) * 256] for i in range(4)]
        lines += [later[at : at + 8], jnp.zeros((8, 256), F32)]
        ref[FIELD_ROWS:SEND_ROWS] = jnp.concatenate(lines, axis=0).astype(BF16)
    copies[3].wait()
    block = field_ref[...].astype(BF16)
    up_ref[0:FIELD_ROWS] = block
    down_ref[0:FIELD_ROWS] = block


def home_first(field_ref, bubble_ref, owner_ref, dest_ref, part_ref, seen_ref, put_ref, pick_ref,
               table_ref, hot_ref, load_ref):
    field = field_ref[...]
    split_table(field, table_ref)
    put_ref[...] = put_matrix(dest_ref[0:1])
    pick_ref[...] = pick_matrix(dest_ref[1:2])
    row, col = home_cells(owner_ref[0], dest_ref[0:1])
    sums = None
    for i in range(3):
        rows = slice(i * 8, i * 8 + 8)
        fill_columns(col[rows], hot_ref.at[i])
        pairs = [hi_lo(bubble_ref[a, rows]) for a in range(3)]
        fill_values(row[rows], [p[0] for p in pairs], [p[1] for p in pairs], load_ref.at[i])
        got = scatter(load_ref.at[i], hot_ref.at[i])
        sums = got if sums is None else sums + got
        seen = gather(table_ref[...], row[rows], hot_ref.at[i])
        for a in range(3):
            seen_ref[a, rows] = seen[a]
    push = push_of(sums, field)
    for a in range(3):
        for z in range(4):
            base = (a * 4 + z) * 16
            part_ref[base : base + 16] = inner_tendency(field_ref, a, z) + push[base : base + 16]


def tail_of(ref):
    return ref[FIELD_ROWS:SEND_ROWS, :].astype(F32)


def tail_cells(tail, line):
    at = tail[line * 8 : line * 8 + 8].astype(jnp.int32)
    return at[:, 0:128] - 1, at[:, 128:256]


def pack_pair(six, out_ref):
    group = lane_group((16, 128))
    group8 = lane_group((8, 128))
    for z in range(4):
        for half in range(2):
            tiles = [six[i][z][:, half * 128 : (half + 1) * 128] for i in range(6)]
            for o in range(4):
                def moved(x, target):
                    shift = ((target - o) % 4) * 32
                    return x if shift == 0 else pltpu.roll(x, shift, 1)
                main = moved(tiles[3], 3)
                for i in range(3):
                    main = jnp.where(group == i, moved(tiles[i], i), main)
                rest = moved(tiles[5][8:16], 3)
                rest = jnp.where(group8 == 2, moved(tiles[4][8:16], 2), rest)
                rest = jnp.where(group8 == 1, moved(tiles[5][0:8], 1), rest)
                rest = jnp.where(group8 == 0, moved(tiles[4][0:8], 0), rest)
                peer = z * 8 + half * 4 + o
                out_ref[peer] = jnp.concatenate([main, rest], axis=0).astype(BF16)


def unpack(ref, second, a, z):
    halves = []
    group = lane_group((16, 128))
    for half in range(2):
        total = None
        for o in range(4):
            chunk = ref[z * 8 + half * 4 + o].astype(F32)
            if not second:
                piece, at = chunk[0:16], a
            elif a == 0:
                piece, at = chunk[0:16], 3
            else:
                rest = chunk[16:24]
                piece, at = jnp.concatenate([rest, pltpu.roll(rest, 64, 1)], axis=0), a - 1
            shift = ((o - at) % 4) * 32
            piece = piece if shift == 0 else pltpu.roll(piece, shift, 1)
            total = piece if total is None else jnp.where(group == o, piece, total)
        halves.append(total)
    return jnp.concatenate(halves, axis=1)


def arrived(cells_ref, values_ref, first_line, cell_line, load_ref):
    row, col = tail_cells(tail_of(cells_ref), cell_line)
    tail = values_ref[first_line : first_line + 48, :].astype(F32)
    highs = [tail[a * 8 : a * 8 + 8, 0:128] for a in range(3)]
    lows = [tail[a * 8 : a * 8 + 8, 128:256] for a in range(3)]
    fill_values(row, highs, lows, load_ref)
    return col


def seen_afar(moved_ref, at, far_ref, hot_ref):
    cells = moved_ref[at : at + 8].astype(jnp.int32)
    fill_columns(cells[:, 128:256], hot_ref)
    return gather(far_ref[0:FIELD_ROWS], cells[:, 0:128] - 1, hot_ref)


def low_first(field_ref, part_ref, low_ref, moved_ref, out_ref, afar_ref, come_ref, hot_ref, far_ref, load_ref):
    fill_columns(tail_cells(tail_of(low_ref), 4)[1], come_ref)
    for a, line in enumerate(seen_afar(moved_ref, 8, low_ref, far_ref)):
        afar_ref[a] = line
    fill_columns(arrived(low_ref, low_ref, FIELD_ROWS, 3, load_ref), hot_ref)
    push = push_of(scatter(load_ref, hot_ref), field_ref[...])
    for a in range(3):
        for z in range(4):
            base = (a * 4 + z) * 16
            total = part_ref[base : base + 16] + push[base : base + 16]
            out_ref[base : base + 16] = total + below_term(field_ref, plane(low_ref, a, 3)) if z == 0 else total


def high_first(field_ref, part_ref, high_ref, moved_ref, afar_ref, seen_ref, bubble_ref, put_ref, pick_ref,
               tend_ref, send_ref, rate_ref, next_ref, slots_ref, come_ref, hot_ref, far_ref, load_ref):
    fill_columns(arrived(high_ref, high_ref, FIELD_ROWS, 3, load_ref), hot_ref)
    sums = scatter(load_ref, hot_ref)
    fill_columns(tail_cells(tail_of(high_ref), 4)[1], come_ref)
    near = seen_afar(moved_ref, 0, high_ref, far_ref)
    found = jnp.concatenate([jnp.concatenate([near[a], afar_ref[a]], axis=0) for a in range(3)], axis=1)
    back = jnp.dot(put_ref[...].astype(BF16), found.astype(BF16), preferred_element_type=F32)
    after = []
    for a in range(3):
        here = bubble_ref[a]
        rate = (seen_ref[a] + back[:, a * 128 : (a + 1) * 128] - here) / relax_time
        if a == 1:
            rate = rate + buoyancy
        rate_ref[a] = rate
        after.append(here + C1 * rate)
        next_ref[a] = after[a]
    parts = jnp.concatenate([piece for x in after for piece in hi_lo(x)], axis=1).astype(BF16)
    picked = jnp.dot(pick_ref[...].astype(BF16), parts, preferred_element_type=F32)
    for at in (0, 8):
        for a in range(3):
            line = at * 3 + a * 8
            slots_ref[line : line + 8] = picked[at : at + 8, a * 256 : (a + 1) * 256]
    push = push_of(sums, field_ref[...])
    six = [[None] * 4 for _ in range(6)]
    for a in range(3):
        for z in range(4):
            base = (a * 4 + z) * 16
            total = part_ref[base : base + 16] + push[base : base + 16]
            if z == 3:
                total = total + above_term(field_ref, plane(high_ref, a, 0))
            tend_ref[base : base + 16] = total
            here = field_ref[base : base + 16]
            six[a][z] = here
            six[3 + a][z] = (here - here.astype(BF16).astype(F32)) + C1 * total
    pack_pair(six, send_ref)


def columns_body(got_ref, first_ref, second_ref, send_ref):
    got = got_ref[...].astype(F32)
    main = got[:, 0:16].reshape(512, 128)
    rest = got[:, 16:24].reshape(256, 128)
    other = pltpu.roll(rest, 64, 1)
    rest = jnp.concatenate([rest.reshape(32, 8, 128), other.reshape(32, 8, 128)], axis=1).reshape(512, 128)
    group = lane_group((512, 128))
    gain = jnp.where(group == 0, pltpu.roll(main, 32, 1), pltpu.roll(rest, 32, 1))

    def wall(x):
        field = x.astype(BF16)
        wide = field.astype(F32)
        normal = jnp.where(group == 0, pltpu.roll(wide, 96, 1), jnp.where(group == 2, pltpu.roll(wide, 32, 1), wide))
        slopes = jnp.dot(first_ref[...], field, preferred_element_type=F32).astype(BF16).astype(F32)
        curves = jnp.dot(second_ref[...], field, preferred_element_type=F32).astype(BF16).astype(F32)
        return (viscosity * curves - normal * slopes).astype(BF16).astype(F32)

    wall_1 = wall(main)
    wall_2 = wall(main + (gain + C1 * wall_1))
    back = pltpu.roll(wall_2, 96, 1)
    ahead = pltpu.roll(wall_2, 32, 1)
    out = jnp.where(group == 3, back, wall_1).reshape(32, 16, 128)
    group8 = lane_group((32, 8, 128))
    tail = jnp.where(group8 < 2, back.reshape(32, 16, 128)[:, 0:8], ahead.reshape(32, 16, 128)[:, 8:16])
    send_ref[...] = jnp.concatenate([out, tail], axis=1).astype(BF16)


def middle_body(wall_ref, field_ref, part_ref, low_ref, high_ref, slots_ref, come_low_ref, come_high_ref,
                next_ref, tend_ref, first_ref, second_ref, table_ref):
    for a in range(3):
        for z in range(4):
            base = (a * 4 + z) * 16
            total = part_ref[base : base + 16] + unpack(wall_ref, False, a, z)
            tend_ref[base : base + 16] = total
            next_ref[base : base + 16] = field_ref[base : base + 16] + C1 * total
    table_ref[...] = next_ref[...].astype(BF16)
    sends = []
    for ref, come_ref, z, at in ((low_ref, come_low_ref, 0, 24), (high_ref, come_high_ref, 3, 0)):
        row, _ = tail_cells(tail_of(ref), 4)
        seen = gather(table_ref[...], row, come_ref)
        lines = [plane(next_ref, a, z) for a in range(3)]
        lines.append(slots_ref[at : at + 24])
        lines += [jnp.concatenate(seen[0:2], axis=1), jnp.concatenate([seen[2], jnp.zeros((8, 128), F32)], axis=1)]
        lines.append(jnp.zeros((8, 256), F32))
        sends.append(jnp.concatenate(lines, axis=0).astype(BF16))
    odd = parity()

    @pl.when(odd == 0)
    def _():
        first_ref[...], second_ref[...] = sends[0], sends[1]

    @pl.when(odd == 1)
    def _():
        first_ref[...], second_ref[...] = sends[1], sends[0]


def home_second(wall_ref, field_ref, tend_ref, bubble_ref, rate_ref, owner_ref, dest_ref,
                base_ref, late_ref, put_ref, table_ref, hot_ref, load_ref):
    field = field_ref[...]
    split_table(field, table_ref)
    put_ref[...] = put_matrix(dest_ref[1:2])
    row, col = home_cells(owner_ref[1], dest_ref[1:2])

    sums = None
    for i in range(3):
        rows = slice(i * 8, i * 8 + 8)
        hot, load = hot_ref.at[i], load_ref.at[i]
        fill_columns(col[rows], hot)
        pairs = [hi_lo(bubble_ref[a, rows]) for a in range(3)]
        fill_values(row[rows], [p[0] for p in pairs], [p[1] for p in pairs], load)
        got = scatter(load_ref.at[i], hot_ref.at[i])
        sums = got if sums is None else sums + got
        seen = gather(table_ref[...], row[rows], hot_ref.at[i])
        for a in range(3):
            here = bubble_ref[a, rows]
            rate = (seen[a] - here) / relax_time
            if a == 1:
                rate = rate + buoyancy
            late_ref[a, rows] = here + (C2 * rate + E2 * rate_ref[a, rows])
    push = push_of(sums, field)
    for a in range(3):
        for z in range(4):
            base = (a * 4 + z) * 16
            total = inner_tendency(field_ref, a, z) + push[base : base + 16] + unpack(wall_ref, True, a, z)
            earlier = tend_ref[base : base + 16]
            base_ref[base : base + 16] = field_ref[base : base + 16] + (C2 * total + E2 * earlier)


def late_push(cells_ref, values_ref, field_ref, come_ref, load_ref):
    arrived(cells_ref, values_ref, 48, 4, load_ref)
    return push_of(scatter(load_ref, come_ref), field_ref[...])


def late_side(below, base_ref, field_ref, cells_ref, come_ref, got_ref, out_ref, load_ref):
    push = late_push(cells_ref, got_ref, field_ref, come_ref, load_ref)
    for a in range(3):
        for z in range(4):
            base = (a * 4 + z) * 16
            total = push[base : base + 16]
            if z == (0 if below else 3):
                term = below_term if below else above_term
                total = total + term(field_ref, got_ref[a * 16 : a * 16 + 16, :].astype(F32))
            out_ref[base : base + 16] = base_ref[base : base + 16] + C2 * total


def first_late(base_ref, field_ref, low_ref, high_ref, come_low_ref, come_high_ref, first_ref, out_ref, load_ref):
    odd = parity()

    @pl.when(odd == 0)
    def _():
        late_side(True, base_ref, field_ref, low_ref, come_low_ref, first_ref, out_ref, load_ref)

    @pl.when(odd == 1)
    def _():
        late_side(False, base_ref, field_ref, high_ref, come_high_ref, first_ref, out_ref, load_ref)


def second_late(base_ref, field_ref, low_ref, high_ref, come_low_ref, come_high_ref, first_ref, second_ref,
                late_ref, put_ref, out_ref, bubble_ref, load_ref):
    odd = parity()

    def bubbles(high2_ref, low2_ref):
        returned = jnp.concatenate(
            [jnp.concatenate([ref[at : at + 8, :].astype(F32) for ref in (high2_ref, low2_ref)], axis=0) for at in (72, 80)],
            axis=1,
        )
        back = jnp.dot(put_ref[...].astype(BF16), returned.astype(BF16), preferred_element_type=F32)
        for a in range(3):
            bubble_ref[a] = late_ref[a] + (C2 / relax_time) * back[:, a * 128 : (a + 1) * 128]

    @pl.when(odd == 0)
    def _():
        bubbles(second_ref, first_ref)
        late_side(False, base_ref, field_ref, high_ref, come_high_ref, second_ref, out_ref, load_ref)

    @pl.when(odd == 1)
    def _():
        bubbles(first_ref, second_ref)
        late_side(True, base_ref, field_ref, low_ref, come_low_ref, second_ref, out_ref, load_ref)


def parity():
    return lax.axis_index("pz") % 2


def swapped(x, first):
    length = lax.axis_size("pz")
    step = [(1 if (i % 2 == 1) == first else -1) for i in range(length)]
    return lax.ppermute(x, "pz", [(i, (i + step[i]) % length) for i in range(length)])


def shifted(x, by):
    length = lax.axis_size("pz")
    return lax.ppermute(x, "pz", [(i, (i + by) % length) for i in range(length)])


def exchange(x):
    return lax.all_to_all(x, "px", split_axis=0, concat_axis=0, tiled=True)


def on_device(velocity, first_deriv, second_deriv, bubble_vel, owner, dest):
    field = velocity.reshape(FIELD_ROWS, 256)
    block = ((FIELD_ROWS, 256), F32)
    rows = ((3, 24, 128), F32)
    hot = pltpu.VMEM((256, 1024), BF16)
    load = pltpu.VMEM((448, 1024), BF16)
    table = pltpu.VMEM((384, 256), BF16)
    hots, loads = pltpu.VMEM((3, 256, 1024), BF16), pltpu.VMEM((3, 448, 1024), BF16)
    packed = ((32, 24, 128), BF16)

    velocity_in, bubbles_in, owner_in, dest_in = (
        pltpu.with_memory_space_constraint(x, pltpu.HBM) for x in (field, bubble_vel, owner, dest)
    )
    up, down, moved, field, bubble_vel, owner, dest = pl.pallas_call(
        first_send,
        in_specs=[pl.BlockSpec(memory_space=pltpu.HBM)] * 4,
        out_shape=(
            pltpu.VMEM((SEND_ROWS, 256), BF16),
            pltpu.VMEM((SEND_ROWS, 256), BF16),
            pltpu.VMEM((16, 256), F32),
            pltpu.VMEM((FIELD_ROWS, 256), F32),
            pltpu.VMEM((3, 24, 128), F32),
            pltpu.VMEM((2, 24, 128), jnp.int32),
            pltpu.VMEM((2, 24), jnp.int32),
        ),
        scratch_shapes=[pltpu.SemaphoreType.DMA((4,))],
    )(velocity_in, bubbles_in, owner_in, dest_in)
    low, high = shifted(up, 1), shifted(down, -1)
    part, seen, put, pick = call(
        home_first, (block, rows, ((24, 16), F32), ((16, 24), F32)), (table, hots, loads)
    )(field, bubble_vel, owner, dest)
    spread_hot = ((256, 1024), BF16)
    part, afar, come_low = call(low_first, (block, ((3, 8, 128), F32), spread_hot), (hot, hot, load))(
        field, part, low, moved
    )
    part, to_columns, rate, bubbles, slots, come_high = call(
        high_first, (block, packed, rows, rows, ((48, 256), F32), spread_hot), (hot, hot, load)
    )(field, part, high, moved, afar, seen, bubble_vel, put, pick)
    columns = exchange(to_columns)
    (walls,) = call(columns_body, (packed,))(columns, first_deriv, second_deriv)
    walls = exchange(walls)
    lasts = ((LAST_ROWS, 256), BF16)
    middle, tend, first, second = call(
        middle_body, (block, block, lasts, lasts), (pltpu.VMEM((FIELD_ROWS, 256), BF16),)
    )(walls, field, part, low, high, slots, come_low, come_high)
    first, second = swapped(first, True), swapped(second, False)
    base, late, put = call(home_second, (block, rows, ((24, 16), F32)), (table, hots, loads))(
        walls, middle, tend, bubbles, rate, owner, dest
    )
    (base,) = call(first_late, (block,), (load,))(base, middle, low, high, come_low, come_high, first)
    field, bubbles = call(second_late, (block, rows), (load,))(
        base, middle, low, high, come_low, come_high, first, second, late, put
    )
    return (field.reshape(velocity.shape), bubbles)


def solution(mesh):
    return jax.shard_map(
        on_device,
        mesh=mesh,
        in_specs=(
            P(None, "pz", "px", None),
            P(),
            P(),
            P(None, ("px", "pz"), None),
            P(None, ("px", "pz"), None),
            P(None, ("px", "pz")),
        ),
        out_specs=(P(None, "pz", "px", None), P(None, ("px", "pz"), None)),
        check_vma=False,
    )
```

```python
import functools

import jax
import jax.numpy as jnp
from jax import lax
from jax.experimental import pallas as pl
from jax.experimental.pallas import tpu as pltpu
from jax.sharding import PartitionSpec as P

step_size = 0.5
viscosity = 0.4
relax_time = 0.5
coupling = 2.0
buoyancy = 0.5
forcing = 1.0
gammas = (8.0 / 15.0, 5.0 / 12.0)
zetas = (0.0, -17.0 / 60.0)

F32 = jnp.float32
BF16 = jnp.bfloat16
C1 = step_size * gammas[0]
C2 = step_size * gammas[1]
E2 = step_size * zetas[1]

ROWS_A = 64
FIELD_ROWS = 192
SEND_ROWS = 240
LAST_ROWS = 96


def iota(shape, dim):
    return lax.broadcasted_iota(jnp.int32, shape, dim)


def call(body, outs, scratch=()):
    return pl.pallas_call(
        body,
        out_shape=tuple(jax.ShapeDtypeStruct(s, d) for s, d in outs),
        scratch_shapes=list(scratch),
        compiler_params=pltpu.CompilerParams(vmem_limit_bytes=48 * 1024 * 1024),
    )


def hi_lo(x):
    hi = x.astype(BF16).astype(F32)
    return hi, x - hi


def pick_matrix(dest_row):
    up = jnp.where(dest_row == 1, 1.0, 0.0).astype(F32)
    down = jnp.where(dest_row == -1, 1.0, 0.0).astype(F32)
    slot = iota((16, 24), 0)
    marks = jnp.where(slot < 8, jnp.broadcast_to(up, (16, 24)), jnp.broadcast_to(down, (16, 24)))
    before = jnp.where(iota((24, 24), 0) < iota((24, 24), 1), 1.0, 0.0).astype(F32)
    rank = jnp.dot(marks.astype(BF16), before.astype(BF16), preferred_element_type=F32)
    wanted = jnp.where(slot < 8, slot, slot - 8).astype(F32)
    return jnp.where((rank == wanted) & (marks > 0.5), 1.0, 0.0).astype(F32)


def put_matrix(dest_row):
    r, c = iota((24, 24), 0), iota((24, 24), 1)
    wide = jnp.broadcast_to(dest_row, (24, 24))
    own = jnp.sum(jnp.where(r == c, wide, 0).astype(F32), axis=1, keepdims=True)
    rank_up = jnp.sum(jnp.where((c < r) & (wide == 1), 1.0, 0.0), axis=1, keepdims=True)
    rank_down = jnp.sum(jnp.where((c < r) & (wide == -1), 1.0, 0.0), axis=1, keepdims=True)
    slot = iota((24, 16), 1).astype(F32)
    hit_up = (own == 1.0) & (rank_up == slot)
    hit_down = (own == -1.0) & (rank_down + 8.0 == slot)
    return jnp.where(hit_up | hit_down, 1.0, 0.0).astype(F32)


def home_cells(cells, dest_row):
    r, c = iota((24, 24), 0), iota((24, 24), 1)
    wide = jnp.broadcast_to(dest_row, (24, 24))
    away = jnp.sum(jnp.where((r == c) & (wide != 0), 1.0, 0.0), axis=1, keepdims=True)
    row = jnp.where(away > 0.5, -1, cells >> 8)
    return row, cells & 255


def spread(line):
    return jnp.broadcast_to(line, (16, 128)).astype(BF16)


def row_numbers(count):
    at = iota((16, 128), 0)
    return [(at + 16 * q).astype(F32).astype(BF16) for q in range(count)]


def fill_columns(col, hot_ref):
    numbers = row_numbers(16)
    one, zero = jnp.ones((16, 128), BF16), jnp.zeros((16, 128), BF16)
    col = col.astype(F32)
    for k in range(8):
        here = spread(col[k : k + 1])
        for q in range(16):
            hot_ref[q * 16 : q * 16 + 16, k * 128 : (k + 1) * 128] = jnp.where(numbers[q] == here, one, zero)


def fill_values(row, highs, lows, load_ref):
    numbers = row_numbers(4)
    one, zero = jnp.ones((16, 128), BF16), jnp.zeros((16, 128), BF16)
    row = row.astype(F32)
    for k in range(8):
        here = spread(row[k : k + 1])
        masks = [numbers[q] == here for q in range(4)]
        values = [spread(x[k : k + 1]) for x in (*highs, *lows)] + [one]
        for part, value in enumerate(values[: load_ref.shape[0] // ROWS_A]):
            for q in range(4):
                at = part * ROWS_A + q * 16
                load_ref[at : at + 16, k * 128 : (k + 1) * 128] = jnp.where(masks[q], value, zero)


def scatter(load_ref, hot_ref):
    return lax.dot_general(
        load_ref[...], hot_ref[...], (((1,), (1,)), ((), ())), preferred_element_type=F32
    )


def gather(table, row, hot_ref):
    found = jnp.dot(table, hot_ref[...], preferred_element_type=F32)
    parts = found.shape[0] // FIELD_ROWS
    at = iota((ROWS_A, 128), 0)
    lines = [[], [], []]
    for k in range(8):
        mask = at == jnp.broadcast_to(row[k : k + 1], (ROWS_A, 128))
        for a in range(3):
            block = found[a * ROWS_A : (a + 1) * ROWS_A, k * 128 : (k + 1) * 128]
            for part in range(1, parts):
                base = part * FIELD_ROWS + a * ROWS_A
                block = block + found[base : base + ROWS_A, k * 128 : (k + 1) * 128]
            lines[a].append(jnp.sum(jnp.where(mask, block, 0.0), axis=0, keepdims=True))
    return [jnp.concatenate(line, axis=0) for line in lines]


def split_table(field, table_ref):
    hi, lo = hi_lo(field)
    table_ref[0:FIELD_ROWS] = hi.astype(BF16)
    table_ref[FIELD_ROWS : 2 * FIELD_ROWS] = lo.astype(BF16)


def push_of(sums, field):
    loads = sums[0:192] + sums[192:384]
    count = sums[384:448]
    return coupling * (loads - jnp.concatenate([count, count, count], axis=0) * field)


def plane(ref, a, z):
    base = (a * 4 + z) * 16
    return ref[base : base + 16, :].astype(F32)


def inner_tendency(f_ref, a, z):
    here = plane(f_ref, a, z)
    next_x = pltpu.roll(here, 255, 1)
    prev_x = pltpu.roll(here, 1, 1)
    across = next_x + prev_x - 4.0 * here
    slope_z = None
    if z < 3:
        next_z = plane(f_ref, a, z + 1)
        across = across + next_z
        slope_z = next_z
    if z > 0:
        prev_z = plane(f_ref, a, z - 1)
        across = across + prev_z
        slope_z = -prev_z if slope_z is None else slope_z - prev_z
    flow = plane(f_ref, 0, z) * (0.5 * (next_x - prev_x)) + plane(f_ref, 2, z) * (0.5 * slope_z)
    total = viscosity * across - flow
    return total + forcing if a == 0 else total


def below_term(f_ref, below):
    return (viscosity + 0.5 * plane(f_ref, 2, 0)) * below


def above_term(f_ref, above):
    return (viscosity - 0.5 * plane(f_ref, 2, 3)) * above


def lane_group(shape):
    return iota(shape, len(shape) - 1) // 32


def first_send(field_hbm, bubble_hbm, owner_hbm, dest_hbm, up_ref, down_ref, moved_ref,
               field_ref, bubble_ref, owner_ref, dest_ref, sems):
    pairs = ((dest_hbm, dest_ref), (owner_hbm, owner_ref), (bubble_hbm, bubble_ref), (field_hbm, field_ref))
    copies = [pltpu.make_async_copy(src, dst, sems.at[i]) for i, (src, dst) in enumerate(pairs)]
    for copy in copies:
        copy.start()
    for copy in copies[:3]:
        copy.wait()
    first, second = owner_ref[0], owner_ref[1]
    parts = []
    for a in range(3):
        parts += hi_lo(bubble_ref[a])
    parts += [((first >> 8) + 1).astype(F32), (first & 255).astype(F32)]
    parts = jnp.concatenate(parts, axis=1).astype(BF16)
    picked = jnp.dot(pick_matrix(dest_ref[0:1]).astype(BF16), parts, preferred_element_type=F32)
    later = jnp.concatenate([((second >> 8) + 1).astype(F32), (second & 255).astype(F32)], axis=1)
    later = jnp.dot(pick_matrix(dest_ref[1:2]).astype(BF16), later.astype(BF16), preferred_element_type=F32)
    moved_ref[...] = picked[:, 768:1024]
    for ref, at in ((up_ref, 0), (down_ref, 8)):
        lines = [picked[at : at + 8, i * 256 : (i + 1) * 256] for i in range(4)]
        lines += [later[at : at + 8], jnp.zeros((8, 256), F32)]
        ref[FIELD_ROWS:SEND_ROWS] = jnp.concatenate(lines, axis=0).astype(BF16)
    copies[3].wait()
    block = field_ref[...].astype(BF16)
    up_ref[0:FIELD_ROWS] = block
    down_ref[0:FIELD_ROWS] = block


def home_first(field_ref, bubble_ref, owner_ref, dest_ref, part_ref, seen_ref, put_ref, pick_ref,
               table_ref, hot_ref, load_ref):
    field = field_ref[...]
    split_table(field, table_ref)
    put_ref[...] = put_matrix(dest_ref[0:1])
    pick_ref[...] = pick_matrix(dest_ref[1:2])
    row, col = home_cells(owner_ref[0], dest_ref[0:1])
    sums = None
    for i in range(3):
        rows = slice(i * 8, i * 8 + 8)
        fill_columns(col[rows], hot_ref.at[i])
        pairs = [hi_lo(bubble_ref[a, rows]) for a in range(3)]
        fill_values(row[rows], [p[0] for p in pairs], [p[1] for p in pairs], load_ref.at[i])
        got = scatter(load_ref.at[i], hot_ref.at[i])
        sums = got if sums is None else sums + got
        seen = gather(table_ref[...], row[rows], hot_ref.at[i])
        for a in range(3):
            seen_ref[a, rows] = seen[a]
    push = push_of(sums, field)
    for a in range(3):
        for z in range(4):
            base = (a * 4 + z) * 16
            part_ref[base : base + 16] = inner_tendency(field_ref, a, z) + push[base : base + 16]


def tail_of(ref):
    return ref[FIELD_ROWS:SEND_ROWS, :].astype(F32)


def tail_cells(tail, line):
    at = tail[line * 8 : line * 8 + 8].astype(jnp.int32)
    return at[:, 0:128] - 1, at[:, 128:256]


def pack_pair(six, out_ref):
    group = lane_group((16, 128))
    group8 = lane_group((8, 128))
    for z in range(4):
        for half in range(2):
            tiles = [six[i][z][:, half * 128 : (half + 1) * 128] for i in range(6)]
            for o in range(4):
                def moved(x, target):
                    shift = ((target - o) % 4) * 32
                    return x if shift == 0 else pltpu.roll(x, shift, 1)
                main = moved(tiles[3], 3)
                for i in range(3):
                    main = jnp.where(group == i, moved(tiles[i], i), main)
                rest = moved(tiles[5][8:16], 3)
                rest = jnp.where(group8 == 2, moved(tiles[4][8:16], 2), rest)
                rest = jnp.where(group8 == 1, moved(tiles[5][0:8], 1), rest)
                rest = jnp.where(group8 == 0, moved(tiles[4][0:8], 0), rest)
                peer = z * 8 + half * 4 + o
                out_ref[peer] = jnp.concatenate([main, rest], axis=0).astype(BF16)


def unpack(ref, second, a, z):
    halves = []
    group = lane_group((16, 128))
    for half in range(2):
        total = None
        for o in range(4):
            chunk = ref[z * 8 + half * 4 + o].astype(F32)
            if not second:
                piece, at = chunk[0:16], a
            elif a == 0:
                piece, at = chunk[0:16], 3
            else:
                rest = chunk[16:24]
                piece, at = jnp.concatenate([rest, pltpu.roll(rest, 64, 1)], axis=0), a - 1
            shift = ((o - at) % 4) * 32
            piece = piece if shift == 0 else pltpu.roll(piece, shift, 1)
            total = piece if total is None else jnp.where(group == o, piece, total)
        halves.append(total)
    return jnp.concatenate(halves, axis=1)


def arrived(cells_ref, values_ref, first_line, cell_line, load_ref):
    row, col = tail_cells(tail_of(cells_ref), cell_line)
    tail = values_ref[first_line : first_line + 48, :].astype(F32)
    highs = [tail[a * 8 : a * 8 + 8, 0:128] for a in range(3)]
    lows = [tail[a * 8 : a * 8 + 8, 128:256] for a in range(3)]
    fill_values(row, highs, lows, load_ref)
    return col


def seen_afar(moved_ref, at, far_ref, hot_ref):
    cells = moved_ref[at : at + 8].astype(jnp.int32)
    fill_columns(cells[:, 128:256], hot_ref)
    return gather(far_ref[0:FIELD_ROWS], cells[:, 0:128] - 1, hot_ref)


def low_first(field_ref, part_ref, low_ref, moved_ref, out_ref, afar_ref, come_ref, hot_ref, far_ref, load_ref):
    fill_columns(tail_cells(tail_of(low_ref), 4)[1], come_ref)
    for a, line in enumerate(seen_afar(moved_ref, 8, low_ref, far_ref)):
        afar_ref[a] = line
    fill_columns(arrived(low_ref, low_ref, FIELD_ROWS, 3, load_ref), hot_ref)
    push = push_of(scatter(load_ref, hot_ref), field_ref[...])
    for a in range(3):
        for z in range(4):
            base = (a * 4 + z) * 16
            total = part_ref[base : base + 16] + push[base : base + 16]
            out_ref[base : base + 16] = total + below_term(field_ref, plane(low_ref, a, 3)) if z == 0 else total


def high_first(field_ref, part_ref, high_ref, moved_ref, afar_ref, seen_ref, bubble_ref, put_ref, pick_ref,
               tend_ref, send_ref, rate_ref, next_ref, slots_ref, come_ref, hot_ref, far_ref, load_ref):
    fill_columns(arrived(high_ref, high_ref, FIELD_ROWS, 3, load_ref), hot_ref)
    sums = scatter(load_ref, hot_ref)
    fill_columns(tail_cells(tail_of(high_ref), 4)[1], come_ref)
    near = seen_afar(moved_ref, 0, high_ref, far_ref)
    found = jnp.concatenate([jnp.concatenate([near[a], afar_ref[a]], axis=0) for a in range(3)], axis=1)
    back = jnp.dot(put_ref[...].astype(BF16), found.astype(BF16), preferred_element_type=F32)
    after = []
    for a in range(3):
        here = bubble_ref[a]
        rate = (seen_ref[a] + back[:, a * 128 : (a + 1) * 128] - here) / relax_time
        if a == 1:
            rate = rate + buoyancy
        rate_ref[a] = rate
        after.append(here + C1 * rate)
        next_ref[a] = after[a]
    parts = jnp.concatenate([piece for x in after for piece in hi_lo(x)], axis=1).astype(BF16)
    picked = jnp.dot(pick_ref[...].astype(BF16), parts, preferred_element_type=F32)
    for at in (0, 8):
        for a in range(3):
            line = at * 3 + a * 8
            slots_ref[line : line + 8] = picked[at : at + 8, a * 256 : (a + 1) * 256]
    push = push_of(sums, field_ref[...])
    six = [[None] * 4 for _ in range(6)]
    for a in range(3):
        for z in range(4):
            base = (a * 4 + z) * 16
            total = part_ref[base : base + 16] + push[base : base + 16]
            if z == 3:
                total = total + above_term(field_ref, plane(high_ref, a, 0))
            tend_ref[base : base + 16] = total
            here = field_ref[base : base + 16]
            six[a][z] = here
            six[3 + a][z] = (here - here.astype(BF16).astype(F32)) + C1 * total
    pack_pair(six, send_ref)


def columns_body(got_ref, first_ref, second_ref, send_ref):
    got = got_ref[...].astype(F32)
    main = got[:, 0:16].reshape(512, 128)
    rest = got[:, 16:24].reshape(256, 128)
    other = pltpu.roll(rest, 64, 1)
    rest = jnp.concatenate([rest.reshape(32, 8, 128), other.reshape(32, 8, 128)], axis=1).reshape(512, 128)
    group = lane_group((512, 128))
    gain = jnp.where(group == 0, pltpu.roll(main, 32, 1), pltpu.roll(rest, 32, 1))

    def wall(x):
        field = x.astype(BF16)
        wide = field.astype(F32)
        normal = jnp.where(group == 0, pltpu.roll(wide, 96, 1), jnp.where(group == 2, pltpu.roll(wide, 32, 1), wide))
        slopes = jnp.dot(first_ref[...], field, preferred_element_type=F32).astype(BF16).astype(F32)
        curves = jnp.dot(second_ref[...], field, preferred_element_type=F32).astype(BF16).astype(F32)
        return (viscosity * curves - normal * slopes).astype(BF16).astype(F32)

    wall_1 = wall(main)
    wall_2 = wall(main + (gain + C1 * wall_1))
    back = pltpu.roll(wall_2, 96, 1)
    ahead = pltpu.roll(wall_2, 32, 1)
    out = jnp.where(group == 3, back, wall_1).reshape(32, 16, 128)
    group8 = lane_group((32, 8, 128))
    tail = jnp.where(group8 < 2, back.reshape(32, 16, 128)[:, 0:8], ahead.reshape(32, 16, 128)[:, 8:16])
    send_ref[...] = jnp.concatenate([out, tail], axis=1).astype(BF16)


def middle_body(wall_ref, field_ref, part_ref, low_ref, high_ref, slots_ref, come_low_ref, come_high_ref,
                next_ref, tend_ref, down_ref, up_ref, table_ref):
    for a in range(3):
        for z in range(4):
            base = (a * 4 + z) * 16
            total = part_ref[base : base + 16] + unpack(wall_ref, False, a, z)
            tend_ref[base : base + 16] = total
            next_ref[base : base + 16] = field_ref[base : base + 16] + C1 * total
    table_ref[...] = next_ref[...].astype(BF16)
    sends = []
    for ref, come_ref, z, at in ((low_ref, come_low_ref, 0, 24), (high_ref, come_high_ref, 3, 0)):
        row, _ = tail_cells(tail_of(ref), 4)
        seen = gather(table_ref[...], row, come_ref)
        lines = [plane(next_ref, a, z) for a in range(3)]
        lines.append(slots_ref[at : at + 24])
        lines += [jnp.concatenate(seen[0:2], axis=1), jnp.concatenate([seen[2], jnp.zeros((8, 128), F32)], axis=1)]
        lines.append(jnp.zeros((8, 256), F32))
        sends.append(jnp.concatenate(lines, axis=0).astype(BF16))
    down_ref[...], up_ref[...] = sends


def home_second(wall_ref, field_ref, tend_ref, bubble_ref, rate_ref, owner_ref, dest_ref,
                base_ref, late_ref, put_ref, table_ref, hot_ref, load_ref):
    field = field_ref[...]
    split_table(field, table_ref)
    put_ref[...] = put_matrix(dest_ref[1:2])
    row, col = home_cells(owner_ref[1], dest_ref[1:2])

    sums = None
    for i in range(3):
        rows = slice(i * 8, i * 8 + 8)
        hot, load = hot_ref.at[i], load_ref.at[i]
        fill_columns(col[rows], hot)
        pairs = [hi_lo(bubble_ref[a, rows]) for a in range(3)]
        fill_values(row[rows], [p[0] for p in pairs], [p[1] for p in pairs], load)
        got = scatter(load_ref.at[i], hot_ref.at[i])
        sums = got if sums is None else sums + got
        seen = gather(table_ref[...], row[rows], hot_ref.at[i])
        for a in range(3):
            here = bubble_ref[a, rows]
            rate = (seen[a] - here) / relax_time
            if a == 1:
                rate = rate + buoyancy
            late_ref[a, rows] = here + (C2 * rate + E2 * rate_ref[a, rows])
    push = push_of(sums, field)
    for a in range(3):
        for z in range(4):
            base = (a * 4 + z) * 16
            total = inner_tendency(field_ref, a, z) + push[base : base + 16] + unpack(wall_ref, True, a, z)
            earlier = tend_ref[base : base + 16]
            base_ref[base : base + 16] = field_ref[base : base + 16] + (C2 * total + E2 * earlier)


def late_push(cells_ref, values_ref, field_ref, come_ref, load_ref):
    arrived(cells_ref, values_ref, 48, 4, load_ref)
    return push_of(scatter(load_ref, come_ref), field_ref[...])


def late_side(below, base_ref, field_ref, cells_ref, come_ref, got_ref, out_ref, load_ref):
    push = late_push(cells_ref, got_ref, field_ref, come_ref, load_ref)
    for a in range(3):
        for z in range(4):
            base = (a * 4 + z) * 16
            total = push[base : base + 16]
            if z == (0 if below else 3):
                term = below_term if below else above_term
                total = total + term(field_ref, got_ref[a * 16 : a * 16 + 16, :].astype(F32))
            out_ref[base : base + 16] = base_ref[base : base + 16] + C2 * total


def high_second(base_ref, field_ref, high_ref, come_ref, high2_ref, out_ref, load_ref):
    late_side(False, base_ref, field_ref, high_ref, come_ref, high2_ref, out_ref, load_ref)


def low_second(base_ref, field_ref, low_ref, come_ref, high2_ref, low2_ref, late_ref, put_ref,
               out_ref, bubble_ref, load_ref):
    returned = jnp.concatenate(
        [jnp.concatenate([ref[at : at + 8, :].astype(F32) for ref in (high2_ref, low2_ref)], axis=0) for at in (72, 80)],
        axis=1,
    )
    back = jnp.dot(put_ref[...].astype(BF16), returned.astype(BF16), preferred_element_type=F32)
    for a in range(3):
        bubble_ref[a] = late_ref[a] + (C2 / relax_time) * back[:, a * 128 : (a + 1) * 128]
    late_side(True, base_ref, field_ref, low_ref, come_ref, low2_ref, out_ref, load_ref)


def shifted(x, by):
    length = lax.axis_size("pz")
    return lax.ppermute(x, "pz", [(i, (i + by) % length) for i in range(length)])


def exchange(x):
    return lax.all_to_all(x, "px", split_axis=0, concat_axis=0, tiled=True)


def on_device(velocity, first_deriv, second_deriv, bubble_vel, owner, dest):
    field = velocity.reshape(FIELD_ROWS, 256)
    block = ((FIELD_ROWS, 256), F32)
    rows = ((3, 24, 128), F32)
    hot = pltpu.VMEM((256, 1024), BF16)
    load = pltpu.VMEM((448, 1024), BF16)
    table = pltpu.VMEM((384, 256), BF16)
    hots, loads = pltpu.VMEM((3, 256, 1024), BF16), pltpu.VMEM((3, 448, 1024), BF16)
    packed = ((32, 24, 128), BF16)

    velocity_in, bubbles_in, owner_in, dest_in = (
        pltpu.with_memory_space_constraint(x, pltpu.HBM) for x in (field, bubble_vel, owner, dest)
    )
    up, down, moved, field, bubble_vel, owner, dest = pl.pallas_call(
        first_send,
        in_specs=[pl.BlockSpec(memory_space=pltpu.HBM)] * 4,
        out_shape=(
            pltpu.VMEM((SEND_ROWS, 256), BF16),
            pltpu.VMEM((SEND_ROWS, 256), BF16),
            pltpu.VMEM((16, 256), F32),
            pltpu.VMEM((FIELD_ROWS, 256), F32),
            pltpu.VMEM((3, 24, 128), F32),
            pltpu.VMEM((2, 24, 128), jnp.int32),
            pltpu.VMEM((2, 24), jnp.int32),
        ),
        scratch_shapes=[pltpu.SemaphoreType.DMA((4,))],
    )(velocity_in, bubbles_in, owner_in, dest_in)
    low, high = shifted(up, 1), shifted(down, -1)
    part, seen, put, pick = call(
        home_first, (block, rows, ((24, 16), F32), ((16, 24), F32)), (table, hots, loads)
    )(field, bubble_vel, owner, dest)
    spread_hot = ((256, 1024), BF16)
    part, afar, come_low = call(low_first, (block, ((3, 8, 128), F32), spread_hot), (hot, hot, load))(
        field, part, low, moved
    )
    part, to_columns, rate, bubbles, slots, come_high = call(
        high_first, (block, packed, rows, rows, ((48, 256), F32), spread_hot), (hot, hot, load)
    )(field, part, high, moved, afar, seen, bubble_vel, put, pick)
    columns = exchange(to_columns)
    (walls,) = call(columns_body, (packed,))(columns, first_deriv, second_deriv)
    walls = exchange(walls)
    lasts = ((LAST_ROWS, 256), BF16)
    middle, tend, down, up = call(
        middle_body, (block, block, lasts, lasts), (pltpu.VMEM((FIELD_ROWS, 256), BF16),)
    )(walls, field, part, low, high, slots, come_low, come_high)
    high2, low2 = shifted(down, -1), shifted(up, 1)
    base, late, put = call(home_second, (block, rows, ((24, 16), F32)), (table, hots, loads))(
        walls, middle, tend, bubbles, rate, owner, dest
    )
    (base,) = call(high_second, (block,), (load,))(base, middle, high, come_high, high2)
    field, bubbles = call(low_second, (block, rows), (load,))(
        base, middle, low, come_low, high2, low2, late, put
    )
    return (field.reshape(velocity.shape), bubbles)


def solution(mesh):
    return jax.shard_map(
        on_device,
        mesh=mesh,
        in_specs=(
            P(None, "pz", "px", None),
            P(),
            P(),
            P(None, ("px", "pz"), None),
            P(None, ("px", "pz"), None),
            P(None, ("px", "pz")),
        ),
        out_specs=(P(None, "pz", "px", None), P(None, ("px", "pz"), None)),
        check_vma=False,
    )
```

```python
import functools

import jax
import jax.numpy as jnp
from jax import lax
from jax.experimental import pallas as pl
from jax.experimental.pallas import tpu as pltpu
from jax.sharding import PartitionSpec as P

step_size = 0.5
viscosity = 0.4
relax_time = 0.5
coupling = 2.0
buoyancy = 0.5
forcing = 1.0
gammas = (8.0 / 15.0, 5.0 / 12.0)
zetas = (0.0, -17.0 / 60.0)

F32 = jnp.float32
BF16 = jnp.bfloat16
C1 = step_size * gammas[0]
C2 = step_size * gammas[1]
E2 = step_size * zetas[1]

ROWS_A = 64
FIELD_ROWS = 192
SEND_ROWS = 240
LAST_ROWS = 96


def iota(shape, dim):
    return lax.broadcasted_iota(jnp.int32, shape, dim)


def call(body, outs, scratch=()):
    return pl.pallas_call(
        body,
        out_shape=tuple(jax.ShapeDtypeStruct(s, d) for s, d in outs),
        scratch_shapes=list(scratch),
        compiler_params=pltpu.CompilerParams(vmem_limit_bytes=48 * 1024 * 1024),
    )


def hi_lo(x):
    hi = x.astype(BF16).astype(F32)
    return hi, x - hi


def pick_matrix(dest_row):
    up = jnp.where(dest_row == 1, 1.0, 0.0).astype(F32)
    down = jnp.where(dest_row == -1, 1.0, 0.0).astype(F32)
    slot = iota((16, 24), 0)
    marks = jnp.where(slot < 8, jnp.broadcast_to(up, (16, 24)), jnp.broadcast_to(down, (16, 24)))
    before = jnp.where(iota((24, 24), 0) < iota((24, 24), 1), 1.0, 0.0).astype(F32)
    rank = jnp.dot(marks.astype(BF16), before.astype(BF16), preferred_element_type=F32)
    wanted = jnp.where(slot < 8, slot, slot - 8).astype(F32)
    return jnp.where((rank == wanted) & (marks > 0.5), 1.0, 0.0).astype(F32)


def put_matrix(dest_row):
    r, c = iota((24, 24), 0), iota((24, 24), 1)
    wide = jnp.broadcast_to(dest_row, (24, 24))
    own = jnp.sum(jnp.where(r == c, wide, 0).astype(F32), axis=1, keepdims=True)
    rank_up = jnp.sum(jnp.where((c < r) & (wide == 1), 1.0, 0.0), axis=1, keepdims=True)
    rank_down = jnp.sum(jnp.where((c < r) & (wide == -1), 1.0, 0.0), axis=1, keepdims=True)
    slot = iota((24, 16), 1).astype(F32)
    hit_up = (own == 1.0) & (rank_up == slot)
    hit_down = (own == -1.0) & (rank_down + 8.0 == slot)
    return jnp.where(hit_up | hit_down, 1.0, 0.0).astype(F32)


def home_cells(cells, dest_row):
    r, c = iota((24, 24), 0), iota((24, 24), 1)
    wide = jnp.broadcast_to(dest_row, (24, 24))
    away = jnp.sum(jnp.where((r == c) & (wide != 0), 1.0, 0.0), axis=1, keepdims=True)
    row = jnp.where(away > 0.5, -1, cells >> 8)
    return row, cells & 255


def spread(line):
    return jnp.broadcast_to(line, (16, 128)).astype(BF16)


def row_numbers(count):
    at = iota((16, 128), 0)
    return [(at + 16 * q).astype(F32).astype(BF16) for q in range(count)]


def fill_columns(col, hot_ref):
    numbers = row_numbers(16)
    one, zero = jnp.ones((16, 128), BF16), jnp.zeros((16, 128), BF16)
    col = col.astype(F32)
    for k in range(8):
        here = spread(col[k : k + 1])
        for q in range(16):
            hot_ref[q * 16 : q * 16 + 16, k * 128 : (k + 1) * 128] = jnp.where(numbers[q] == here, one, zero)


def fill_values(row, highs, lows, load_ref):
    numbers = row_numbers(4)
    one, zero = jnp.ones((16, 128), BF16), jnp.zeros((16, 128), BF16)
    row = row.astype(F32)
    for k in range(8):
        here = spread(row[k : k + 1])
        masks = [numbers[q] == here for q in range(4)]
        values = [spread(x[k : k + 1]) for x in (*highs, *lows)] + [one]
        for part, value in enumerate(values[: load_ref.shape[0] // ROWS_A]):
            for q in range(4):
                at = part * ROWS_A + q * 16
                load_ref[at : at + 16, k * 128 : (k + 1) * 128] = jnp.where(masks[q], value, zero)


def scatter(load_ref, hot_ref):
    return lax.dot_general(
        load_ref[...], hot_ref[...], (((1,), (1,)), ((), ())), preferred_element_type=F32
    )


def gather(table, row, hot_ref):
    found = jnp.dot(table, hot_ref[...], preferred_element_type=F32)
    parts = found.shape[0] // FIELD_ROWS
    at = iota((ROWS_A, 128), 0)
    lines = [[], [], []]
    for k in range(8):
        mask = at == jnp.broadcast_to(row[k : k + 1], (ROWS_A, 128))
        for a in range(3):
            block = found[a * ROWS_A : (a + 1) * ROWS_A, k * 128 : (k + 1) * 128]
            for part in range(1, parts):
                base = part * FIELD_ROWS + a * ROWS_A
                block = block + found[base : base + ROWS_A, k * 128 : (k + 1) * 128]
            lines[a].append(jnp.sum(jnp.where(mask, block, 0.0), axis=0, keepdims=True))
    return [jnp.concatenate(line, axis=0) for line in lines]


def split_table(field, table_ref):
    hi, lo = hi_lo(field)
    table_ref[0:FIELD_ROWS] = hi.astype(BF16)
    table_ref[FIELD_ROWS : 2 * FIELD_ROWS] = lo.astype(BF16)


def push_of(sums, field):
    loads = sums[0:192] + sums[192:384]
    count = sums[384:448]
    return coupling * (loads - jnp.concatenate([count, count, count], axis=0) * field)


def plane(ref, a, z):
    base = (a * 4 + z) * 16
    return ref[base : base + 16, :].astype(F32)


def inner_tendency(f_ref, a, z):
    here = plane(f_ref, a, z)
    next_x = pltpu.roll(here, 255, 1)
    prev_x = pltpu.roll(here, 1, 1)
    across = next_x + prev_x - 4.0 * here
    slope_z = None
    if z < 3:
        next_z = plane(f_ref, a, z + 1)
        across = across + next_z
        slope_z = next_z
    if z > 0:
        prev_z = plane(f_ref, a, z - 1)
        across = across + prev_z
        slope_z = -prev_z if slope_z is None else slope_z - prev_z
    flow = plane(f_ref, 0, z) * (0.5 * (next_x - prev_x)) + plane(f_ref, 2, z) * (0.5 * slope_z)
    total = viscosity * across - flow
    return total + forcing if a == 0 else total


def below_term(f_ref, below):
    return (viscosity + 0.5 * plane(f_ref, 2, 0)) * below


def above_term(f_ref, above):
    return (viscosity - 0.5 * plane(f_ref, 2, 3)) * above


def lane_group(shape):
    return iota(shape, len(shape) - 1) // 32


def first_send(field_hbm, bubble_hbm, owner_hbm, dest_hbm, up_ref, down_ref, moved_ref,
               field_ref, bubble_ref, owner_ref, dest_ref, sems):
    pairs = ((dest_hbm, dest_ref), (owner_hbm, owner_ref), (bubble_hbm, bubble_ref), (field_hbm, field_ref))
    copies = [pltpu.make_async_copy(src, dst, sems.at[i]) for i, (src, dst) in enumerate(pairs)]
    for copy in copies:
        copy.start()
    for copy in copies[:3]:
        copy.wait()
    first, second = owner_ref[0], owner_ref[1]
    parts = []
    for a in range(3):
        parts += hi_lo(bubble_ref[a])
    parts += [((first >> 8) + 1).astype(F32), (first & 255).astype(F32)]
    parts = jnp.concatenate(parts, axis=1).astype(BF16)
    picked = jnp.dot(pick_matrix(dest_ref[0:1]).astype(BF16), parts, preferred_element_type=F32)
    later = jnp.concatenate([((second >> 8) + 1).astype(F32), (second & 255).astype(F32)], axis=1)
    later = jnp.dot(pick_matrix(dest_ref[1:2]).astype(BF16), later.astype(BF16), preferred_element_type=F32)
    moved_ref[...] = picked[:, 768:1024]
    for ref, at in ((up_ref, 0), (down_ref, 8)):
        lines = [picked[at : at + 8, i * 256 : (i + 1) * 256] for i in range(4)]
        lines += [later[at : at + 8], jnp.zeros((8, 256), F32)]
        ref[FIELD_ROWS:SEND_ROWS] = jnp.concatenate(lines, axis=0).astype(BF16)
    copies[3].wait()
    block = field_ref[...].astype(BF16)
    up_ref[0:FIELD_ROWS] = block
    down_ref[0:FIELD_ROWS] = block


def home_first(field_ref, bubble_ref, owner_ref, dest_ref, part_ref, seen_ref, put_ref, pick_ref,
               table_ref, hot_ref, load_ref):
    field = field_ref[...]
    split_table(field, table_ref)
    put_ref[...] = put_matrix(dest_ref[0:1])
    pick_ref[...] = pick_matrix(dest_ref[1:2])
    row, col = home_cells(owner_ref[0], dest_ref[0:1])
    sums = None
    for i in range(3):
        rows = slice(i * 8, i * 8 + 8)
        fill_columns(col[rows], hot_ref.at[i])
        pairs = [hi_lo(bubble_ref[a, rows]) for a in range(3)]
        fill_values(row[rows], [p[0] for p in pairs], [p[1] for p in pairs], load_ref.at[i])
        got = scatter(load_ref.at[i], hot_ref.at[i])
        sums = got if sums is None else sums + got
        seen = gather(table_ref[...], row[rows], hot_ref.at[i])
        for a in range(3):
            seen_ref[a, rows] = seen[a]
    push = push_of(sums, field)
    for a in range(3):
        for z in range(4):
            base = (a * 4 + z) * 16
            part_ref[base : base + 16] = inner_tendency(field_ref, a, z) + push[base : base + 16]


def tail_of(ref):
    return ref[FIELD_ROWS:SEND_ROWS, :].astype(F32)


def tail_cells(tail, line):
    at = tail[line * 8 : line * 8 + 8].astype(jnp.int32)
    return at[:, 0:128] - 1, at[:, 128:256]


def pack_pair(six, out_ref):
    group = lane_group((16, 128))
    group8 = lane_group((8, 128))
    for z in range(4):
        for half in range(2):
            tiles = [six[i][z][:, half * 128 : (half + 1) * 128] for i in range(6)]
            for o in range(4):
                def moved(x, target):
                    shift = ((target - o) % 4) * 32
                    return x if shift == 0 else pltpu.roll(x, shift, 1)
                main = moved(tiles[3], 3)
                for i in range(3):
                    main = jnp.where(group == i, moved(tiles[i], i), main)
                rest = moved(tiles[5][8:16], 3)
                rest = jnp.where(group8 == 2, moved(tiles[4][8:16], 2), rest)
                rest = jnp.where(group8 == 1, moved(tiles[5][0:8], 1), rest)
                rest = jnp.where(group8 == 0, moved(tiles[4][0:8], 0), rest)
                peer = z * 8 + half * 4 + o
                out_ref[peer] = jnp.concatenate([main, rest], axis=0).astype(BF16)


def unpack(ref, second, a, z):
    halves = []
    group = lane_group((16, 128))
    for half in range(2):
        total = None
        for o in range(4):
            chunk = ref[z * 8 + half * 4 + o].astype(F32)
            if not second:
                piece, at = chunk[0:16], a
            elif a == 0:
                piece, at = chunk[0:16], 3
            else:
                rest = chunk[16:24]
                piece, at = jnp.concatenate([rest, pltpu.roll(rest, 64, 1)], axis=0), a - 1
            shift = ((o - at) % 4) * 32
            piece = piece if shift == 0 else pltpu.roll(piece, shift, 1)
            total = piece if total is None else jnp.where(group == o, piece, total)
        halves.append(total)
    return jnp.concatenate(halves, axis=1)


def arrived(cells_ref, values_ref, first_line, cell_line, load_ref):
    row, col = tail_cells(tail_of(cells_ref), cell_line)
    tail = values_ref[first_line : first_line + 48, :].astype(F32)
    highs = [tail[a * 8 : a * 8 + 8, 0:128] for a in range(3)]
    lows = [tail[a * 8 : a * 8 + 8, 128:256] for a in range(3)]
    fill_values(row, highs, lows, load_ref)
    return col


def seen_afar(moved_ref, at, far_ref, hot_ref):
    cells = moved_ref[at : at + 8].astype(jnp.int32)
    fill_columns(cells[:, 128:256], hot_ref)
    return gather(far_ref[0:FIELD_ROWS], cells[:, 0:128] - 1, hot_ref)


def low_first(field_ref, part_ref, low_ref, moved_ref, out_ref, afar_ref, come_ref, hot_ref, far_ref, load_ref):
    fill_columns(tail_cells(tail_of(low_ref), 4)[1], come_ref)
    for a, line in enumerate(seen_afar(moved_ref, 8, low_ref, far_ref)):
        afar_ref[a] = line
    fill_columns(arrived(low_ref, low_ref, FIELD_ROWS, 3, load_ref), hot_ref)
    push = push_of(scatter(load_ref, hot_ref), field_ref[...])
    for a in range(3):
        for z in range(4):
            base = (a * 4 + z) * 16
            total = part_ref[base : base + 16] + push[base : base + 16]
            out_ref[base : base + 16] = total + below_term(field_ref, plane(low_ref, a, 3)) if z == 0 else total


def high_first(field_ref, part_ref, high_ref, moved_ref, afar_ref, seen_ref, bubble_ref, put_ref, pick_ref,
               tend_ref, send_ref, rate_ref, next_ref, slots_ref, come_ref, hot_ref, far_ref, load_ref):
    fill_columns(arrived(high_ref, high_ref, FIELD_ROWS, 3, load_ref), hot_ref)
    sums = scatter(load_ref, hot_ref)
    fill_columns(tail_cells(tail_of(high_ref), 4)[1], come_ref)
    near = seen_afar(moved_ref, 0, high_ref, far_ref)
    found = jnp.concatenate([jnp.concatenate([near[a], afar_ref[a]], axis=0) for a in range(3)], axis=1)
    back = jnp.dot(put_ref[...].astype(BF16), found.astype(BF16), preferred_element_type=F32)
    after = []
    for a in range(3):
        here = bubble_ref[a]
        rate = (seen_ref[a] + back[:, a * 128 : (a + 1) * 128] - here) / relax_time
        if a == 1:
            rate = rate + buoyancy
        rate_ref[a] = rate
        after.append(here + C1 * rate)
        next_ref[a] = after[a]
    parts = jnp.concatenate([piece for x in after for piece in hi_lo(x)], axis=1).astype(BF16)
    picked = jnp.dot(pick_ref[...].astype(BF16), parts, preferred_element_type=F32)
    for at in (0, 8):
        for a in range(3):
            line = at * 3 + a * 8
            slots_ref[line : line + 8] = picked[at : at + 8, a * 256 : (a + 1) * 256]
    push = push_of(sums, field_ref[...])
    six = [[None] * 4 for _ in range(6)]
    for a in range(3):
        for z in range(4):
            base = (a * 4 + z) * 16
            total = part_ref[base : base + 16] + push[base : base + 16]
            if z == 3:
                total = total + above_term(field_ref, plane(high_ref, a, 0))
            tend_ref[base : base + 16] = total
            here = field_ref[base : base + 16]
            six[a][z] = here
            six[3 + a][z] = (here - here.astype(BF16).astype(F32)) + C1 * total
    pack_pair(six, send_ref)


def columns_body(got_ref, first_ref, second_ref, send_ref):
    got = got_ref[...].astype(F32)
    main = got[:, 0:16].reshape(512, 128)
    rest = got[:, 16:24].reshape(256, 128)
    other = pltpu.roll(rest, 64, 1)
    rest = jnp.concatenate([rest.reshape(32, 8, 128), other.reshape(32, 8, 128)], axis=1).reshape(512, 128)
    group = lane_group((512, 128))
    gain = jnp.where(group == 0, pltpu.roll(main, 32, 1), pltpu.roll(rest, 32, 1))

    def wall(x):
        field = x.astype(BF16)
        wide = field.astype(F32)
        normal = jnp.where(group == 0, pltpu.roll(wide, 96, 1), jnp.where(group == 2, pltpu.roll(wide, 32, 1), wide))
        slopes = jnp.dot(first_ref[...], field, preferred_element_type=F32).astype(BF16).astype(F32)
        curves = jnp.dot(second_ref[...], field, preferred_element_type=F32).astype(BF16).astype(F32)
        return (viscosity * curves - normal * slopes).astype(BF16).astype(F32)

    wall_1 = wall(main)
    wall_2 = wall(main + (gain + C1 * wall_1))
    back = pltpu.roll(wall_2, 96, 1)
    ahead = pltpu.roll(wall_2, 32, 1)
    out = jnp.where(group == 3, back, wall_1).reshape(32, 16, 128)
    group8 = lane_group((32, 8, 128))
    tail = jnp.where(group8 < 2, back.reshape(32, 16, 128)[:, 0:8], ahead.reshape(32, 16, 128)[:, 8:16])
    send_ref[...] = jnp.concatenate([out, tail], axis=1).astype(BF16)


def middle_body(wall_ref, field_ref, part_ref, low_ref, high_ref, slots_ref, come_low_ref, come_high_ref,
                next_ref, tend_ref, first_ref, second_ref, table_ref):
    for a in range(3):
        for z in range(4):
            base = (a * 4 + z) * 16
            total = part_ref[base : base + 16] + unpack(wall_ref, False, a, z)
            tend_ref[base : base + 16] = total
            next_ref[base : base + 16] = field_ref[base : base + 16] + C1 * total
    table_ref[...] = next_ref[...].astype(BF16)
    sends = []
    for ref, come_ref, z, at in ((low_ref, come_low_ref, 0, 24), (high_ref, come_high_ref, 3, 0)):
        row, _ = tail_cells(tail_of(ref), 4)
        seen = gather(table_ref[...], row, come_ref)
        lines = [plane(next_ref, a, z) for a in range(3)]
        lines.append(slots_ref[at : at + 24])
        lines += [jnp.concatenate(seen[0:2], axis=1), jnp.concatenate([seen[2], jnp.zeros((8, 128), F32)], axis=1)]
        lines.append(jnp.zeros((8, 256), F32))
        sends.append(jnp.concatenate(lines, axis=0).astype(BF16))
    odd = parity()

    @pl.when(odd == 0)
    def _():
        first_ref[...], second_ref[...] = sends[0], sends[1]

    @pl.when(odd == 1)
    def _():
        first_ref[...], second_ref[...] = sends[1], sends[0]


def home_second(wall_ref, field_ref, tend_ref, bubble_ref, rate_ref, owner_ref, dest_ref,
                base_ref, late_ref, put_ref, table_ref, hot_ref, load_ref):
    field = field_ref[...]
    split_table(field, table_ref)
    put_ref[...] = put_matrix(dest_ref[1:2])
    row, col = home_cells(owner_ref[1], dest_ref[1:2])

    sums = None
    for i in range(3):
        rows = slice(i * 8, i * 8 + 8)
        hot, load = hot_ref.at[i], load_ref.at[i]
        fill_columns(col[rows], hot)
        pairs = [hi_lo(bubble_ref[a, rows]) for a in range(3)]
        fill_values(row[rows], [p[0] for p in pairs], [p[1] for p in pairs], load)
        got = scatter(load_ref.at[i], hot_ref.at[i])
        sums = got if sums is None else sums + got
        seen = gather(table_ref[...], row[rows], hot_ref.at[i])
        for a in range(3):
            here = bubble_ref[a, rows]
            rate = (seen[a] - here) / relax_time
            if a == 1:
                rate = rate + buoyancy
            late_ref[a, rows] = here + (C2 * rate + E2 * rate_ref[a, rows])
    push = push_of(sums, field)
    for a in range(3):
        for z in range(4):
            base = (a * 4 + z) * 16
            total = inner_tendency(field_ref, a, z) + push[base : base + 16] + unpack(wall_ref, True, a, z)
            earlier = tend_ref[base : base + 16]
            base_ref[base : base + 16] = field_ref[base : base + 16] + (C2 * total + E2 * earlier)


def late_push(cells_ref, values_ref, field_ref, come_ref, load_ref):
    arrived(cells_ref, values_ref, 48, 4, load_ref)
    return push_of(scatter(load_ref, come_ref), field_ref[...])


def late_side(below, base_ref, field_ref, cells_ref, come_ref, got_ref, out_ref, load_ref):
    push = late_push(cells_ref, got_ref, field_ref, come_ref, load_ref)
    for a in range(3):
        for z in range(4):
            base = (a * 4 + z) * 16
            total = push[base : base + 16]
            if z == (0 if below else 3):
                term = below_term if below else above_term
                total = total + term(field_ref, got_ref[a * 16 : a * 16 + 16, :].astype(F32))
            out_ref[base : base + 16] = base_ref[base : base + 16] + C2 * total


def first_late(base_ref, field_ref, low_ref, high_ref, come_low_ref, come_high_ref, first_ref, out_ref, load_ref):
    odd = parity()

    @pl.when(odd == 0)
    def _():
        late_side(True, base_ref, field_ref, low_ref, come_low_ref, first_ref, out_ref, load_ref)

    @pl.when(odd == 1)
    def _():
        late_side(False, base_ref, field_ref, high_ref, come_high_ref, first_ref, out_ref, load_ref)


def second_late(base_ref, field_ref, low_ref, high_ref, come_low_ref, come_high_ref, first_ref, second_ref,
                late_ref, put_ref, out_ref, bubble_ref, load_ref):
    odd = parity()

    def bubbles(high2_ref, low2_ref):
        returned = jnp.concatenate(
            [jnp.concatenate([ref[at : at + 8, :].astype(F32) for ref in (high2_ref, low2_ref)], axis=0) for at in (72, 80)],
            axis=1,
        )
        back = jnp.dot(put_ref[...].astype(BF16), returned.astype(BF16), preferred_element_type=F32)
        for a in range(3):
            bubble_ref[a] = late_ref[a] + (C2 / relax_time) * back[:, a * 128 : (a + 1) * 128]

    @pl.when(odd == 0)
    def _():
        bubbles(second_ref, first_ref)
        late_side(False, base_ref, field_ref, high_ref, come_high_ref, second_ref, out_ref, load_ref)

    @pl.when(odd == 1)
    def _():
        bubbles(first_ref, second_ref)
        late_side(True, base_ref, field_ref, low_ref, come_low_ref, second_ref, out_ref, load_ref)


def parity():
    return (lax.axis_index("pz") + 1) % 2


def swapped(x, first):
    length = lax.axis_size("pz")
    step = [(1 if (i % 2 == 0) == first else -1) for i in range(length)]
    return lax.ppermute(x, "pz", [(i, (i + step[i]) % length) for i in range(length)])


def shifted(x, by):
    length = lax.axis_size("pz")
    return lax.ppermute(x, "pz", [(i, (i + by) % length) for i in range(length)])


def exchange(x):
    return lax.all_to_all(x, "px", split_axis=0, concat_axis=0, tiled=True)


def on_device(velocity, first_deriv, second_deriv, bubble_vel, owner, dest):
    field = velocity.reshape(FIELD_ROWS, 256)
    block = ((FIELD_ROWS, 256), F32)
    rows = ((3, 24, 128), F32)
    hot = pltpu.VMEM((256, 1024), BF16)
    load = pltpu.VMEM((448, 1024), BF16)
    table = pltpu.VMEM((384, 256), BF16)
    hots, loads = pltpu.VMEM((3, 256, 1024), BF16), pltpu.VMEM((3, 448, 1024), BF16)
    packed = ((32, 24, 128), BF16)

    velocity_in, bubbles_in, owner_in, dest_in = (
        pltpu.with_memory_space_constraint(x, pltpu.HBM) for x in (field, bubble_vel, owner, dest)
    )
    up, down, moved, field, bubble_vel, owner, dest = pl.pallas_call(
        first_send,
        in_specs=[pl.BlockSpec(memory_space=pltpu.HBM)] * 4,
        out_shape=(
            pltpu.VMEM((SEND_ROWS, 256), BF16),
            pltpu.VMEM((SEND_ROWS, 256), BF16),
            pltpu.VMEM((16, 256), F32),
            pltpu.VMEM((FIELD_ROWS, 256), F32),
            pltpu.VMEM((3, 24, 128), F32),
            pltpu.VMEM((2, 24, 128), jnp.int32),
            pltpu.VMEM((2, 24), jnp.int32),
        ),
        scratch_shapes=[pltpu.SemaphoreType.DMA((4,))],
    )(velocity_in, bubbles_in, owner_in, dest_in)
    low, high = shifted(up, 1), shifted(down, -1)
    part, seen, put, pick = call(
        home_first, (block, rows, ((24, 16), F32), ((16, 24), F32)), (table, hots, loads)
    )(field, bubble_vel, owner, dest)
    spread_hot = ((256, 1024), BF16)
    part, afar, come_low = call(low_first, (block, ((3, 8, 128), F32), spread_hot), (hot, hot, load))(
        field, part, low, moved
    )
    part, to_columns, rate, bubbles, slots, come_high = call(
        high_first, (block, packed, rows, rows, ((48, 256), F32), spread_hot), (hot, hot, load)
    )(field, part, high, moved, afar, seen, bubble_vel, put, pick)
    columns = exchange(to_columns)
    (walls,) = call(columns_body, (packed,))(columns, first_deriv, second_deriv)
    walls = exchange(walls)
    lasts = ((LAST_ROWS, 256), BF16)
    middle, tend, first, second = call(
        middle_body, (block, block, lasts, lasts), (pltpu.VMEM((FIELD_ROWS, 256), BF16),)
    )(walls, field, part, low, high, slots, come_low, come_high)
    first, second = swapped(first, True), swapped(second, False)
    base, late, put = call(home_second, (block, rows, ((24, 16), F32)), (table, hots, loads))(
        walls, middle, tend, bubbles, rate, owner, dest
    )
    (base,) = call(first_late, (block,), (load,))(base, middle, low, high, come_low, come_high, first)
    field, bubbles = call(second_late, (block, rows), (load,))(
        base, middle, low, high, come_low, come_high, first, second, late, put
    )
    return (field.reshape(velocity.shape), bubbles)


def solution(mesh):
    return jax.shard_map(
        on_device,
        mesh=mesh,
        in_specs=(
            P(None, "pz", "px", None),
            P(),
            P(),
            P(None, ("px", "pz"), None),
            P(None, ("px", "pz"), None),
            P(None, ("px", "pz")),
        ),
        out_specs=(P(None, "pz", "px", None), P(None, ("px", "pz"), None)),
        check_vma=False,
    )
```

```python
import functools

import jax
import jax.numpy as jnp
from jax import lax
from jax.experimental import pallas as pl
from jax.experimental.pallas import tpu as pltpu
from jax.sharding import PartitionSpec as P

step_size = 0.5
viscosity = 0.4
relax_time = 0.5
coupling = 2.0
buoyancy = 0.5
forcing = 1.0
gammas = (8.0 / 15.0, 5.0 / 12.0)
zetas = (0.0, -17.0 / 60.0)

F32 = jnp.float32
BF16 = jnp.bfloat16
C1 = step_size * gammas[0]
C2 = step_size * gammas[1]
E2 = step_size * zetas[1]

ROWS_A = 64
FIELD_ROWS = 192
SEND_ROWS = 240
LAST_ROWS = 96


def iota(shape, dim):
    return lax.broadcasted_iota(jnp.int32, shape, dim)


def call(body, outs, scratch=()):
    return pl.pallas_call(
        body,
        out_shape=tuple(jax.ShapeDtypeStruct(s, d) for s, d in outs),
        scratch_shapes=list(scratch),
        compiler_params=pltpu.CompilerParams(vmem_limit_bytes=48 * 1024 * 1024),
    )


def hi_lo(x):
    hi = x.astype(BF16).astype(F32)
    return hi, x - hi


def pick_matrix(dest_row):
    up = jnp.where(dest_row == 1, 1.0, 0.0).astype(F32)
    down = jnp.where(dest_row == -1, 1.0, 0.0).astype(F32)
    slot = iota((16, 24), 0)
    marks = jnp.where(slot < 8, jnp.broadcast_to(up, (16, 24)), jnp.broadcast_to(down, (16, 24)))
    before = jnp.where(iota((24, 24), 0) < iota((24, 24), 1), 1.0, 0.0).astype(F32)
    rank = jnp.dot(marks.astype(BF16), before.astype(BF16), preferred_element_type=F32)
    wanted = jnp.where(slot < 8, slot, slot - 8).astype(F32)
    return jnp.where((rank == wanted) & (marks > 0.5), 1.0, 0.0).astype(F32)


def put_matrix(dest_row):
    r, c = iota((24, 24), 0), iota((24, 24), 1)
    wide = jnp.broadcast_to(dest_row, (24, 24))
    own = jnp.sum(jnp.where(r == c, wide, 0).astype(F32), axis=1, keepdims=True)
    rank_up = jnp.sum(jnp.where((c < r) & (wide == 1), 1.0, 0.0), axis=1, keepdims=True)
    rank_down = jnp.sum(jnp.where((c < r) & (wide == -1), 1.0, 0.0), axis=1, keepdims=True)
    slot = iota((24, 16), 1).astype(F32)
    hit_up = (own == 1.0) & (rank_up == slot)
    hit_down = (own == -1.0) & (rank_down + 8.0 == slot)
    return jnp.where(hit_up | hit_down, 1.0, 0.0).astype(F32)


def home_cells(cells, dest_row):
    r, c = iota((24, 24), 0), iota((24, 24), 1)
    wide = jnp.broadcast_to(dest_row, (24, 24))
    away = jnp.sum(jnp.where((r == c) & (wide != 0), 1.0, 0.0), axis=1, keepdims=True)
    row = jnp.where(away > 0.5, -1, cells >> 8)
    return row, cells & 255


def spread(line):
    return jnp.broadcast_to(line, (16, 128)).astype(BF16)


def row_numbers(count):
    at = iota((16, 128), 0)
    return [(at + 16 * q).astype(F32).astype(BF16) for q in range(count)]


def fill_columns(col, hot_ref):
    numbers = row_numbers(16)
    one, zero = jnp.ones((16, 128), BF16), jnp.zeros((16, 128), BF16)
    col = col.astype(F32)
    for k in range(8):
        here = spread(col[k : k + 1])
        for q in range(16):
            hot_ref[q * 16 : q * 16 + 16, k * 128 : (k + 1) * 128] = jnp.where(numbers[q] == here, one, zero)


def fill_values(row, highs, lows, load_ref):
    numbers = row_numbers(4)
    one, zero = jnp.ones((16, 128), BF16), jnp.zeros((16, 128), BF16)
    row = row.astype(F32)
    for k in range(8):
        here = spread(row[k : k + 1])
        masks = [numbers[q] == here for q in range(4)]
        values = [spread(x[k : k + 1]) for x in (*highs, *lows)] + [one]
        for part, value in enumerate(values[: load_ref.shape[0] // ROWS_A]):
            for q in range(4):
                at = part * ROWS_A + q * 16
                load_ref[at : at + 16, k * 128 : (k + 1) * 128] = jnp.where(masks[q], value, zero)


def scatter(load_ref, hot_ref):
    return lax.dot_general(
        load_ref[...], hot_ref[...], (((1,), (1,)), ((), ())), preferred_element_type=F32
    )


def gather(table, row, hot_ref):
    found = jnp.dot(table, hot_ref[...], preferred_element_type=F32)
    parts = found.shape[0] // FIELD_ROWS
    at = iota((ROWS_A, 128), 0)
    lines = [[], [], []]
    for k in range(8):
        mask = at == jnp.broadcast_to(row[k : k + 1], (ROWS_A, 128))
        for a in range(3):
            block = found[a * ROWS_A : (a + 1) * ROWS_A, k * 128 : (k + 1) * 128]
            for part in range(1, parts):
                base = part * FIELD_ROWS + a * ROWS_A
                block = block + found[base : base + ROWS_A, k * 128 : (k + 1) * 128]
            lines[a].append(jnp.sum(jnp.where(mask, block, 0.0), axis=0, keepdims=True))
    return [jnp.concatenate(line, axis=0) for line in lines]


def split_table(field, table_ref):
    hi, lo = hi_lo(field)
    table_ref[0:FIELD_ROWS] = hi.astype(BF16)
    table_ref[FIELD_ROWS : 2 * FIELD_ROWS] = lo.astype(BF16)


def push_of(sums, field):
    loads = sums[0:192] + sums[192:384]
    count = sums[384:448]
    return coupling * (loads - jnp.concatenate([count, count, count], axis=0) * field)


def plane(ref, a, z):
    base = (a * 4 + z) * 16
    return ref[base : base + 16, :].astype(F32)


def inner_tendency(f_ref, a, z):
    here = plane(f_ref, a, z)
    next_x = pltpu.roll(here, 255, 1)
    prev_x = pltpu.roll(here, 1, 1)
    across = next_x + prev_x - 4.0 * here
    slope_z = None
    if z < 3:
        next_z = plane(f_ref, a, z + 1)
        across = across + next_z
        slope_z = next_z
    if z > 0:
        prev_z = plane(f_ref, a, z - 1)
        across = across + prev_z
        slope_z = -prev_z if slope_z is None else slope_z - prev_z
    flow = plane(f_ref, 0, z) * (0.5 * (next_x - prev_x)) + plane(f_ref, 2, z) * (0.5 * slope_z)
    total = viscosity * across - flow
    return total + forcing if a == 0 else total


def below_term(f_ref, below):
    return (viscosity + 0.5 * plane(f_ref, 2, 0)) * below


def above_term(f_ref, above):
    return (viscosity - 0.5 * plane(f_ref, 2, 3)) * above


def lane_group(shape):
    return iota(shape, len(shape) - 1) // 32


def first_send(field_hbm, bubble_hbm, owner_hbm, dest_hbm, up_ref, down_ref, moved_ref,
               field_ref, bubble_ref, owner_ref, dest_ref, sems):
    pairs = ((dest_hbm, dest_ref), (owner_hbm, owner_ref), (bubble_hbm, bubble_ref), (field_hbm, field_ref))
    copies = [pltpu.make_async_copy(src, dst, sems.at[i]) for i, (src, dst) in enumerate(pairs)]
    for copy in copies:
        copy.start()
    for copy in copies[:3]:
        copy.wait()
    first, second = owner_ref[0], owner_ref[1]
    parts = []
    for a in range(3):
        parts += hi_lo(bubble_ref[a])
    parts += [((first >> 8) + 1).astype(F32), (first & 255).astype(F32)]
    parts = jnp.concatenate(parts, axis=1).astype(BF16)
    picked = jnp.dot(pick_matrix(dest_ref[0:1]).astype(BF16), parts, preferred_element_type=F32)
    later = jnp.concatenate([((second >> 8) + 1).astype(F32), (second & 255).astype(F32)], axis=1)
    later = jnp.dot(pick_matrix(dest_ref[1:2]).astype(BF16), later.astype(BF16), preferred_element_type=F32)
    moved_ref[...] = picked[:, 768:1024]
    for ref, at in ((up_ref, 0), (down_ref, 8)):
        lines = [picked[at : at + 8, i * 256 : (i + 1) * 256] for i in range(4)]
        lines += [later[at : at + 8], jnp.zeros((8, 256), F32)]
        ref[FIELD_ROWS:SEND_ROWS] = jnp.concatenate(lines, axis=0).astype(BF16)
    copies[3].wait()
    block = field_ref[...].astype(BF16)
    up_ref[0:FIELD_ROWS] = block
    down_ref[0:FIELD_ROWS] = block


def home_first(field_ref, bubble_ref, owner_ref, dest_ref, part_ref, seen_ref, put_ref, pick_ref,
               table_ref, hot_ref, load_ref):
    field = field_ref[...]
    split_table(field, table_ref)
    put_ref[...] = put_matrix(dest_ref[0:1])
    pick_ref[...] = pick_matrix(dest_ref[1:2])
    row, col = home_cells(owner_ref[0], dest_ref[0:1])
    sums = None
    for i in range(3):
        rows = slice(i * 8, i * 8 + 8)
        fill_columns(col[rows], hot_ref.at[i])
        pairs = [hi_lo(bubble_ref[a, rows]) for a in range(3)]
        fill_values(row[rows], [p[0] for p in pairs], [p[1] for p in pairs], load_ref.at[i])
        got = scatter(load_ref.at[i], hot_ref.at[i])
        sums = got if sums is None else sums + got
        seen = gather(table_ref[...], row[rows], hot_ref.at[i])
        for a in range(3):
            seen_ref[a, rows] = seen[a]
    push = push_of(sums, field)
    for a in range(3):
        for z in range(4):
            base = (a * 4 + z) * 16
            part_ref[base : base + 16] = inner_tendency(field_ref, a, z) + push[base : base + 16]


def tail_of(ref):
    return ref[FIELD_ROWS:SEND_ROWS, :].astype(F32)


def tail_cells(tail, line):
    at = tail[line * 8 : line * 8 + 8].astype(jnp.int32)
    return at[:, 0:128] - 1, at[:, 128:256]


def pack_pair(six, out_ref):
    group = lane_group((16, 128))
    group8 = lane_group((8, 128))
    for z in range(4):
        for half in range(2):
            tiles = [six[i][z][:, half * 128 : (half + 1) * 128] for i in range(6)]
            for o in range(4):
                def moved(x, target):
                    shift = ((target - o) % 4) * 32
                    return x if shift == 0 else pltpu.roll(x, shift, 1)
                main = moved(tiles[3], 3)
                for i in range(3):
                    main = jnp.where(group == i, moved(tiles[i], i), main)
                rest = moved(tiles[5][8:16], 3)
                rest = jnp.where(group8 == 2, moved(tiles[4][8:16], 2), rest)
                rest = jnp.where(group8 == 1, moved(tiles[5][0:8], 1), rest)
                rest = jnp.where(group8 == 0, moved(tiles[4][0:8], 0), rest)
                peer = z * 8 + half * 4 + o
                out_ref[peer] = jnp.concatenate([main, rest], axis=0).astype(BF16)


def unpack(ref, second, a, z):
    halves = []
    group = lane_group((16, 128))
    for half in range(2):
        total = None
        for o in range(4):
            chunk = ref[z * 8 + half * 4 + o].astype(F32)
            if not second:
                piece, at = chunk[0:16], a
            elif a == 0:
                piece, at = chunk[0:16], 3
            else:
                rest = chunk[16:24]
                piece, at = jnp.concatenate([rest, pltpu.roll(rest, 64, 1)], axis=0), a - 1
            shift = ((o - at) % 4) * 32
            piece = piece if shift == 0 else pltpu.roll(piece, shift, 1)
            total = piece if total is None else jnp.where(group == o, piece, total)
        halves.append(total)
    return jnp.concatenate(halves, axis=1)


def arrived(cells_ref, values_ref, first_line, cell_line, load_ref):
    row, col = tail_cells(tail_of(cells_ref), cell_line)
    tail = values_ref[first_line : first_line + 48, :].astype(F32)
    highs = [tail[a * 8 : a * 8 + 8, 0:128] for a in range(3)]
    lows = [tail[a * 8 : a * 8 + 8, 128:256] for a in range(3)]
    fill_values(row, highs, lows, load_ref)
    return col


def seen_afar(moved_ref, at, far_ref, hot_ref):
    cells = moved_ref[at : at + 8].astype(jnp.int32)
    fill_columns(cells[:, 128:256], hot_ref)
    return gather(far_ref[0:FIELD_ROWS], cells[:, 0:128] - 1, hot_ref)


def low_first(field_ref, part_ref, low_ref, moved_ref, out_ref, afar_ref, come_ref, hot_ref, far_ref, load_ref):
    fill_columns(tail_cells(tail_of(low_ref), 4)[1], come_ref)
    for a, line in enumerate(seen_afar(moved_ref, 8, low_ref, far_ref)):
        afar_ref[a] = line
    fill_columns(arrived(low_ref, low_ref, FIELD_ROWS, 3, load_ref), hot_ref)
    push = push_of(scatter(load_ref, hot_ref), field_ref[...])
    for a in range(3):
        for z in range(4):
            base = (a * 4 + z) * 16
            total = part_ref[base : base + 16] + push[base : base + 16]
            out_ref[base : base + 16] = total + below_term(field_ref, plane(low_ref, a, 3)) if z == 0 else total


def high_first(field_ref, part_ref, high_ref, moved_ref, afar_ref, seen_ref, bubble_ref, put_ref, pick_ref,
               tend_ref, send_ref, rate_ref, next_ref, slots_ref, come_ref, hot_ref, far_ref, load_ref):
    fill_columns(arrived(high_ref, high_ref, FIELD_ROWS, 3, load_ref), hot_ref)
    sums = scatter(load_ref, hot_ref)
    fill_columns(tail_cells(tail_of(high_ref), 4)[1], come_ref)
    near = seen_afar(moved_ref, 0, high_ref, far_ref)
    found = jnp.concatenate([jnp.concatenate([near[a], afar_ref[a]], axis=0) for a in range(3)], axis=1)
    back = jnp.dot(put_ref[...].astype(BF16), found.astype(BF16), preferred_element_type=F32)
    after = []
    for a in range(3):
        here = bubble_ref[a]
        rate = (seen_ref[a] + back[:, a * 128 : (a + 1) * 128] - here) / relax_time
        if a == 1:
            rate = rate + buoyancy
        rate_ref[a] = rate
        after.append(here + C1 * rate)
        next_ref[a] = after[a]
    parts = jnp.concatenate([piece for x in after for piece in hi_lo(x)], axis=1).astype(BF16)
    picked = jnp.dot(pick_ref[...].astype(BF16), parts, preferred_element_type=F32)
    for at in (0, 8):
        for a in range(3):
            line = at * 3 + a * 8
            slots_ref[line : line + 8] = picked[at : at + 8, a * 256 : (a + 1) * 256]
    push = push_of(sums, field_ref[...])
    six = [[None] * 4 for _ in range(6)]
    for a in range(3):
        for z in range(4):
            base = (a * 4 + z) * 16
            total = part_ref[base : base + 16] + push[base : base + 16]
            if z == 3:
                total = total + above_term(field_ref, plane(high_ref, a, 0))
            tend_ref[base : base + 16] = total
            here = field_ref[base : base + 16]
            six[a][z] = here
            six[3 + a][z] = (here - here.astype(BF16).astype(F32)) + C1 * total
    pack_pair(six, send_ref)


def columns_body(got_ref, first_ref, second_ref, send_ref):
    got = got_ref[...].astype(F32)
    main = got[:, 0:16].reshape(512, 128)
    rest = got[:, 16:24].reshape(256, 128)
    other = pltpu.roll(rest, 64, 1)
    rest = jnp.concatenate([rest.reshape(32, 8, 128), other.reshape(32, 8, 128)], axis=1).reshape(512, 128)
    group = lane_group((512, 128))
    gain = jnp.where(group == 0, pltpu.roll(main, 32, 1), pltpu.roll(rest, 32, 1))

    def wall(x):
        field = x.astype(BF16)
        wide = field.astype(F32)
        normal = jnp.where(group == 0, pltpu.roll(wide, 96, 1), jnp.where(group == 2, pltpu.roll(wide, 32, 1), wide))
        slopes = jnp.dot(first_ref[...], field, preferred_element_type=F32).astype(BF16).astype(F32)
        curves = jnp.dot(second_ref[...], field, preferred_element_type=F32).astype(BF16).astype(F32)
        return (viscosity * curves - normal * slopes).astype(BF16).astype(F32)

    wall_1 = wall(main)
    wall_2 = wall(main + (gain + C1 * wall_1))
    back = pltpu.roll(wall_2, 96, 1)
    ahead = pltpu.roll(wall_2, 32, 1)
    out = jnp.where(group == 3, back, wall_1).reshape(32, 16, 128)
    group8 = lane_group((32, 8, 128))
    tail = jnp.where(group8 < 2, back.reshape(32, 16, 128)[:, 0:8], ahead.reshape(32, 16, 128)[:, 8:16])
    send_ref[...] = jnp.concatenate([out, tail], axis=1).astype(BF16)


def middle_body(wall_ref, field_ref, part_ref, low_ref, high_ref, slots_ref, come_low_ref, come_high_ref,
                next_ref, tend_ref, up_ref, down_ref, table_ref):
    for a in range(3):
        for z in range(4):
            base = (a * 4 + z) * 16
            total = part_ref[base : base + 16] + unpack(wall_ref, False, a, z)
            tend_ref[base : base + 16] = total
            next_ref[base : base + 16] = field_ref[base : base + 16] + C1 * total
    table_ref[...] = next_ref[...].astype(BF16)
    ends = ((low_ref, come_low_ref, down_ref, 0, 24), (high_ref, come_high_ref, up_ref, 3, 0))
    for ref, come_ref, out_ref, z, at in ends:
        row, _ = tail_cells(tail_of(ref), 4)
        seen = gather(table_ref[...], row, come_ref)
        lines = [plane(next_ref, a, z) for a in range(3)]
        lines.append(slots_ref[at : at + 24])
        lines += [jnp.concatenate(seen[0:2], axis=1), jnp.concatenate([seen[2], jnp.zeros((8, 128), F32)], axis=1)]
        lines.append(jnp.zeros((8, 256), F32))
        out_ref[...] = jnp.concatenate(lines, axis=0).astype(BF16)


def home_second(wall_ref, field_ref, tend_ref, bubble_ref, rate_ref, owner_ref, dest_ref,
                base_ref, late_ref, put_ref, table_ref, hot_ref, load_ref):
    field = field_ref[...]
    split_table(field, table_ref)
    put_ref[...] = put_matrix(dest_ref[1:2])
    row, col = home_cells(owner_ref[1], dest_ref[1:2])

    sums = None
    for i in range(3):
        rows = slice(i * 8, i * 8 + 8)
        hot, load = hot_ref.at[i], load_ref.at[i]
        fill_columns(col[rows], hot)
        pairs = [hi_lo(bubble_ref[a, rows]) for a in range(3)]
        fill_values(row[rows], [p[0] for p in pairs], [p[1] for p in pairs], load)
        got = scatter(load_ref.at[i], hot_ref.at[i])
        sums = got if sums is None else sums + got
        seen = gather(table_ref[...], row[rows], hot_ref.at[i])
        for a in range(3):
            here = bubble_ref[a, rows]
            rate = (seen[a] - here) / relax_time
            if a == 1:
                rate = rate + buoyancy
            late_ref[a, rows] = here + (C2 * rate + E2 * rate_ref[a, rows])
    push = push_of(sums, field)
    for a in range(3):
        for z in range(4):
            base = (a * 4 + z) * 16
            total = inner_tendency(field_ref, a, z) + push[base : base + 16] + unpack(wall_ref, True, a, z)
            earlier = tend_ref[base : base + 16]
            base_ref[base : base + 16] = field_ref[base : base + 16] + (C2 * total + E2 * earlier)


def late_push(cells_ref, values_ref, field_ref, come_ref, load_ref):
    arrived(cells_ref, values_ref, 48, 4, load_ref)
    return push_of(scatter(load_ref, come_ref), field_ref[...])


def low_second(base_ref, field_ref, low_ref, low2_ref, come_ref, out_ref, load_ref):
    push = late_push(low_ref, low2_ref, field_ref, come_ref, load_ref)
    for a in range(3):
        for z in range(4):
            base = (a * 4 + z) * 16
            total = base_ref[base : base + 16] + C2 * push[base : base + 16]
            if z == 0:
                total = total + C2 * below_term(field_ref, low2_ref[a * 16 : a * 16 + 16, :].astype(F32))
            out_ref[base : base + 16] = total


def high_second(base_ref, field_ref, high_ref, low2_ref, high2_ref, late_ref, put_ref, come_ref,
                out_ref, bubble_ref, load_ref):
    push = late_push(high_ref, high2_ref, field_ref, come_ref, load_ref)
    returned = jnp.concatenate(
        [jnp.concatenate([ref[at : at + 8, :].astype(F32) for ref in (high2_ref, low2_ref)], axis=0) for at in (72, 80)],
        axis=1,
    )
    back = jnp.dot(put_ref[...].astype(BF16), returned.astype(BF16), preferred_element_type=F32)
    for a in range(3):
        bubble_ref[a] = late_ref[a] + (C2 / relax_time) * back[:, a * 128 : (a + 1) * 128]
    for a in range(3):
        for z in range(4):
            base = (a * 4 + z) * 16
            total = base_ref[base : base + 16] + C2 * push[base : base + 16]
            if z == 3:
                total = total + C2 * above_term(field_ref, high2_ref[a * 16 : a * 16 + 16, :].astype(F32))
            out_ref[base : base + 16] = total


def shifted(x, by):
    length = lax.axis_size("pz")
    return lax.ppermute(x, "pz", [(i, (i + by) % length) for i in range(length)])


def exchange(x):
    return lax.all_to_all(x, "px", split_axis=0, concat_axis=0, tiled=True)


def on_device(velocity, first_deriv, second_deriv, bubble_vel, owner, dest):
    field = velocity.reshape(FIELD_ROWS, 256)
    block = ((FIELD_ROWS, 256), F32)
    rows = ((3, 24, 128), F32)
    hot = pltpu.VMEM((256, 1024), BF16)
    load = pltpu.VMEM((448, 1024), BF16)
    table = pltpu.VMEM((384, 256), BF16)
    hots, loads = pltpu.VMEM((3, 256, 1024), BF16), pltpu.VMEM((3, 448, 1024), BF16)
    packed = ((32, 24, 128), BF16)

    velocity_in, bubbles_in, owner_in, dest_in = (
        pltpu.with_memory_space_constraint(x, pltpu.HBM) for x in (field, bubble_vel, owner, dest)
    )
    up, down, moved, field, bubble_vel, owner, dest = pl.pallas_call(
        first_send,
        in_specs=[pl.BlockSpec(memory_space=pltpu.HBM)] * 4,
        out_shape=(
            pltpu.VMEM((SEND_ROWS, 256), BF16),
            pltpu.VMEM((SEND_ROWS, 256), BF16),
            pltpu.VMEM((16, 256), F32),
            pltpu.VMEM((FIELD_ROWS, 256), F32),
            pltpu.VMEM((3, 24, 128), F32),
            pltpu.VMEM((2, 24, 128), jnp.int32),
            pltpu.VMEM((2, 24), jnp.int32),
        ),
        scratch_shapes=[pltpu.SemaphoreType.DMA((4,))],
    )(velocity_in, bubbles_in, owner_in, dest_in)
    low, high = shifted(up, 1), shifted(down, -1)
    part, seen, put, pick = call(
        home_first, (block, rows, ((24, 16), F32), ((16, 24), F32)), (table, hots, loads)
    )(field, bubble_vel, owner, dest)
    spread_hot = ((256, 1024), BF16)
    part, afar, come_low = call(low_first, (block, ((3, 8, 128), F32), spread_hot), (hot, hot, load))(
        field, part, low, moved
    )
    part, to_columns, rate, bubbles, slots, come_high = call(
        high_first, (block, packed, rows, rows, ((48, 256), F32), spread_hot), (hot, hot, load)
    )(field, part, high, moved, afar, seen, bubble_vel, put, pick)
    columns = exchange(to_columns)
    (walls,) = call(columns_body, (packed,))(columns, first_deriv, second_deriv)
    walls = exchange(walls)
    lasts = ((LAST_ROWS, 256), BF16)
    middle, tend, up, down = call(middle_body, (block, block, lasts, lasts), (pltpu.VMEM((FIELD_ROWS, 256), BF16),))(
        walls, field, part, low, high, slots, come_low, come_high
    )
    low2, high2 = shifted(up, 1), shifted(down, -1)
    base, late, put = call(
        home_second, (block, rows, ((24, 16), F32)), (table, hots, loads)
    )(walls, middle, tend, bubbles, rate, owner, dest)
    (base,) = call(low_second, (block,), (load,))(base, middle, low, low2, come_low)
    field, bubbles = call(high_second, (block, rows), (load,))(
        base, middle, high, low2, high2, late, put, come_high
    )
    return (field.reshape(velocity.shape), bubbles)


def solution(mesh):
    return jax.shard_map(
        on_device,
        mesh=mesh,
        in_specs=(
            P(None, "pz", "px", None),
            P(),
            P(),
            P(None, ("px", "pz"), None),
            P(None, ("px", "pz"), None),
            P(None, ("px", "pz")),
        ),
        out_specs=(P(None, "pz", "px", None), P(None, ("px", "pz"), None)),
        check_vma=False,
    )
```

```python
import functools

import jax
import jax.numpy as jnp
from jax import lax
from jax.experimental import pallas as pl
from jax.experimental.pallas import tpu as pltpu
from jax.sharding import PartitionSpec as P

step_size = 0.5
viscosity = 0.4
relax_time = 0.5
coupling = 2.0
buoyancy = 0.5
forcing = 1.0
gammas = (8.0 / 15.0, 5.0 / 12.0)
zetas = (0.0, -17.0 / 60.0)

F32 = jnp.float32
BF16 = jnp.bfloat16
C1 = step_size * gammas[0]
C2 = step_size * gammas[1]
E2 = step_size * zetas[1]

ROWS_A = 64
FIELD_ROWS = 192
SEND_ROWS = 232
LAST_ROWS = 88


def iota(shape, dim):
    return lax.broadcasted_iota(jnp.int32, shape, dim)


def call(body, outs, scratch=()):
    return pl.pallas_call(
        body,
        out_shape=tuple(jax.ShapeDtypeStruct(s, d) for s, d in outs),
        scratch_shapes=list(scratch),
        compiler_params=pltpu.CompilerParams(vmem_limit_bytes=48 * 1024 * 1024),
    )


def hi_lo(x):
    hi = x.astype(BF16).astype(F32)
    return hi, x - hi


def pick_matrix(dest_row):
    up = jnp.where(dest_row == 1, 1.0, 0.0).astype(F32)
    down = jnp.where(dest_row == -1, 1.0, 0.0).astype(F32)
    slot = iota((16, 24), 0)
    marks = jnp.where(slot < 8, jnp.broadcast_to(up, (16, 24)), jnp.broadcast_to(down, (16, 24)))
    before = jnp.where(iota((24, 24), 0) < iota((24, 24), 1), 1.0, 0.0).astype(F32)
    rank = jnp.dot(marks.astype(BF16), before.astype(BF16), preferred_element_type=F32)
    wanted = jnp.where(slot < 8, slot, slot - 8).astype(F32)
    return jnp.where((rank == wanted) & (marks > 0.5), 1.0, 0.0).astype(F32)


def put_matrix(dest_row):
    r, c = iota((24, 24), 0), iota((24, 24), 1)
    wide = jnp.broadcast_to(dest_row, (24, 24))
    own = jnp.sum(jnp.where(r == c, wide, 0).astype(F32), axis=1, keepdims=True)
    rank_up = jnp.sum(jnp.where((c < r) & (wide == 1), 1.0, 0.0), axis=1, keepdims=True)
    rank_down = jnp.sum(jnp.where((c < r) & (wide == -1), 1.0, 0.0), axis=1, keepdims=True)
    slot = iota((24, 16), 1).astype(F32)
    hit_up = (own == 1.0) & (rank_up == slot)
    hit_down = (own == -1.0) & (rank_down + 8.0 == slot)
    return jnp.where(hit_up | hit_down, 1.0, 0.0).astype(F32)


def home_cells(cells, dest_row):
    r, c = iota((24, 24), 0), iota((24, 24), 1)
    wide = jnp.broadcast_to(dest_row, (24, 24))
    away = jnp.sum(jnp.where((r == c) & (wide != 0), 1.0, 0.0), axis=1, keepdims=True)
    row = jnp.where(away > 0.5, -1, cells >> 8)
    return row, cells & 255


def spread(line):
    return jnp.broadcast_to(line, (16, 128)).astype(BF16)


def row_numbers(count):
    at = iota((16, 128), 0)
    return [(at + 16 * q).astype(F32).astype(BF16) for q in range(count)]


def fill_columns(col, hot_ref):
    numbers = row_numbers(16)
    one, zero = jnp.ones((16, 128), BF16), jnp.zeros((16, 128), BF16)
    col = col.astype(F32)
    for k in range(8):
        here = spread(col[k : k + 1])
        for q in range(16):
            hot_ref[q * 16 : q * 16 + 16, k * 128 : (k + 1) * 128] = jnp.where(numbers[q] == here, one, zero)


def fill_values(row, highs, lows, load_ref):
    numbers = row_numbers(4)
    one, zero = jnp.ones((16, 128), BF16), jnp.zeros((16, 128), BF16)
    row = row.astype(F32)
    for k in range(8):
        here = spread(row[k : k + 1])
        masks = [numbers[q] == here for q in range(4)]
        values = [spread(x[k : k + 1]) for x in (*highs, *lows)] + [one]
        for part, value in enumerate(values[: load_ref.shape[0] // ROWS_A]):
            for q in range(4):
                at = part * ROWS_A + q * 16
                load_ref[at : at + 16, k * 128 : (k + 1) * 128] = jnp.where(masks[q], value, zero)


def scatter(load_ref, hot_ref):
    return lax.dot_general(
        load_ref[...], hot_ref[...], (((1,), (1,)), ((), ())), preferred_element_type=F32
    )


def gather(table, row, hot_ref):
    found = jnp.dot(table, hot_ref[...], preferred_element_type=F32)
    parts = found.shape[0] // FIELD_ROWS
    at = iota((ROWS_A, 128), 0)
    lines = [[], [], []]
    for k in range(8):
        mask = at == jnp.broadcast_to(row[k : k + 1], (ROWS_A, 128))
        for a in range(3):
            block = found[a * ROWS_A : (a + 1) * ROWS_A, k * 128 : (k + 1) * 128]
            for part in range(1, parts):
                base = part * FIELD_ROWS + a * ROWS_A
                block = block + found[base : base + ROWS_A, k * 128 : (k + 1) * 128]
            lines[a].append(jnp.sum(jnp.where(mask, block, 0.0), axis=0, keepdims=True))
    return [jnp.concatenate(line, axis=0) for line in lines]


def split_table(field, table_ref):
    hi, lo = hi_lo(field)
    table_ref[0:FIELD_ROWS] = hi.astype(BF16)
    table_ref[FIELD_ROWS : 2 * FIELD_ROWS] = lo.astype(BF16)


def push_of(sums, field):
    loads = sums[0:192] + sums[192:384]
    count = sums[384:448]
    return coupling * (loads - jnp.concatenate([count, count, count], axis=0) * field)


def plane(ref, a, z):
    base = (a * 4 + z) * 16
    return ref[base : base + 16, :].astype(F32)


def inner_tendency(f_ref, a, z):
    here = plane(f_ref, a, z)
    next_x = pltpu.roll(here, 255, 1)
    prev_x = pltpu.roll(here, 1, 1)
    across = next_x + prev_x - 4.0 * here
    slope_z = None
    if z < 3:
        next_z = plane(f_ref, a, z + 1)
        across = across + next_z
        slope_z = next_z
    if z > 0:
        prev_z = plane(f_ref, a, z - 1)
        across = across + prev_z
        slope_z = -prev_z if slope_z is None else slope_z - prev_z
    flow = plane(f_ref, 0, z) * (0.5 * (next_x - prev_x)) + plane(f_ref, 2, z) * (0.5 * slope_z)
    total = viscosity * across - flow
    return total + forcing if a == 0 else total


def below_term(f_ref, below):
    return (viscosity + 0.5 * plane(f_ref, 2, 0)) * below


def above_term(f_ref, above):
    return (viscosity - 0.5 * plane(f_ref, 2, 3)) * above


def lane_group(shape):
    return iota(shape, len(shape) - 1) // 32


def first_send(field_hbm, bubble_hbm, owner_hbm, dest_hbm, up_ref, down_ref, moved_ref,
               field_ref, bubble_ref, owner_ref, dest_ref, sems):
    pairs = ((dest_hbm, dest_ref), (owner_hbm, owner_ref), (bubble_hbm, bubble_ref), (field_hbm, field_ref))
    copies = [pltpu.make_async_copy(src, dst, sems.at[i]) for i, (src, dst) in enumerate(pairs)]
    for copy in copies:
        copy.start()
    for copy in copies[:3]:
        copy.wait()
    first, second = owner_ref[0], owner_ref[1]
    parts = []
    for a in range(3):
        parts += hi_lo(bubble_ref[a])
    parts += [((first >> 8) + 1).astype(F32), (first & 255).astype(F32)]
    parts = jnp.concatenate(parts, axis=1).astype(BF16)
    picked = jnp.dot(pick_matrix(dest_ref[0:1]).astype(BF16), parts, preferred_element_type=F32)
    later = jnp.concatenate([((second >> 8) + 1).astype(F32), (second & 255).astype(F32)], axis=1)
    later = jnp.dot(pick_matrix(dest_ref[1:2]).astype(BF16), later.astype(BF16), preferred_element_type=F32)
    moved_ref[...] = picked[:, 768:1024]
    for ref, at in ((up_ref, 0), (down_ref, 8)):
        lines = [picked[at : at + 8, i * 256 : (i + 1) * 256] for i in range(4)]
        lines.append(later[at : at + 8])
        ref[FIELD_ROWS:SEND_ROWS] = jnp.concatenate(lines, axis=0).astype(BF16)
    copies[3].wait()
    block = field_ref[...].astype(BF16)
    up_ref[0:FIELD_ROWS] = block
    down_ref[0:FIELD_ROWS] = block


def home_first(field_ref, bubble_ref, owner_ref, dest_ref, part_ref, seen_ref, put_ref, pick_ref,
               table_ref, hot_ref, load_ref):
    field = field_ref[...]
    split_table(field, table_ref)
    put_ref[...] = put_matrix(dest_ref[0:1])
    pick_ref[...] = pick_matrix(dest_ref[1:2])
    row, col = home_cells(owner_ref[0], dest_ref[0:1])
    sums = None
    for i in range(3):
        rows = slice(i * 8, i * 8 + 8)
        fill_columns(col[rows], hot_ref.at[i])
        pairs = [hi_lo(bubble_ref[a, rows]) for a in range(3)]
        fill_values(row[rows], [p[0] for p in pairs], [p[1] for p in pairs], load_ref.at[i])
        got = scatter(load_ref.at[i], hot_ref.at[i])
        sums = got if sums is None else sums + got
        seen = gather(table_ref[...], row[rows], hot_ref.at[i])
        for a in range(3):
            seen_ref[a, rows] = seen[a]
    push = push_of(sums, field)
    for a in range(3):
        for z in range(4):
            base = (a * 4 + z) * 16
            part_ref[base : base + 16] = inner_tendency(field_ref, a, z) + push[base : base + 16]


def tail_of(ref):
    return ref[FIELD_ROWS:SEND_ROWS, :].astype(F32)


def tail_cells(tail, line):
    at = tail[line * 8 : line * 8 + 8].astype(jnp.int32)
    return at[:, 0:128] - 1, at[:, 128:256]


def pack_pair(six, out_ref):
    group = lane_group((16, 128))
    group8 = lane_group((8, 128))
    for z in range(4):
        for half in range(2):
            tiles = [six[i][z][:, half * 128 : (half + 1) * 128] for i in range(6)]
            for o in range(4):
                def moved(x, target):
                    shift = ((target - o) % 4) * 32
                    return x if shift == 0 else pltpu.roll(x, shift, 1)
                main = moved(tiles[3], 3)
                for i in range(3):
                    main = jnp.where(group == i, moved(tiles[i], i), main)
                rest = moved(tiles[5][8:16], 3)
                rest = jnp.where(group8 == 2, moved(tiles[4][8:16], 2), rest)
                rest = jnp.where(group8 == 1, moved(tiles[5][0:8], 1), rest)
                rest = jnp.where(group8 == 0, moved(tiles[4][0:8], 0), rest)
                peer = z * 8 + half * 4 + o
                out_ref[peer] = jnp.concatenate([main, rest], axis=0).astype(BF16)


def unpack(ref, second, a, z):
    halves = []
    group = lane_group((16, 128))
    for half in range(2):
        total = None
        for o in range(4):
            chunk = ref[z * 8 + half * 4 + o].astype(F32)
            if not second:
                piece, at = chunk[0:16], a
            elif a == 0:
                piece, at = chunk[0:16], 3
            else:
                rest = chunk[16:24]
                piece, at = jnp.concatenate([rest, pltpu.roll(rest, 64, 1)], axis=0), a - 1
            shift = ((o - at) % 4) * 32
            piece = piece if shift == 0 else pltpu.roll(piece, shift, 1)
            total = piece if total is None else jnp.where(group == o, piece, total)
        halves.append(total)
    return jnp.concatenate(halves, axis=1)


def arrived(cells_ref, values_ref, first_line, cell_line, load_ref):
    row, col = tail_cells(tail_of(cells_ref), cell_line)
    tail = values_ref[first_line : first_line + 40, :].astype(F32)
    highs = [tail[a * 8 : a * 8 + 8, 0:128] for a in range(3)]
    lows = [tail[a * 8 : a * 8 + 8, 128:256] for a in range(3)]
    fill_values(row, highs, lows, load_ref)
    return col


def seen_afar(moved_ref, at, far_ref, hot_ref):
    cells = moved_ref[at : at + 8].astype(jnp.int32)
    fill_columns(cells[:, 128:256], hot_ref)
    return gather(far_ref[0:FIELD_ROWS], cells[:, 0:128] - 1, hot_ref)


def low_first(field_ref, part_ref, low_ref, moved_ref, out_ref, afar_ref, come_ref, hot_ref, far_ref, load_ref):
    fill_columns(tail_cells(tail_of(low_ref), 4)[1], come_ref)
    for a, line in enumerate(seen_afar(moved_ref, 8, low_ref, far_ref)):
        afar_ref[a] = line
    fill_columns(arrived(low_ref, low_ref, FIELD_ROWS, 3, load_ref), hot_ref)
    push = push_of(scatter(load_ref, hot_ref), field_ref[...])
    for a in range(3):
        for z in range(4):
            base = (a * 4 + z) * 16
            total = part_ref[base : base + 16] + push[base : base + 16]
            out_ref[base : base + 16] = total + below_term(field_ref, plane(low_ref, a, 3)) if z == 0 else total


def high_first(field_ref, part_ref, high_ref, moved_ref, afar_ref, seen_ref, bubble_ref, put_ref, pick_ref,
               tend_ref, send_ref, rate_ref, next_ref, slots_ref, come_ref, hot_ref, far_ref, load_ref):
    fill_columns(arrived(high_ref, high_ref, FIELD_ROWS, 3, load_ref), hot_ref)
    sums = scatter(load_ref, hot_ref)
    fill_columns(tail_cells(tail_of(high_ref), 4)[1], come_ref)
    near = seen_afar(moved_ref, 0, high_ref, far_ref)
    found = jnp.concatenate([jnp.concatenate([near[a], afar_ref[a]], axis=0) for a in range(3)], axis=1)
    back = jnp.dot(put_ref[...].astype(BF16), found.astype(BF16), preferred_element_type=F32)
    after = []
    for a in range(3):
        here = bubble_ref[a]
        rate = (seen_ref[a] + back[:, a * 128 : (a + 1) * 128] - here) / relax_time
        if a == 1:
            rate = rate + buoyancy
        rate_ref[a] = rate
        after.append(here + C1 * rate)
        next_ref[a] = after[a]
    parts = jnp.concatenate([piece for x in after for piece in hi_lo(x)], axis=1).astype(BF16)
    picked = jnp.dot(pick_ref[...].astype(BF16), parts, preferred_element_type=F32)
    for at in (0, 8):
        for a in range(3):
            line = at * 3 + a * 8
            slots_ref[line : line + 8] = picked[at : at + 8, a * 256 : (a + 1) * 256]
    push = push_of(sums, field_ref[...])
    six = [[None] * 4 for _ in range(6)]
    for a in range(3):
        for z in range(4):
            base = (a * 4 + z) * 16
            total = part_ref[base : base + 16] + push[base : base + 16]
            if z == 3:
                total = total + above_term(field_ref, plane(high_ref, a, 0))
            tend_ref[base : base + 16] = total
            here = field_ref[base : base + 16]
            six[a][z] = here
            six[3 + a][z] = (here - here.astype(BF16).astype(F32)) + C1 * total
    pack_pair(six, send_ref)


def columns_body(got_ref, first_ref, second_ref, send_ref):
    got = got_ref[...].astype(F32)
    main = got[:, 0:16].reshape(512, 128)
    rest = got[:, 16:24].reshape(256, 128)
    other = pltpu.roll(rest, 64, 1)
    rest = jnp.concatenate([rest.reshape(32, 8, 128), other.reshape(32, 8, 128)], axis=1).reshape(512, 128)
    group = lane_group((512, 128))
    gain = jnp.where(group == 0, pltpu.roll(main, 32, 1), pltpu.roll(rest, 32, 1))

    def wall(x):
        field = x.astype(BF16)
        wide = field.astype(F32)
        normal = jnp.where(group == 0, pltpu.roll(wide, 96, 1), jnp.where(group == 2, pltpu.roll(wide, 32, 1), wide))
        slopes = jnp.dot(first_ref[...], field, preferred_element_type=F32).astype(BF16).astype(F32)
        curves = jnp.dot(second_ref[...], field, preferred_element_type=F32).astype(BF16).astype(F32)
        return (viscosity * curves - normal * slopes).astype(BF16).astype(F32)

    wall_1 = wall(main)
    wall_2 = wall(main + (gain + C1 * wall_1))
    back = pltpu.roll(wall_2, 96, 1)
    ahead = pltpu.roll(wall_2, 32, 1)
    out = jnp.where(group == 3, back, wall_1).reshape(32, 16, 128)
    group8 = lane_group((32, 8, 128))
    tail = jnp.where(group8 < 2, back.reshape(32, 16, 128)[:, 0:8], ahead.reshape(32, 16, 128)[:, 8:16])
    send_ref[...] = jnp.concatenate([out, tail], axis=1).astype(BF16)


def middle_body(wall_ref, field_ref, part_ref, low_ref, high_ref, slots_ref, come_low_ref, come_high_ref,
                next_ref, tend_ref, up_ref, down_ref, table_ref):
    for a in range(3):
        for z in range(4):
            base = (a * 4 + z) * 16
            total = part_ref[base : base + 16] + unpack(wall_ref, False, a, z)
            tend_ref[base : base + 16] = total
            next_ref[base : base + 16] = field_ref[base : base + 16] + C1 * total
    table_ref[...] = next_ref[...].astype(BF16)
    ends = ((low_ref, come_low_ref, down_ref, 0, 24), (high_ref, come_high_ref, up_ref, 3, 0))
    for ref, come_ref, out_ref, z, at in ends:
        row, _ = tail_cells(tail_of(ref), 4)
        seen = gather(table_ref[...], row, come_ref)
        lines = [plane(next_ref, a, z) for a in range(3)]
        lines.append(slots_ref[at : at + 24])
        lines += [jnp.concatenate(seen[0:2], axis=1), jnp.concatenate([seen[2], jnp.zeros((8, 128), F32)], axis=1)]
        out_ref[...] = jnp.concatenate(lines, axis=0).astype(BF16)


def home_second(wall_ref, field_ref, tend_ref, bubble_ref, rate_ref, owner_ref, dest_ref,
                base_ref, late_ref, put_ref, table_ref, hot_ref, load_ref):
    field = field_ref[...]
    split_table(field, table_ref)
    put_ref[...] = put_matrix(dest_ref[1:2])
    row, col = home_cells(owner_ref[1], dest_ref[1:2])

    sums = None
    for i in range(3):
        rows = slice(i * 8, i * 8 + 8)
        hot, load = hot_ref.at[i], load_ref.at[i]
        fill_columns(col[rows], hot)
        pairs = [hi_lo(bubble_ref[a, rows]) for a in range(3)]
        fill_values(row[rows], [p[0] for p in pairs], [p[1] for p in pairs], load)
        got = scatter(load_ref.at[i], hot_ref.at[i])
        sums = got if sums is None else sums + got
        seen = gather(table_ref[...], row[rows], hot_ref.at[i])
        for a in range(3):
            here = bubble_ref[a, rows]
            rate = (seen[a] - here) / relax_time
            if a == 1:
                rate = rate + buoyancy
            late_ref[a, rows] = here + (C2 * rate + E2 * rate_ref[a, rows])
    push = push_of(sums, field)
    for a in range(3):
        for z in range(4):
            base = (a * 4 + z) * 16
            total = inner_tendency(field_ref, a, z) + push[base : base + 16] + unpack(wall_ref, True, a, z)
            earlier = tend_ref[base : base + 16]
            base_ref[base : base + 16] = field_ref[base : base + 16] + (C2 * total + E2 * earlier)


def late_push(cells_ref, values_ref, field_ref, come_ref, load_ref):
    arrived(cells_ref, values_ref, 48, 4, load_ref)
    return push_of(scatter(load_ref, come_ref), field_ref[...])


def low_second(base_ref, field_ref, low_ref, low2_ref, come_ref, out_ref, load_ref):
    push = late_push(low_ref, low2_ref, field_ref, come_ref, load_ref)
    for a in range(3):
        for z in range(4):
            base = (a * 4 + z) * 16
            total = base_ref[base : base + 16] + C2 * push[base : base + 16]
            if z == 0:
                total = total + C2 * below_term(field_ref, low2_ref[a * 16 : a * 16 + 16, :].astype(F32))
            out_ref[base : base + 16] = total


def high_second(base_ref, field_ref, high_ref, low2_ref, high2_ref, late_ref, put_ref, come_ref,
                out_ref, bubble_ref, load_ref):
    push = late_push(high_ref, high2_ref, field_ref, come_ref, load_ref)
    returned = jnp.concatenate(
        [jnp.concatenate([ref[at : at + 8, :].astype(F32) for ref in (high2_ref, low2_ref)], axis=0) for at in (72, 80)],
        axis=1,
    )
    back = jnp.dot(put_ref[...].astype(BF16), returned.astype(BF16), preferred_element_type=F32)
    for a in range(3):
        bubble_ref[a] = late_ref[a] + (C2 / relax_time) * back[:, a * 128 : (a + 1) * 128]
    for a in range(3):
        for z in range(4):
            base = (a * 4 + z) * 16
            total = base_ref[base : base + 16] + C2 * push[base : base + 16]
            if z == 3:
                total = total + C2 * above_term(field_ref, high2_ref[a * 16 : a * 16 + 16, :].astype(F32))
            out_ref[base : base + 16] = total


def shifted(x, by):
    length = lax.axis_size("pz")
    return lax.ppermute(x, "pz", [(i, (i + by) % length) for i in range(length)])


def exchange(x):
    return lax.all_to_all(x, "px", split_axis=0, concat_axis=0, tiled=True)


def on_device(velocity, first_deriv, second_deriv, bubble_vel, owner, dest):
    field = velocity.reshape(FIELD_ROWS, 256)
    block = ((FIELD_ROWS, 256), F32)
    rows = ((3, 24, 128), F32)
    hot = pltpu.VMEM((256, 1024), BF16)
    load = pltpu.VMEM((448, 1024), BF16)
    table = pltpu.VMEM((384, 256), BF16)
    hots, loads = pltpu.VMEM((3, 256, 1024), BF16), pltpu.VMEM((3, 448, 1024), BF16)
    packed = ((32, 24, 128), BF16)

    velocity_in, bubbles_in, owner_in, dest_in = (
        pltpu.with_memory_space_constraint(x, pltpu.HBM) for x in (field, bubble_vel, owner, dest)
    )
    up, down, moved, field, bubble_vel, owner, dest = pl.pallas_call(
        first_send,
        in_specs=[pl.BlockSpec(memory_space=pltpu.HBM)] * 4,
        out_shape=(
            pltpu.VMEM((SEND_ROWS, 256), BF16),
            pltpu.VMEM((SEND_ROWS, 256), BF16),
            pltpu.VMEM((16, 256), F32),
            pltpu.VMEM((FIELD_ROWS, 256), F32),
            pltpu.VMEM((3, 24, 128), F32),
            pltpu.VMEM((2, 24, 128), jnp.int32),
            pltpu.VMEM((2, 24), jnp.int32),
        ),
        scratch_shapes=[pltpu.SemaphoreType.DMA((4,))],
    )(velocity_in, bubbles_in, owner_in, dest_in)
    low, high = shifted(up, 1), shifted(down, -1)
    part, seen, put, pick = call(
        home_first, (block, rows, ((24, 16), F32), ((16, 24), F32)), (table, hots, loads)
    )(field, bubble_vel, owner, dest)
    spread_hot = ((256, 1024), BF16)
    part, afar, come_low = call(low_first, (block, ((3, 8, 128), F32), spread_hot), (hot, hot, load))(
        field, part, low, moved
    )
    part, to_columns, rate, bubbles, slots, come_high = call(
        high_first, (block, packed, rows, rows, ((48, 256), F32), spread_hot), (hot, hot, load)
    )(field, part, high, moved, afar, seen, bubble_vel, put, pick)
    columns = exchange(to_columns)
    (walls,) = call(columns_body, (packed,))(columns, first_deriv, second_deriv)
    walls = exchange(walls)
    lasts = ((LAST_ROWS, 256), BF16)
    middle, tend, up, down = call(middle_body, (block, block, lasts, lasts), (pltpu.VMEM((FIELD_ROWS, 256), BF16),))(
        walls, field, part, low, high, slots, come_low, come_high
    )
    low2, high2 = shifted(up, 1), shifted(down, -1)
    base, late, put = call(
        home_second, (block, rows, ((24, 16), F32)), (table, hots, loads)
    )(walls, middle, tend, bubbles, rate, owner, dest)
    (base,) = call(low_second, (block,), (load,))(base, middle, low, low2, come_low)
    field, bubbles = call(high_second, (block, rows), (load,))(
        base, middle, high, low2, high2, late, put, come_high
    )
    return (field.reshape(velocity.shape), bubbles)


def solution(mesh):
    return jax.shard_map(
        on_device,
        mesh=mesh,
        in_specs=(
            P(None, "pz", "px", None),
            P(),
            P(),
            P(None, ("px", "pz"), None),
            P(None, ("px", "pz"), None),
            P(None, ("px", "pz")),
        ),
        out_specs=(P(None, "pz", "px", None), P(None, ("px", "pz"), None)),
        check_vma=False,
    )
```

```python
import functools

import jax
import jax.numpy as jnp
from jax import lax
from jax.experimental import pallas as pl
from jax.experimental.pallas import tpu as pltpu
from jax.sharding import PartitionSpec as P

step_size = 0.5
viscosity = 0.4
relax_time = 0.5
coupling = 2.0
buoyancy = 0.5
forcing = 1.0
gammas = (8.0 / 15.0, 5.0 / 12.0)
zetas = (0.0, -17.0 / 60.0)

F32 = jnp.float32
BF16 = jnp.bfloat16
C1 = step_size * gammas[0]
C2 = step_size * gammas[1]
E2 = step_size * zetas[1]

ROWS_A = 64
FIELD_ROWS = 192
SEND_ROWS = 232
LAST_ROWS = 88


def iota(shape, dim):
    return lax.broadcasted_iota(jnp.int32, shape, dim)


def call(body, outs, scratch=()):
    return pl.pallas_call(
        body,
        out_shape=tuple(jax.ShapeDtypeStruct(s, d) for s, d in outs),
        scratch_shapes=list(scratch),
        compiler_params=pltpu.CompilerParams(vmem_limit_bytes=48 * 1024 * 1024),
    )


def hi_lo(x):
    hi = x.astype(BF16).astype(F32)
    return hi, x - hi


def pick_matrix(dest_row):
    up = jnp.where(dest_row == 1, 1.0, 0.0).astype(F32)
    down = jnp.where(dest_row == -1, 1.0, 0.0).astype(F32)
    slot = iota((16, 24), 0)
    marks = jnp.where(slot < 8, jnp.broadcast_to(up, (16, 24)), jnp.broadcast_to(down, (16, 24)))
    before = jnp.where(iota((24, 24), 0) < iota((24, 24), 1), 1.0, 0.0).astype(F32)
    rank = jnp.dot(marks.astype(BF16), before.astype(BF16), preferred_element_type=F32)
    wanted = jnp.where(slot < 8, slot, slot - 8).astype(F32)
    return jnp.where((rank == wanted) & (marks > 0.5), 1.0, 0.0).astype(F32)


def put_matrix(dest_row):
    r, c = iota((24, 24), 0), iota((24, 24), 1)
    wide = jnp.broadcast_to(dest_row, (24, 24))
    own = jnp.sum(jnp.where(r == c, wide, 0).astype(F32), axis=1, keepdims=True)
    rank_up = jnp.sum(jnp.where((c < r) & (wide == 1), 1.0, 0.0), axis=1, keepdims=True)
    rank_down = jnp.sum(jnp.where((c < r) & (wide == -1), 1.0, 0.0), axis=1, keepdims=True)
    slot = iota((24, 16), 1).astype(F32)
    hit_up = (own == 1.0) & (rank_up == slot)
    hit_down = (own == -1.0) & (rank_down + 8.0 == slot)
    return jnp.where(hit_up | hit_down, 1.0, 0.0).astype(F32)


def home_cells(cells, dest_row):
    r, c = iota((24, 24), 0), iota((24, 24), 1)
    wide = jnp.broadcast_to(dest_row, (24, 24))
    away = jnp.sum(jnp.where((r == c) & (wide != 0), 1.0, 0.0), axis=1, keepdims=True)
    row = jnp.where(away > 0.5, -1, cells >> 8)
    return row, cells & 255


def spread(line):
    return jnp.broadcast_to(line, (16, 128)).astype(BF16)


def row_numbers(count):
    at = iota((16, 128), 0)
    return [(at + 16 * q).astype(F32).astype(BF16) for q in range(count)]


def fill_columns(col, hot_ref):
    numbers = row_numbers(16)
    one, zero = jnp.ones((16, 128), BF16), jnp.zeros((16, 128), BF16)
    col = col.astype(F32)
    for k in range(8):
        here = spread(col[k : k + 1])
        for q in range(16):
            hot_ref[q * 16 : q * 16 + 16, k * 128 : (k + 1) * 128] = jnp.where(numbers[q] == here, one, zero)


def fill_values(row, highs, lows, load_ref):
    numbers = row_numbers(4)
    one, zero = jnp.ones((16, 128), BF16), jnp.zeros((16, 128), BF16)
    row = row.astype(F32)
    for k in range(8):
        here = spread(row[k : k + 1])
        masks = [numbers[q] == here for q in range(4)]
        values = [spread(x[k : k + 1]) for x in (*highs, *lows)] + [one]
        for part, value in enumerate(values[: load_ref.shape[0] // ROWS_A]):
            for q in range(4):
                at = part * ROWS_A + q * 16
                load_ref[at : at + 16, k * 128 : (k + 1) * 128] = jnp.where(masks[q], value, zero)


def scatter(load_ref, hot_ref):
    return lax.dot_general(
        load_ref[...], hot_ref[...], (((1,), (1,)), ((), ())), preferred_element_type=F32
    )


def gather(table, row, hot_ref):
    found = jnp.dot(table, hot_ref[...], preferred_element_type=F32)
    parts = found.shape[0] // FIELD_ROWS
    at = iota((ROWS_A, 128), 0)
    lines = [[], [], []]
    for k in range(8):
        mask = at == jnp.broadcast_to(row[k : k + 1], (ROWS_A, 128))
        for a in range(3):
            block = found[a * ROWS_A : (a + 1) * ROWS_A, k * 128 : (k + 1) * 128]
            for part in range(1, parts):
                base = part * FIELD_ROWS + a * ROWS_A
                block = block + found[base : base + ROWS_A, k * 128 : (k + 1) * 128]
            lines[a].append(jnp.sum(jnp.where(mask, block, 0.0), axis=0, keepdims=True))
    return [jnp.concatenate(line, axis=0) for line in lines]


def split_table(field, table_ref):
    hi, lo = hi_lo(field)
    table_ref[0:FIELD_ROWS] = hi.astype(BF16)
    table_ref[FIELD_ROWS : 2 * FIELD_ROWS] = lo.astype(BF16)


def push_of(sums, field):
    loads = sums[0:192] + sums[192:384]
    count = sums[384:448]
    return coupling * (loads - jnp.concatenate([count, count, count], axis=0) * field)


def plane(ref, a, z):
    base = (a * 4 + z) * 16
    return ref[base : base + 16, :].astype(F32)


def inner_tendency(f_ref, a, z):
    here = plane(f_ref, a, z)
    next_x = pltpu.roll(here, 255, 1)
    prev_x = pltpu.roll(here, 1, 1)
    across = next_x + prev_x - 4.0 * here
    slope_z = None
    if z < 3:
        next_z = plane(f_ref, a, z + 1)
        across = across + next_z
        slope_z = next_z
    if z > 0:
        prev_z = plane(f_ref, a, z - 1)
        across = across + prev_z
        slope_z = -prev_z if slope_z is None else slope_z - prev_z
    flow = plane(f_ref, 0, z) * (0.5 * (next_x - prev_x)) + plane(f_ref, 2, z) * (0.5 * slope_z)
    total = viscosity * across - flow
    return total + forcing if a == 0 else total


def below_term(f_ref, below):
    return (viscosity + 0.5 * plane(f_ref, 2, 0)) * below


def above_term(f_ref, above):
    return (viscosity - 0.5 * plane(f_ref, 2, 3)) * above


def lane_group(shape):
    return iota(shape, len(shape) - 1) // 32


def first_send(field_hbm, bubble_hbm, owner_hbm, dest_hbm, up_ref, down_ref, moved_ref,
               field_ref, bubble_ref, owner_ref, dest_ref, sems):
    pairs = ((dest_hbm, dest_ref), (owner_hbm, owner_ref), (bubble_hbm, bubble_ref), (field_hbm, field_ref))
    copies = [pltpu.make_async_copy(src, dst, sems.at[i]) for i, (src, dst) in enumerate(pairs)]
    for copy in copies:
        copy.start()
    for copy in copies[:3]:
        copy.wait()
    first, second = owner_ref[0], owner_ref[1]
    parts = []
    for a in range(3):
        parts += hi_lo(bubble_ref[a])
    parts += [((first >> 8) + 1).astype(F32), (first & 255).astype(F32)]
    parts = jnp.concatenate(parts, axis=1).astype(BF16)
    picked = jnp.dot(pick_matrix(dest_ref[0:1]).astype(BF16), parts, preferred_element_type=F32)
    later = jnp.concatenate([((second >> 8) + 1).astype(F32), (second & 255).astype(F32)], axis=1)
    later = jnp.dot(pick_matrix(dest_ref[1:2]).astype(BF16), later.astype(BF16), preferred_element_type=F32)
    moved_ref[...] = picked[:, 768:1024]
    for ref, at in ((up_ref, 0), (down_ref, 8)):
        lines = [picked[at : at + 8, i * 256 : (i + 1) * 256] for i in range(4)]
        lines.append(later[at : at + 8])
        ref[FIELD_ROWS:SEND_ROWS] = jnp.concatenate(lines, axis=0).astype(BF16)
    copies[3].wait()
    block = field_ref[...].astype(BF16)
    up_ref[0:FIELD_ROWS] = block
    down_ref[0:FIELD_ROWS] = block


def home_first(field_ref, bubble_ref, owner_ref, dest_ref, part_ref, seen_ref, put_ref, pick_ref,
               table_ref, hot_ref, load_ref):
    field = field_ref[...]
    split_table(field, table_ref)
    put_ref[...] = put_matrix(dest_ref[0:1])
    pick_ref[...] = pick_matrix(dest_ref[1:2])
    row, col = home_cells(owner_ref[0], dest_ref[0:1])
    sums = None
    for i in range(3):
        rows = slice(i * 8, i * 8 + 8)
        fill_columns(col[rows], hot_ref.at[i])
        pairs = [hi_lo(bubble_ref[a, rows]) for a in range(3)]
        fill_values(row[rows], [p[0] for p in pairs], [p[1] for p in pairs], load_ref.at[i])
        got = scatter(load_ref.at[i], hot_ref.at[i])
        sums = got if sums is None else sums + got
        seen = gather(table_ref[...], row[rows], hot_ref.at[i])
        for a in range(3):
            seen_ref[a, rows] = seen[a]
    push = push_of(sums, field)
    for a in range(3):
        for z in range(4):
            base = (a * 4 + z) * 16
            part_ref[base : base + 16] = inner_tendency(field_ref, a, z) + push[base : base + 16]


def tail_of(ref):
    return ref[FIELD_ROWS:SEND_ROWS, :].astype(F32)


def tail_cells(tail, line):
    at = tail[line * 8 : line * 8 + 8].astype(jnp.int32)
    return at[:, 0:128] - 1, at[:, 128:256]


def pack_pair(six, out_ref):
    group = lane_group((16, 128))
    group8 = lane_group((8, 128))
    for z in range(4):
        for half in range(2):
            tiles = [six[i][z][:, half * 128 : (half + 1) * 128] for i in range(6)]
            for o in range(4):
                def moved(x, target):
                    shift = ((target - o) % 4) * 32
                    return x if shift == 0 else pltpu.roll(x, shift, 1)
                main = moved(tiles[3], 3)
                for i in range(3):
                    main = jnp.where(group == i, moved(tiles[i], i), main)
                rest = moved(tiles[5][8:16], 3)
                rest = jnp.where(group8 == 2, moved(tiles[4][8:16], 2), rest)
                rest = jnp.where(group8 == 1, moved(tiles[5][0:8], 1), rest)
                rest = jnp.where(group8 == 0, moved(tiles[4][0:8], 0), rest)
                peer = z * 8 + half * 4 + o
                out_ref[peer] = jnp.concatenate([main, rest], axis=0).astype(BF16)


def unpack(ref, second, a, z):
    halves = []
    group = lane_group((16, 128))
    for half in range(2):
        total = None
        for o in range(4):
            chunk = ref[z * 8 + half * 4 + o].astype(F32)
            if not second:
                piece, at = chunk[0:16], a
            elif a == 0:
                piece, at = chunk[0:16], 3
            else:
                rest = chunk[16:24]
                piece, at = jnp.concatenate([rest, pltpu.roll(rest, 64, 1)], axis=0), a - 1
            shift = ((o - at) % 4) * 32
            piece = piece if shift == 0 else pltpu.roll(piece, shift, 1)
            total = piece if total is None else jnp.where(group == o, piece, total)
        halves.append(total)
    return jnp.concatenate(halves, axis=1)


def arrived(cells_ref, values_ref, first_line, cell_line, load_ref):
    row, col = tail_cells(tail_of(cells_ref), cell_line)
    tail = values_ref[first_line : first_line + 40, :].astype(F32)
    highs = [tail[a * 8 : a * 8 + 8, 0:128] for a in range(3)]
    lows = [tail[a * 8 : a * 8 + 8, 128:256] for a in range(3)]
    fill_values(row, highs, lows, load_ref)
    return col


def seen_afar(moved_ref, at, far_ref, hot_ref):
    cells = moved_ref[at : at + 8].astype(jnp.int32)
    fill_columns(cells[:, 128:256], hot_ref)
    return gather(far_ref[0:FIELD_ROWS], cells[:, 0:128] - 1, hot_ref)


def low_first(field_ref, part_ref, low_ref, moved_ref, out_ref, afar_ref, come_ref, hot_ref, far_ref, load_ref):
    fill_columns(tail_cells(tail_of(low_ref), 4)[1], come_ref)
    for a, line in enumerate(seen_afar(moved_ref, 8, low_ref, far_ref)):
        afar_ref[a] = line
    fill_columns(arrived(low_ref, low_ref, FIELD_ROWS, 3, load_ref), hot_ref)
    push = push_of(scatter(load_ref, hot_ref), field_ref[...])
    for a in range(3):
        for z in range(4):
            base = (a * 4 + z) * 16
            total = part_ref[base : base + 16] + push[base : base + 16]
            out_ref[base : base + 16] = total + below_term(field_ref, plane(low_ref, a, 3)) if z == 0 else total


def high_first(field_ref, part_ref, high_ref, moved_ref, afar_ref, seen_ref, bubble_ref, put_ref, pick_ref,
               tend_ref, send_ref, rate_ref, next_ref, slots_ref, come_ref, hot_ref, far_ref, load_ref):
    fill_columns(arrived(high_ref, high_ref, FIELD_ROWS, 3, load_ref), hot_ref)
    sums = scatter(load_ref, hot_ref)
    fill_columns(tail_cells(tail_of(high_ref), 4)[1], come_ref)
    near = seen_afar(moved_ref, 0, high_ref, far_ref)
    found = jnp.concatenate([jnp.concatenate([near[a], afar_ref[a]], axis=0) for a in range(3)], axis=1)
    back = jnp.dot(put_ref[...].astype(BF16), found.astype(BF16), preferred_element_type=F32)
    after = []
    for a in range(3):
        here = bubble_ref[a]
        rate = (seen_ref[a] + back[:, a * 128 : (a + 1) * 128] - here) / relax_time
        if a == 1:
            rate = rate + buoyancy
        rate_ref[a] = rate
        after.append(here + C1 * rate)
        next_ref[a] = after[a]
    parts = jnp.concatenate([piece for x in after for piece in hi_lo(x)], axis=1).astype(BF16)
    picked = jnp.dot(pick_ref[...].astype(BF16), parts, preferred_element_type=F32)
    for at in (0, 8):
        for a in range(3):
            line = at * 3 + a * 8
            slots_ref[line : line + 8] = picked[at : at + 8, a * 256 : (a + 1) * 256]
    push = push_of(sums, field_ref[...])
    six = [[None] * 4 for _ in range(6)]
    for a in range(3):
        for z in range(4):
            base = (a * 4 + z) * 16
            total = part_ref[base : base + 16] + push[base : base + 16]
            if z == 3:
                total = total + above_term(field_ref, plane(high_ref, a, 0))
            tend_ref[base : base + 16] = total
            here = field_ref[base : base + 16]
            six[a][z] = here
            six[3 + a][z] = (here - here.astype(BF16).astype(F32)) + C1 * total
    pack_pair(six, send_ref)


def columns_body(got_ref, first_ref, second_ref, send_ref):
    got = got_ref[...].astype(F32)
    main = got[:, 0:16].reshape(512, 128)
    rest = got[:, 16:24].reshape(256, 128)
    other = pltpu.roll(rest, 64, 1)
    rest = jnp.concatenate([rest.reshape(32, 8, 128), other.reshape(32, 8, 128)], axis=1).reshape(512, 128)
    group = lane_group((512, 128))
    gain = jnp.where(group == 0, pltpu.roll(main, 32, 1), pltpu.roll(rest, 32, 1))

    def wall(x):
        field = x.astype(BF16)
        wide = field.astype(F32)
        normal = jnp.where(group == 0, pltpu.roll(wide, 96, 1), jnp.where(group == 2, pltpu.roll(wide, 32, 1), wide))
        slopes = jnp.dot(first_ref[...], field, preferred_element_type=F32).astype(BF16).astype(F32)
        curves = jnp.dot(second_ref[...], field, preferred_element_type=F32).astype(BF16).astype(F32)
        return (viscosity * curves - normal * slopes).astype(BF16).astype(F32)

    wall_1 = wall(main)
    wall_2 = wall(main + (gain + C1 * wall_1))
    back = pltpu.roll(wall_2, 96, 1)
    ahead = pltpu.roll(wall_2, 32, 1)
    out = jnp.where(group == 3, back, wall_1).reshape(32, 16, 128)
    group8 = lane_group((32, 8, 128))
    tail = jnp.where(group8 < 2, back.reshape(32, 16, 128)[:, 0:8], ahead.reshape(32, 16, 128)[:, 8:16])
    send_ref[...] = jnp.concatenate([out, tail], axis=1).astype(BF16)


def middle_body(wall_ref, field_ref, part_ref, low_ref, high_ref, slots_ref, come_low_ref, come_high_ref,
                next_ref, tend_ref, up_ref, down_ref, table_ref):
    for a in range(3):
        for z in range(4):
            base = (a * 4 + z) * 16
            total = part_ref[base : base + 16] + unpack(wall_ref, False, a, z)
            tend_ref[base : base + 16] = total
            next_ref[base : base + 16] = field_ref[base : base + 16] + C1 * total
    table_ref[...] = next_ref[...].astype(BF16)
    ends = ((low_ref, come_low_ref, down_ref, 0, 24), (high_ref, come_high_ref, up_ref, 3, 0))
    for ref, come_ref, out_ref, z, at in ends:
        row, _ = tail_cells(tail_of(ref), 4)
        seen = gather(table_ref[...], row, come_ref)
        lines = [plane(next_ref, a, z) for a in range(3)]
        lines.append(slots_ref[at : at + 24])
        lines += [jnp.concatenate(seen[0:2], axis=1), jnp.concatenate([seen[2], jnp.zeros((8, 128), F32)], axis=1)]
        out_ref[...] = jnp.concatenate(lines, axis=0).astype(BF16)


def home_second(wall_ref, field_ref, tend_ref, bubble_ref, rate_ref, owner_ref, dest_ref,
                base_ref, late_ref, put_ref, table_ref, hot_ref, load_ref):
    field = field_ref[...]
    table_ref[0:FIELD_ROWS] = field.astype(BF16)
    put_ref[...] = put_matrix(dest_ref[1:2])
    row, col = home_cells(owner_ref[1], dest_ref[1:2])

    sums = None
    for i in range(3):
        rows = slice(i * 8, i * 8 + 8)
        hot, load = hot_ref.at[i], load_ref.at[i]
        fill_columns(col[rows], hot)
        pairs = [hi_lo(bubble_ref[a, rows]) for a in range(3)]
        fill_values(row[rows], [p[0] for p in pairs], [p[1] for p in pairs], load)
        got = scatter(load_ref.at[i], hot_ref.at[i])
        sums = got if sums is None else sums + got
        seen = gather(table_ref[0:FIELD_ROWS], row[rows], hot_ref.at[i])
        for a in range(3):
            here = bubble_ref[a, rows]
            rate = (seen[a] - here) / relax_time
            if a == 1:
                rate = rate + buoyancy
            late_ref[a, rows] = here + (C2 * rate + E2 * rate_ref[a, rows])
    push = push_of(sums, field)
    for a in range(3):
        for z in range(4):
            base = (a * 4 + z) * 16
            total = inner_tendency(field_ref, a, z) + push[base : base + 16] + unpack(wall_ref, True, a, z)
            earlier = tend_ref[base : base + 16]
            base_ref[base : base + 16] = field_ref[base : base + 16] + (C2 * total + E2 * earlier)


def late_push(cells_ref, values_ref, field_ref, come_ref, load_ref):
    arrived(cells_ref, values_ref, 48, 4, load_ref)
    return push_of(scatter(load_ref, come_ref), field_ref[...])


def low_second(base_ref, field_ref, low_ref, low2_ref, come_ref, out_ref, load_ref):
    push = late_push(low_ref, low2_ref, field_ref, come_ref, load_ref)
    for a in range(3):
        for z in range(4):
            base = (a * 4 + z) * 16
            total = base_ref[base : base + 16] + C2 * push[base : base + 16]
            if z == 0:
                total = total + C2 * below_term(field_ref, low2_ref[a * 16 : a * 16 + 16, :].astype(F32))
            out_ref[base : base + 16] = total


def high_second(base_ref, field_ref, high_ref, low2_ref, high2_ref, late_ref, put_ref, come_ref,
                out_ref, bubble_ref, load_ref):
    push = late_push(high_ref, high2_ref, field_ref, come_ref, load_ref)
    returned = jnp.concatenate(
        [jnp.concatenate([ref[at : at + 8, :].astype(F32) for ref in (high2_ref, low2_ref)], axis=0) for at in (72, 80)],
        axis=1,
    )
    back = jnp.dot(put_ref[...].astype(BF16), returned.astype(BF16), preferred_element_type=F32)
    for a in range(3):
        bubble_ref[a] = late_ref[a] + (C2 / relax_time) * back[:, a * 128 : (a + 1) * 128]
    for a in range(3):
        for z in range(4):
            base = (a * 4 + z) * 16
            total = base_ref[base : base + 16] + C2 * push[base : base + 16]
            if z == 3:
                total = total + C2 * above_term(field_ref, high2_ref[a * 16 : a * 16 + 16, :].astype(F32))
            out_ref[base : base + 16] = total


def shifted(x, by):
    length = lax.axis_size("pz")
    return lax.ppermute(x, "pz", [(i, (i + by) % length) for i in range(length)])


def exchange(x):
    return lax.all_to_all(x, "px", split_axis=0, concat_axis=0, tiled=True)


def on_device(velocity, first_deriv, second_deriv, bubble_vel, owner, dest):
    field = velocity.reshape(FIELD_ROWS, 256)
    block = ((FIELD_ROWS, 256), F32)
    rows = ((3, 24, 128), F32)
    hot = pltpu.VMEM((256, 1024), BF16)
    load = pltpu.VMEM((448, 1024), BF16)
    table = pltpu.VMEM((384, 256), BF16)
    hots, loads = pltpu.VMEM((3, 256, 1024), BF16), pltpu.VMEM((3, 448, 1024), BF16)
    packed = ((32, 24, 128), BF16)

    velocity_in, bubbles_in, owner_in, dest_in = (
        pltpu.with_memory_space_constraint(x, pltpu.HBM) for x in (field, bubble_vel, owner, dest)
    )
    up, down, moved, field, bubble_vel, owner, dest = pl.pallas_call(
        first_send,
        in_specs=[pl.BlockSpec(memory_space=pltpu.HBM)] * 4,
        out_shape=(
            pltpu.VMEM((SEND_ROWS, 256), BF16),
            pltpu.VMEM((SEND_ROWS, 256), BF16),
            pltpu.VMEM((16, 256), F32),
            pltpu.VMEM((FIELD_ROWS, 256), F32),
            pltpu.VMEM((3, 24, 128), F32),
            pltpu.VMEM((2, 24, 128), jnp.int32),
            pltpu.VMEM((2, 24), jnp.int32),
        ),
        scratch_shapes=[pltpu.SemaphoreType.DMA((4,))],
    )(velocity_in, bubbles_in, owner_in, dest_in)
    low, high = shifted(up, 1), shifted(down, -1)
    part, seen, put, pick = call(
        home_first, (block, rows, ((24, 16), F32), ((16, 24), F32)), (table, hots, loads)
    )(field, bubble_vel, owner, dest)
    spread_hot = ((256, 1024), BF16)
    part, afar, come_low = call(low_first, (block, ((3, 8, 128), F32), spread_hot), (hot, hot, load))(
        field, part, low, moved
    )
    part, to_columns, rate, bubbles, slots, come_high = call(
        high_first, (block, packed, rows, rows, ((48, 256), F32), spread_hot), (hot, hot, load)
    )(field, part, high, moved, afar, seen, bubble_vel, put, pick)
    columns = exchange(to_columns)
    (walls,) = call(columns_body, (packed,))(columns, first_deriv, second_deriv)
    walls = exchange(walls)
    lasts = ((LAST_ROWS, 256), BF16)
    middle, tend, up, down = call(middle_body, (block, block, lasts, lasts), (pltpu.VMEM((FIELD_ROWS, 256), BF16),))(
        walls, field, part, low, high, slots, come_low, come_high
    )
    low2, high2 = shifted(up, 1), shifted(down, -1)
    base, late, put = call(
        home_second, (block, rows, ((24, 16), F32)), (table, hots, loads)
    )(walls, middle, tend, bubbles, rate, owner, dest)
    (base,) = call(low_second, (block,), (load,))(base, middle, low, low2, come_low)
    field, bubbles = call(high_second, (block, rows), (load,))(
        base, middle, high, low2, high2, late, put, come_high
    )
    return (field.reshape(velocity.shape), bubbles)


def solution(mesh):
    return jax.shard_map(
        on_device,
        mesh=mesh,
        in_specs=(
            P(None, "pz", "px", None),
            P(),
            P(),
            P(None, ("px", "pz"), None),
            P(None, ("px", "pz"), None),
            P(None, ("px", "pz")),
        ),
        out_specs=(P(None, "pz", "px", None), P(None, ("px", "pz"), None)),
        check_vma=False,
    )
```
